256 devices in a mesh: tok: 64 (over x, z, y_hi), head: 4 (over y_lo, core).
Axes of the slice: x: 4, y: 4 (y_hi: 2, y_lo: 2; y = y_hi * 2 + y_lo), z: 8, core: 2. Of those that a mesh axis runs over, the one named last changes fastest.
Arguments:
- queries: bfloat16 [16384, 3072], P('tok', 'head'), may hold values from -96 to 96
- key_rows: bfloat16 [16384, 512], P('tok', 'head'), may hold values from -6 to 6
- value_rows: bfloat16 [16384, 512], P('tok', 'head'), may hold values from -12 to 12
- tile_mask: int32 [128, 128], P('tok'), may hold values from 0 to 1, as said below
- out_weight: bfloat16 [3072, 6144], P('head'), may hold values from -0.109375 to 0.109375
Outputs:
- mixed: bfloat16 [16384, 6144], P('tok', 'head')
The draws below stay inside these ranges and needn't reach their ends.
Inputs may be any that keep to these rules, and one draw needn't show every extreme that they name: `tile_mask`: row r keeps key tile r; every row keeps between 1 and 64 tiles, and some row keeps exactly 64.
All inputs are finite; a program needn't handle non-finite values.
Results may differ from the reference program's by a relative error of at most 0.012.
Values may be sent and summed in bfloat16 or wider, within the bound.
No kernel may reach another device: no remote copies, remote signals or barrier semaphores. Data moves between devices by JAX's collectives and lax.ppermute only.
A program may use at most 128 MiB of HBM per device.

```python
import math
import jax
import jax.numpy as jnp
from jax import lax

D = 6144
HD = 128
QH = 24
KVH = 4
TILE = 128
TOKENS = 16384


def draw_pair(key):
    base_key = jax.random.fold_in(key, 11)
    streams = jax.random.split(base_key, 2)
    key_vals = jnp.clip(jax.random.normal(streams[0], (TOKENS, KVH * HD), jnp.float32), -6.0, 6.0)
    query_vals = jnp.clip(2.5 * jax.random.normal(streams[1], (TOKENS, QH * HD), jnp.float32), -15.0, 15.0)
    return (query_vals, key_vals)


def draw_queries(key, part):
    return draw_pair(key)[0].astype(jnp.bfloat16)


def draw_key_rows(key, part):
    return draw_pair(key)[1].astype(jnp.bfloat16)


def draw_tile_mask(key, part):
    tile_count = TOKENS // TILE
    base_key = jax.random.fold_in(key, 23)
    streams = jax.random.split(base_key, 3)
    counts = jax.random.randint(streams[0], (tile_count, 1), 1, tile_count // 2 + 1)
    full_row = jax.random.randint(streams[1], (), 0, tile_count)
    counts = jnp.where(jnp.arange(tile_count)[:, None] == full_row, tile_count // 2, counts)
    scores = jax.random.randint(streams[2], (tile_count, tile_count), 0, 65536) * tile_count + jnp.arange(tile_count)[None, :]
    diagonal = jnp.arange(tile_count)[:, None] == jnp.arange(tile_count)[None, :]
    scores = jnp.where(diagonal, -1, scores)
    ranking = jnp.argsort(jnp.argsort(scores, axis=1), axis=1)
    return (ranking < counts).astype(jnp.int32)


def steps_of(stream_key, extent, cuts, smallest, high):
    factor_of = 1.0
    for dim, shards_of in cuts:
        heights = jax.random.uniform(jax.random.fold_in(jax.random.fold_in(stream_key, 6), dim), (shards_of,), jnp.float32, smallest / len(cuts), high / len(cuts))
        factor_of = factor_of * jnp.repeat(jnp.exp(heights), extent[dim] // shards_of).reshape((-1,) + (1,) * (len(extent) - 1 - dim))
    return factor_of


def centred(rng, dims, width, limit, cuts=(), dtype=jnp.bfloat16):
    result = width * jax.random.normal(rng, dims, jnp.float32)
    if cuts:
        result = result * steps_of(rng, dims, cuts, -0.22, 0.18)
    return jnp.clip(result, -limit, limit).astype(dtype)


def setup_inputs(seed: int = 0) -> dict:
    streams_of = jax.random.split(jax.random.key(seed), 6)
    return {
        "queries": draw_queries(jax.random.fold_in(streams_of[5], 71), 0),
        "key_rows": draw_key_rows(jax.random.fold_in(streams_of[5], 71), 0),
        "value_rows": centred(streams_of[2], (TOKENS, KVH * HD), 2.0, 12.0, ((0, 64), (1, 4))),
        "tile_mask": draw_tile_mask(jax.random.fold_in(streams_of[5], 71), 0),
        "out_weight": centred(streams_of[4], (QH * HD, D), (QH * HD) ** -0.5, 0.109375, ((0, 4),)),
    }


NEGATIVE = -1e+30

def reference(queries, key_rows, value_rows, tile_mask, out_weight):
    tile_count = TOKENS // TILE
    group_size = QH // KVH
    kept_most = tile_count // 2
    score_scale = 1.0 / math.sqrt(HD)
    key_blocks = key_rows.reshape(tile_count, TILE, KVH, HD)
    value_blocks = value_rows.reshape(tile_count, TILE, KVH, HD)

    def one_tile(inputs):
        query_tile, mask_row = inputs
        ordering = jnp.argsort(1 - mask_row, stable=True)[:kept_most].astype(jnp.int32)
        kept_flags = jnp.take(mask_row, ordering) > 0
        key_chosen = jnp.take(key_blocks, ordering, axis=0).astype(jnp.float32)
        value_chosen = jnp.take(value_blocks, ordering, axis=0).astype(jnp.float32)
        query_f32 = query_tile.reshape(TILE, KVH, group_size, HD).astype(jnp.float32)
        scores = jnp.einsum('qgjd,ckgd->gjqck', query_f32, key_chosen) * score_scale
        shown = kept_flags[None, None, None, :]
        tile_max = jnp.where(shown, lax.optimization_barrier(jnp.max(scores, axis=-1)), NEGATIVE)
        prob_bf = jnp.where(shown[..., None], jnp.exp(scores - tile_max[..., None]), 0.0).astype(jnp.bfloat16)
        prob_f32 = prob_bf.astype(jnp.float32)
        tile_sums = lax.optimization_barrier(jnp.sum(prob_f32, axis=-1))
        tile_parts = jnp.einsum('gjqck,ckgd->gjqcd', prob_f32, value_chosen)
        row_max = lax.optimization_barrier(jnp.max(tile_max, axis=-1))
        tile_weight = jnp.where(shown, jnp.exp(tile_max - row_max[..., None]), 0.0)
        numerator = lax.optimization_barrier(jnp.sum(tile_weight[..., None] * tile_parts, axis=3))
        denominator = lax.optimization_barrier(jnp.sum(tile_weight * tile_sums, axis=-1))
        attended = numerator / denominator[..., None]
        return attended.transpose(2, 0, 1, 3).reshape(TILE, QH * HD).astype(jnp.bfloat16)
    attention = lax.map(one_tile, (queries.reshape(tile_count, TILE, QH * HD), tile_mask))
    attention = attention.reshape(TOKENS, QH * HD)
    return jnp.dot(attention, out_weight, preferred_element_type=jnp.float32).astype(jnp.bfloat16)
```

```python
import math

import jax
import jax.numpy as jnp
from jax import lax
from jax.experimental import pallas as pl
from jax.experimental.pallas import tpu as pltpu
from jax.sharding import Mesh, PartitionSpec as P

HD = 128
TILE = 128
NX, NZ = 4, 8
HEADS = 6
WIDE = HEADS * TILE
SUM_ROW = HD
MAX_ROW = HD + 16
ROWS = HD + 24
NEGATIVE = -1e30
EXP2_SCALE = math.log2(math.e) / math.sqrt(HD)
Z_ORDER = (0, -1, 1, -2, 2, -3, 3, 4)


def vmem():
    return pl.BlockSpec(memory_space=pltpu.VMEM)


def smem():
    return pl.BlockSpec(memory_space=pltpu.SMEM)


def call(kernel, out_shape, args, in_specs, scratch=(), aliases=None, name=None):
    return pl.pallas_call(
        kernel,
        out_shape=out_shape,
        in_specs=in_specs,
        out_specs=jax.tree.map(lambda s: vmem(), out_shape),
        scratch_shapes=list(scratch),
        input_output_aliases=aliases or {},
        compiler_params=pltpu.CompilerParams(vmem_limit_bytes=48 * 1024 * 1024),
        name=name,
    )(*args)


def pack_kernel(key_ref, value_ref, out_ref):
    for t in range(2):
        rows = pl.ds(t * TILE, TILE)
        out_ref[t] = key_ref[rows, :]
        out_ref[2 + t] = value_ref[rows, :].astype(jnp.float32).T.astype(jnp.bfloat16)


def join_kernel(*refs):
    out_ref = refs[-1]
    at = 0
    for ref in refs[:-1]:
        out_ref[pl.ds(at, ref.shape[0])] = ref[...]
        at += ref.shape[0]


def join(parts):
    total = sum(p.shape[0] for p in parts)
    shape = jax.ShapeDtypeStruct((total, *parts[0].shape[1:]), parts[0].dtype)
    return call(join_kernel, shape, parts, [vmem()] * len(parts), name="join")


def stage_kernel(columns, count, first, place_ref, mask_ref, mine_ref, theirs_ref, *refs):
    parts, refs = refs[:count], refs[count:]
    if not first:
        refs = refs[2:]
    keep_ref, send_ref, tiles_ref, query_ref, list_ref = refs
    x, z, core = place_ref[0], place_ref[1], place_ref[2]
    at = 0
    for part in parts:
        tiles_ref[pl.ds(at, part.shape[0])] = part[...]
        at += part.shape[0]
    for number in range(4):
        source = mine_ref if number < 2 else theirs_ref
        rows = pl.ds(number % 2 * TILE, TILE)
        for h in range(HEADS):
            query_ref[number, pl.ds(h * TILE, TILE), :] = source[rows, pl.ds(h * HD, HD)]
    if first:
        for ref in (keep_ref, send_ref):
            ref[:, :MAX_ROW, :] = jnp.zeros((2, MAX_ROW, WIDE), jnp.float32)
            ref[:, MAX_ROW:, :] = jnp.full((2, ROWS - MAX_ROW, WIDE), NEGATIVE, jnp.float32)

    counts = [jnp.int32(0)] * 4
    slot = 0
    for dx, order in columns:
        for dz in order:
            block = lax.rem(x + dx + NX, NX) * NZ + lax.rem(z + dz + NZ, NZ)
            for r in range(2):
                tile = (block * 2 + core) * 2 + r
                for number in range(4):
                    list_ref[number, counts[number]] = slot // 2 * 4 + slot % 2
                    counts[number] = counts[number] + mask_ref[number, tile]
                slot += 1

    for number in range(4):
        state_ref = keep_ref if number < 2 else send_ref
        row = number % 2
        total = counts[number]

        def one_pair(turn, carry, number=number, state_ref=state_ref, row=row, total=total):
            first_at = list_ref[number, 2 * turn]
            both = 2 * turn + 1 < total
            second_at = jnp.where(both, list_ref[number, 2 * turn + 1], first_at)
            keys = jnp.concatenate([tiles_ref[first_at], tiles_ref[second_at]], axis=0)
            shown = jnp.where(both, 1.0, 0.0).astype(jnp.float32)
            lane = lax.broadcasted_iota(jnp.int32, (HD + 16, 2 * TILE), 1)
            shown_lanes = jnp.where(lane < TILE, 1.0, shown).astype(jnp.bfloat16)
            values = jnp.concatenate([tiles_ref[first_at + 2], tiles_ref[second_at + 2]], axis=1)
            values = jnp.concatenate(
                [values, jnp.ones((16, 2 * TILE), jnp.bfloat16)], axis=0
            ) * shown_lanes
            for chunk in range(3):
                lanes = pl.ds(chunk * 256, 256)
                scores = lax.dot_general(
                    keys,
                    query_ref[number, lanes, :],
                    (((1,), (1,)), ((), ())),
                    preferred_element_type=jnp.float32,
                )
                old_max = state_ref[row, pl.ds(MAX_ROW, 1), lanes]
                new_max = jnp.maximum(old_max, jnp.max(scores, axis=0, keepdims=True))
                prob = jnp.exp2((scores - new_max) * EXP2_SCALE).astype(jnp.bfloat16)
                fade = jnp.exp2((old_max - new_max) * EXP2_SCALE)
                part = lax.dot_general(
                    values, prob, (((1,), (0,)), ((), ())), preferred_element_type=jnp.float32
                )
                state_ref[row, pl.ds(0, MAX_ROW), lanes] = (
                    state_ref[row, pl.ds(0, MAX_ROW), lanes] * fade + part
                )
                state_ref[row, pl.ds(MAX_ROW, 8), lanes] = jnp.broadcast_to(new_max, (8, 256))
            return carry

        lax.fori_loop(0, (total + 1) // 2, one_pair, 0)


def stage(columns, place, mask, mine, theirs, parts, state, name):
    shape = jax.ShapeDtypeStruct((2, ROWS, WIDE), jnp.float32)
    slots = sum(2 * len(order) for _, order in columns)
    args = [place, mask, mine, theirs, *parts]
    aliases = {}
    if state is not None:
        aliases = {len(args): 0, len(args) + 1: 1}
        args += list(state)
    kernel = lambda *refs: stage_kernel(columns, len(parts), state is None, *refs)
    return call(
        kernel,
        (shape, shape),
        args,
        [smem(), smem()] + [vmem()] * (len(args) - 2),
        scratch=(
            pltpu.VMEM((2 * slots, TILE, TILE), jnp.bfloat16),
            pltpu.VMEM((4, WIDE, HD), jnp.bfloat16),
            pltpu.SMEM((4, slots + 1), jnp.int32),
        ),
        aliases=aliases,
        name=name,
    )


def merge_kernel(own_ref, other_ref, out_ref):
    for t in range(2):
        own_max = own_ref[t, pl.ds(MAX_ROW, 1), :]
        other_max = other_ref[t, pl.ds(MAX_ROW, 1), :]
        row_max = jnp.maximum(own_max, other_max)
        own_weight = jnp.exp2((own_max - row_max) * EXP2_SCALE)
        other_weight = jnp.exp2((other_max - row_max) * EXP2_SCALE)
        total = (
            own_ref[t, pl.ds(SUM_ROW, 1), :] * own_weight
            + other_ref[t, pl.ds(SUM_ROW, 1), :] * other_weight
        )
        own_weight = own_weight / total
        other_weight = other_weight / total
        for h in range(HEADS):
            lanes = slice(h * TILE, (h + 1) * TILE)
            attended = (
                own_ref[t, pl.ds(0, HD), lanes] * own_weight[:, lanes]
                + other_ref[t, pl.ds(0, HD), lanes] * other_weight[:, lanes]
            )
            out_ref[pl.ds(t * TILE, TILE), pl.ds(h * HD, HD)] = attended.T.astype(jnp.bfloat16)


def ring(size, step):
    return [(i, (i + step) % size) for i in range(size)]


def along_y(move):
    pairs = []
    for i in range(8):
        yh, yl, core = move(i // 4, i // 2 % 2, i % 2)
        pairs.append((i, yh % 2 * 4 + yl % 2 * 2 + core % 2))
    return pairs


def next_y(yh, yl, step):
    y = (yh * 2 + yl + step) % 4
    return y // 2, y % 2


Y = ("yh", "yl", "core")
YZ = ("z", "yh", "yl", "core")


def turned(shift):
    turn = along_y(lambda yh, yl, core: (core, yl, yh))
    return [(z * 8 + a, (z + shift) % NZ * 8 + b) for z in range(NZ) for a, b in turn]


def per_device(queries, key_rows, value_rows, tile_mask, out_weight):
    x, z = lax.axis_index("x"), lax.axis_index("z")
    yh, yl, core = lax.axis_index("yh"), lax.axis_index("yl"), lax.axis_index("core")
    turn = along_y(lambda yh, yl, core: (core, yl, yh))
    f32 = jnp.float32

    unit_shape = jax.ShapeDtypeStruct((4, TILE, TILE), jnp.bfloat16)
    unit = call(pack_kernel, unit_shape, (key_rows, value_rows), [vmem()] * 2, name="pack")
    up, down = ring(NZ, 1), ring(NZ, -1)
    own = lax.ppermute(unit, YZ, turned(0))
    units = {0: own}
    units[-1] = lax.ppermute(unit, YZ, turned(1))
    units[1] = lax.ppermute(unit, YZ, turned(-1))
    mine = lax.ppermute(queries, Y, turn)
    other_mask = lax.ppermute(tile_mask, "yh", [(0, 1), (1, 0)])
    for step in (2, 3):
        units[-step] = lax.ppermute(units[1 - step], "z", up)
        units[step] = lax.ppermute(units[step - 1], "z", down)
    far = (
        lax.ppermute(units[-3][:2], "z", up),
        lax.ppermute(units[3][2:], "z", down),
    )
    theirs = lax.ppermute(mine, "core", [(0, 1), (1, 0)])
    same = yh == core
    mask = jnp.concatenate(
        [jnp.where(same, tile_mask, other_mask), jnp.where(same, other_mask, tile_mask)]
    )
    place = jnp.stack([x, z, core]).astype(jnp.int32)

    column = join([units[d] for d in Z_ORDER[:-1]] + list(far))
    before = lax.ppermute(column, "x", ring(NX, 1))
    after = lax.ppermute(column, "x", ring(NX, -1))
    half = column.shape[0] // 2
    first_half = lax.ppermute(before[:half], "x", ring(NX, 1))
    second_half = lax.ppermute(after[half:], "x", ring(NX, -1))

    block = out_weight.shape[1] // 4
    column_block = lambda yl, core: lax.dynamic_slice_in_dim(
        out_weight, (yl * 2 + core) * block, block, 1
    )
    weight_own = column_block(yl, core)
    weight_core = lax.ppermute(column_block(yl, 1 - core), "core", [(0, 1), (1, 0)])
    weight_up = lax.ppermute(
        column_block(1 - yl, core), Y, along_y(lambda yh, yl, core: (*next_y(yh, yl, 1), core))
    )
    weight_down = lax.ppermute(
        column_block(1 - yl, 1 - core),
        Y,
        along_y(lambda yh, yl, core: (*next_y(yh, yl, -1), 1 - core)),
    )

    near = (place, mask, mine, theirs)
    state = stage(((0, Z_ORDER),), *near, [column], None, "stage_a")
    state = stage(((-1, Z_ORDER), (1, Z_ORDER)), *near, [before, after], state, "stage_b")
    state = stage(((2, Z_ORDER),), *near, [first_half, second_half], state, "stage_c")
    keep, send = state
    received = lax.ppermute(send, "core", [(0, 1), (1, 0)])
    shape = jax.ShapeDtypeStruct((2 * TILE, WIDE), jnp.bfloat16)
    attended = call(merge_kernel, shape, (keep, received), [vmem()] * 2, name="merge")

    near_part = lax.ppermute(attended, Y, turn)
    far_part = lax.ppermute(attended, Y, along_y(lambda yh, yl, core: (core, 1 - yl, yh)))
    swap = [(0, 1), (1, 0)]
    near_other = lax.ppermute(near_part, "core", swap)
    far_other = lax.ppermute(far_part, "core", swap)
    dot = lambda a, b: jnp.dot(a, b, preferred_element_type=f32)
    mixed = dot(near_part, weight_own) + dot(far_part, weight_up)
    mixed = mixed + dot(near_other, weight_core) + dot(far_other, weight_down)
    return mixed.astype(jnp.bfloat16)


def solution(mesh):
    fine = Mesh(mesh.devices.reshape(NX, NZ, 2, 2, 2), ("x", "z", "yh", "yl", "core"))
    tok, head = ("x", "z", "yh"), ("yl", "core")
    return jax.shard_map(
        per_device,
        mesh=fine,
        in_specs=(P(tok, head), P(tok, head), P(tok, head), P(tok, None), P(head, None)),
        out_specs=P(tok, head),
        check_vma=False,
    )
```

```python
import math

import jax
import jax.numpy as jnp
from jax import lax
from jax.experimental import pallas as pl
from jax.experimental.pallas import tpu as pltpu
from jax.sharding import Mesh, PartitionSpec as P

HD = 128
TILE = 128
NX, NZ = 4, 8
HEADS = 6
WIDE = HEADS * TILE
SUM_ROW = HD
MAX_ROW = HD + 16
ROWS = HD + 24
NEGATIVE = -1e30
BLOCK = 4
EXP2_SCALE = math.log2(math.e) / math.sqrt(HD)
Z_ORDER = (0, -1, 1, -2, 2, -3, 3, 4)


def vmem():
    return pl.BlockSpec(memory_space=pltpu.VMEM)


def smem():
    return pl.BlockSpec(memory_space=pltpu.SMEM)


def call(kernel, out_shape, args, in_specs, scratch=(), aliases=None, name=None, flops=0):
    return pl.pallas_call(
        kernel,
        out_shape=out_shape,
        in_specs=in_specs,
        out_specs=jax.tree.map(lambda s: vmem(), out_shape),
        scratch_shapes=list(scratch),
        input_output_aliases=aliases or {},
        compiler_params=pltpu.CompilerParams(vmem_limit_bytes=48 * 1024 * 1024),
        cost_estimate=pl.CostEstimate(flops=flops, transcendentals=0, bytes_accessed=0),
        name=name,
    )(*args)


def pack_kernel(key_ref, value_ref, out_ref):
    for t in range(2):
        rows = pl.ds(t * TILE, TILE)
        out_ref[t] = key_ref[rows, :]
        out_ref[2 + t] = value_ref[rows, :].astype(jnp.float32).T.astype(jnp.bfloat16)


def join_kernel(*refs):
    out_ref = refs[-1]
    at = 0
    for ref in refs[:-1]:
        out_ref[pl.ds(at, ref.shape[0])] = ref[...]
        at += ref.shape[0]


def join(parts):
    total = sum(p.shape[0] for p in parts)
    shape = jax.ShapeDtypeStruct((total, *parts[0].shape[1:]), parts[0].dtype)
    return call(join_kernel, shape, parts, [vmem()] * len(parts), name="join")


def stage_kernel(columns, count, numbers, first, table_ref, mine_ref, theirs_ref, *refs):
    parts, refs = refs[:count], refs[count:]
    targets = sorted({number // 2 for number in numbers})
    if not first:
        refs = refs[len(targets) :]
    states, (tiles_ref, query_ref, list_ref) = refs[: len(targets)], refs[len(targets) :]
    x, z, core = table_ref[4, 0], table_ref[4, 1], table_ref[4, 2]
    at = 0
    for part in parts:
        tiles_ref[pl.ds(at, part.shape[0])] = part[...]
        at += part.shape[0]
    for number in numbers:
        source = mine_ref if number < 2 else theirs_ref
        rows = pl.ds(number % 2 * TILE, TILE)
        for h in range(HEADS):
            query_ref[number, pl.ds(h * TILE, TILE), :] = source[rows, pl.ds(h * HD, HD)]
    if first:
        for ref in states:
            ref[:, :MAX_ROW, :] = jnp.zeros((2, MAX_ROW, WIDE), jnp.float32)
            ref[:, MAX_ROW:, :] = jnp.full((2, ROWS - MAX_ROW, WIDE), NEGATIVE, jnp.float32)

    counts = [jnp.int32(0)] * 4
    slot = 0
    for dx, order in columns:
        for dz in order:
            block = lax.rem(x + dx + NX, NX) * NZ + lax.rem(z + dz + NZ, NZ)
            for r in range(2):
                tile = (block * 2 + core) * 2 + r
                for number in numbers:
                    list_ref[number, counts[number]] = slot // 2 * 4 + slot % 2
                    counts[number] = counts[number] + table_ref[number, tile]
                slot += 1

    for number in numbers:
        state_ref = states[targets.index(number // 2)]
        row = number % 2
        total = counts[number]

        def one_block(turn, carry, number=number, state_ref=state_ref, row=row, total=total):
            base = turn * BLOCK
            first_at = list_ref[number, base]
            at, values = [first_at], []
            ones = jnp.ones((16, TILE), jnp.bfloat16)
            for j in range(BLOCK):
                if j:
                    live = base + j < total
                    at.append(jnp.where(live, list_ref[number, base + j], first_at))
                value = jnp.concatenate([tiles_ref[at[j] + 2], ones], axis=0)
                if j:
                    value = value * jnp.where(live, 1.0, 0.0).astype(jnp.bfloat16)
                values.append(value)
            values = jnp.concatenate(values, axis=1)
            keys = jnp.concatenate([tiles_ref[i] for i in at], axis=0)
            chunks = [pl.ds(c * TILE, TILE) for c in range(HEADS)]
            scores = [
                lax.dot_general(
                    keys,
                    query_ref[number, lanes, :],
                    (((1,), (1,)), ((), ())),
                    preferred_element_type=jnp.float32,
                )
                for lanes in chunks
            ]
            probs = []
            for lanes, score in zip(chunks, scores):
                old_max = state_ref[row, pl.ds(MAX_ROW, 1), lanes]
                new_max = jnp.maximum(old_max, jnp.max(score, axis=0, keepdims=True))
                prob = jnp.exp2((score - new_max) * EXP2_SCALE).astype(jnp.bfloat16)
                probs.append((prob, jnp.exp2((old_max - new_max) * EXP2_SCALE)))
                state_ref[row, pl.ds(MAX_ROW, 8), lanes] = jnp.broadcast_to(new_max, (8, TILE))
            for lanes, (prob, fade) in zip(chunks, probs):
                part = lax.dot_general(
                    values, prob, (((1,), (0,)), ((), ())), preferred_element_type=jnp.float32
                )
                state_ref[row, pl.ds(0, MAX_ROW), lanes] = (
                    state_ref[row, pl.ds(0, MAX_ROW), lanes] * fade + part
                )
            return carry

        lax.fori_loop(0, (total + BLOCK - 1) // BLOCK, one_block, 0)


def stage(columns, near, parts, state, numbers, name):
    shape = jax.ShapeDtypeStruct((2, ROWS, WIDE), jnp.float32)
    slots = sum(2 * len(order) for _, order in columns)
    args = [*near, *parts]
    outs = len({number // 2 for number in numbers})
    aliases = {}
    if state is not None:
        aliases = {len(args) + i: i for i in range(outs)}
        args += list(state)
    kernel = lambda *refs: stage_kernel(columns, len(parts), numbers, state is None, *refs)
    return call(
        kernel,
        (shape,) * outs,
        args,
        [smem()] + [vmem()] * (len(args) - 1),
        scratch=(
            pltpu.VMEM((2 * slots, TILE, TILE), jnp.bfloat16),
            pltpu.VMEM((4, WIDE, HD), jnp.bfloat16),
            pltpu.SMEM((4, slots + BLOCK), jnp.int32),
        ),
        aliases=aliases,
        name=name,
    )


def merge_kernel(own_ref, other_ref, out_ref):
    for t in range(2):
        own_max = own_ref[t, pl.ds(MAX_ROW, 1), :]
        other_max = other_ref[t, pl.ds(MAX_ROW, 1), :]
        row_max = jnp.maximum(own_max, other_max)
        own_weight = jnp.exp2((own_max - row_max) * EXP2_SCALE)
        other_weight = jnp.exp2((other_max - row_max) * EXP2_SCALE)
        total = (
            own_ref[t, pl.ds(SUM_ROW, 1), :] * own_weight
            + other_ref[t, pl.ds(SUM_ROW, 1), :] * other_weight
        )
        own_weight = own_weight / total
        other_weight = other_weight / total
        for h in range(HEADS):
            lanes = slice(h * TILE, (h + 1) * TILE)
            attended = (
                own_ref[t, pl.ds(0, HD), lanes] * own_weight[:, lanes]
                + other_ref[t, pl.ds(0, HD), lanes] * other_weight[:, lanes]
            )
            out_ref[pl.ds(t * TILE, TILE), pl.ds(h * HD, HD)] = attended.T.astype(jnp.bfloat16)


def ring(size, step):
    return [(i, (i + step) % size) for i in range(size)]


def along_y(move):
    pairs = []
    for i in range(8):
        yh, yl, core = move(i // 4, i // 2 % 2, i % 2)
        pairs.append((i, yh % 2 * 4 + yl % 2 * 2 + core % 2))
    return pairs


def next_y(yh, yl, step):
    y = (yh * 2 + yl + step) % 4
    return y // 2, y % 2


Y = ("yh", "yl", "core")
YZ = ("z", "yh", "yl", "core")


def turned(shift):
    turn = along_y(lambda yh, yl, core: (core, yl, yh))
    return [(z * 8 + a, (z + shift) % NZ * 8 + b) for z in range(NZ) for a, b in turn]


def project_kernel(count, *refs):
    out_ref = refs[-1]
    before = refs[-2] if count < len(refs) - 1 else None
    pairs, at = [], 0
    while at < count:
        left, depth, used = refs[at], refs[at].shape[1], 0
        at += 1
        while used < depth:
            pairs.append((left, used, refs[at]))
            used += refs[at].shape[0]
            at += 1
    for n in range(out_ref.shape[1] // 256):
        lanes = pl.ds(n * 256, 256)
        total = None if before is None else before[:, lanes]
        for left, used, right in pairs:
            part = jnp.dot(
                left[:, pl.ds(used, right.shape[0])],
                right[:, lanes],
                preferred_element_type=jnp.float32,
            )
            total = part if total is None else total + part
        out_ref[:, lanes] = total.astype(out_ref.dtype)


def project(args, before, dtype, name):
    count = len(args)
    shape = jax.ShapeDtypeStruct((args[0].shape[0], args[1].shape[1]), dtype)
    args = args + ([] if before is None else [before])
    kernel = lambda *refs: project_kernel(count, *refs)
    return call(kernel, shape, args, [vmem()] * len(args), name=name, flops=args[0].size * args[1].shape[1] * 4)


def per_device(queries, key_rows, value_rows, tile_mask, out_weight):
    x, z = lax.axis_index("x"), lax.axis_index("z")
    yh, yl, core = lax.axis_index("yh"), lax.axis_index("yl"), lax.axis_index("core")
    turn = along_y(lambda yh, yl, core: (core, yl, yh))
    swap = [(0, 1), (1, 0)]
    together = lax.optimization_barrier

    block = out_weight.shape[1] // 4
    depth = out_weight.shape[0]

    def columns_of(source, yl, core, start=0, rows=depth):
        return lax.dynamic_slice(source, (jnp.int32(start), (yl * 2 + core) * block), (rows, block))

    unit_shape = jax.ShapeDtypeStruct((4, TILE, TILE), jnp.bfloat16)
    unit = call(pack_kernel, unit_shape, (key_rows, value_rows), [vmem()] * 2, name="pack")
    up, down = ring(NZ, 1), ring(NZ, -1)
    units = {0: lax.ppermute(unit, YZ, turned(0))}
    units[-1] = lax.ppermute(unit, YZ, turned(1))
    units[1] = lax.ppermute(unit, YZ, turned(-1))
    queries, tile_mask, _ = together((queries, tile_mask, units[-1]))
    mine = lax.ppermute(queries, Y, turn)
    other_mask = lax.ppermute(tile_mask, "yh", swap)
    units[-2] = lax.ppermute(units[-1], "z", up)
    units[2] = lax.ppermute(units[1], "z", down)
    weight_own = columns_of(out_weight, yl, core)
    weight_core = lax.ppermute(columns_of(out_weight, yl, 1 - core), "core", swap)
    units[-2], units[2], weight_core = together((units[-2], units[2], weight_core))
    units[-3] = lax.ppermute(units[-2], "z", up)
    units[3] = lax.ppermute(units[2], "z", down)
    units[-3], units[3], mine, other_mask = together((units[-3], units[3], mine, other_mask))
    far = [
        lax.ppermute(units[-3][:2], "z", up),
        lax.ppermute(units[3][2:], "z", down),
    ]
    theirs = lax.ppermute(mine, "core", swap)
    *far, theirs = together((*far, theirs))
    same = yh == core
    place = jnp.pad(jnp.stack([x, z, core]).astype(jnp.int32), (0, 125))[None]
    table = jnp.concatenate(
        [
            jnp.where(same, tile_mask, other_mask),
            jnp.where(same, other_mask, tile_mask),
            place,
            jnp.zeros((3, 128), jnp.int32),
        ]
    )

    same_core = along_y(lambda yh, yl, core: (*next_y(yh, yl, 1 - 2 * core), core))
    other_core = along_y(lambda yh, yl, core: (*next_y(yh, yl, 1 - 2 * core), 1 - core))
    source, _ = together((out_weight, mine))
    weight_far = lax.ppermute(columns_of(source, 1 - yl, core), Y, same_core)

    def send_half(number, after):
        source, _ = together((out_weight, after))
        piece = columns_of(source, 1 - yl, 1 - core, number * depth // 2, depth // 2)
        return lax.ppermute(piece, Y, other_core)

    low = join([units[d] for d in Z_ORDER[:4]])
    high = join([units[d] for d in Z_ORDER[4:7]] + far)
    forth, back = ring(NX, 1), ring(NX, -1)
    before_low = lax.ppermute(low, "x", forth)
    after_high = lax.ppermute(high, "x", back)
    before_high = lax.ppermute(high, "x", forth)
    after_low = lax.ppermute(low, "x", back)

    near = (table, mine, theirs)
    every = (0, 1, 2, 3)
    state = stage(((0, Z_ORDER),), near, [low, high], None, every, "stage_a")
    before_low, after_high, weight_far, *state = together(
        (before_low, after_high, weight_far, *state)
    )
    weight_cross = [send_half(0, weight_far)]
    far_low = lax.ppermute(before_low, "x", forth)
    far_high = lax.ppermute(after_high, "x", back)
    before_high, after_low, weight_cross[0] = together((before_high, after_low, weight_cross[0]))
    weight_cross.append(send_half(1, weight_cross[0]))
    low_order, high_order = Z_ORDER[:4], Z_ORDER[4:]
    keep, send = stage(
        ((-1, low_order), (1, high_order), (-1, high_order), (1, low_order)),
        near,
        [before_low, after_high, before_high, after_low],
        state,
        every,
        "stage_b",
    )
    far_low, far_high, keep, send = together((far_low, far_high, keep, send))
    last = (((2, Z_ORDER),), near, [far_low, far_high])
    (send,) = stage(*last, (send,), (2, 3), "stage_c")
    received = lax.ppermute(send, "core", swap)
    (keep,) = stage(*last, (keep,), (0, 1), "stage_d")
    keep, received, weight_cross[1] = together((keep, received, weight_cross[1]))
    shape = jax.ShapeDtypeStruct((2 * TILE, WIDE), jnp.bfloat16)
    attended = call(merge_kernel, shape, (keep, received), [vmem()] * 2, name="merge")

    near_part = lax.ppermute(attended, Y, turn)
    far_part = lax.ppermute(attended, Y, along_y(lambda yh, yl, core: (core, 1 - yl, yh)))
    near_other = lax.ppermute(near_part, "core", swap)
    far_other = lax.ppermute(far_part, "core", swap)
    half = project([near_part, weight_own, far_part, weight_far], None, jnp.float32, "project_a")
    return project(
        [near_other, weight_core, far_other, *weight_cross], half, jnp.bfloat16, "project_b"
    )


def solution(mesh):
    fine = Mesh(mesh.devices.reshape(NX, NZ, 2, 2, 2), ("x", "z", "yh", "yl", "core"))
    tok, head = ("x", "z", "yh"), ("yl", "core")
    return jax.shard_map(
        per_device,
        mesh=fine,
        in_specs=(P(tok, head), P(tok, head), P(tok, head), P(tok, None), P(head, None)),
        out_specs=P(tok, head),
        check_vma=False,
    )
```

```python
import math

import jax
import jax.numpy as jnp
from jax import lax
from jax.experimental import pallas as pl
from jax.experimental.pallas import tpu as pltpu
from jax.sharding import Mesh, PartitionSpec as P

HD = 128
TILE = 128
NX, NZ = 4, 8
HEADS = 6
WIDE = HEADS * TILE
SUM_ROW = HD
MAX_ROW = HD + 16
ROWS = HD + 24
NEGATIVE = -1e30
BLOCK = 4
MASK_AT = 2 * HEADS
UNIT_AT = MASK_AT + 1
EXP2_SCALE = math.log2(math.e) / math.sqrt(HD)
Z_ORDER = (0, -1, 1, -2, 2, -3, 3, 4)


def vmem():
    return pl.BlockSpec(memory_space=pltpu.VMEM)


def smem():
    return pl.BlockSpec(memory_space=pltpu.SMEM)


def hbm():
    return pl.BlockSpec(memory_space=pl.ANY)


def call(kernel, out_shape, args, in_specs, scratch=(), aliases=None, name=None, flops=0):
    return pl.pallas_call(
        kernel,
        out_shape=out_shape,
        in_specs=in_specs,
        out_specs=jax.tree.map(lambda s: vmem(), out_shape),
        scratch_shapes=list(scratch),
        input_output_aliases=aliases or {},
        compiler_params=pltpu.CompilerParams(vmem_limit_bytes=24 * 1024 * 1024),
        cost_estimate=pl.CostEstimate(flops=flops, transcendentals=0, bytes_accessed=0),
        name=name,
    )(*args)


def pack_kernel(key_hbm, value_hbm, out_ref, key_ref, value_ref, sems):
    copies = [
        pltpu.make_async_copy(key_hbm, key_ref, sems.at[0]),
        pltpu.make_async_copy(value_hbm, value_ref, sems.at[1]),
    ]
    for copy in copies:
        copy.start()
    for copy in copies:
        copy.wait()
    for t in range(2):
        rows = pl.ds(t * TILE, TILE)
        out_ref[t] = key_ref[rows, :]
        out_ref[2 + t] = value_ref[rows, :].astype(jnp.float32).T.astype(jnp.bfloat16)


def pack(key_rows, value_rows):
    rows = pltpu.VMEM((2 * TILE, HD), jnp.bfloat16)
    return call(
        pack_kernel,
        jax.ShapeDtypeStruct((4, TILE, TILE), jnp.bfloat16),
        (key_rows, value_rows),
        [hbm()] * 2,
        scratch=(rows, rows, pltpu.SemaphoreType.DMA((2,))),
        name="pack",
    )


def bundle_kernel(query_ref, mask_ref, unit_ref, out_ref):
    for t in range(2):
        for h in range(HEADS):
            out_ref[t * HEADS + h] = query_ref[pl.ds(t * TILE, TILE), pl.ds(h * HD, HD)]
    out_ref[MASK_AT] = jnp.zeros((TILE, TILE), jnp.bfloat16)
    out_ref[MASK_AT, 0:2, :] = mask_ref[...].astype(jnp.float32).astype(jnp.bfloat16)
    out_ref[UNIT_AT:] = unit_ref[...]


def bundle(queries, tile_mask, unit):
    shape = jax.ShapeDtypeStruct((UNIT_AT + 4, TILE, TILE), jnp.bfloat16)
    return call(bundle_kernel, shape, (queries, tile_mask, unit), [vmem()] * 3, name="bundle")


def half_kernel(half_ref, source_ref, out_ref, sems):
    rows = out_ref.shape[0] // 8
    start = pl.multiple_of(half_ref[0] * out_ref.shape[1], out_ref.shape[1])
    copies = [
        pltpu.make_async_copy(
            source_ref.at[pl.ds(i * rows, rows), pl.ds(start, out_ref.shape[1])],
            out_ref.at[pl.ds(i * rows, rows), :],
            sems.at[i],
        )
        for i in range(8)
    ]
    for copy in copies:
        copy.start()
    for copy in copies:
        copy.wait()


def column_half(source, number):
    return pl.pallas_call(
        half_kernel,
        out_shape=jax.ShapeDtypeStruct((source.shape[0], source.shape[1] // 2), source.dtype),
        in_specs=[smem(), hbm()],
        out_specs=hbm(),
        scratch_shapes=[pltpu.SemaphoreType.DMA((8,))],
        name="column_half",
    )(number.reshape(1).astype(jnp.int32), source)


def join_kernel(*refs):
    out_ref = refs[-1]
    at = 0
    for ref in refs[:-1]:
        out_ref[pl.ds(at, ref.shape[0])] = ref[...]
        at += ref.shape[0]


def join(parts):
    total = sum(p.shape[0] for p in parts)
    shape = jax.ShapeDtypeStruct((total, *parts[0].shape[1:]), parts[0].dtype)
    return call(join_kernel, shape, parts, [vmem()] * len(parts), name="join")


def stage_kernel(columns, count, numbers, first, table_ref, mine_ref, theirs_ref, *refs):
    parts, refs = refs[:count], refs[count:]
    targets = sorted({number // 2 for number in numbers})
    if not first:
        refs = refs[len(targets) :]
    states, (tiles_ref, list_ref) = refs[: len(targets)], refs[len(targets) :]
    x, z, core = table_ref[4, 0], table_ref[4, 1], table_ref[4, 2]
    at = 0
    for part in parts:
        tiles_ref[pl.ds(at, part.shape[0])] = part[...]
        at += part.shape[0]
    if first:
        for ref in states:
            ref[:, :MAX_ROW, :] = jnp.zeros((2, MAX_ROW, WIDE), jnp.float32)
            ref[:, MAX_ROW:, :] = jnp.full((2, ROWS - MAX_ROW, WIDE), NEGATIVE, jnp.float32)

    counts = [jnp.int32(0)] * 4
    slot = 0
    for dx, order in columns:
        for dz in order:
            block = lax.rem(x + dx + NX, NX) * NZ + lax.rem(z + dz + NZ, NZ)
            for r in range(2):
                tile = (block * 2 + core) * 2 + r
                for number in numbers:
                    list_ref[number, counts[number]] = slot // 2 * 4 + slot % 2
                    counts[number] = counts[number] + table_ref[number, tile]
                slot += 1

    for number in numbers:
        state_ref = states[targets.index(number // 2)]
        total = counts[number]
        source = mine_ref if number < 2 else theirs_ref

        def one_block(turn, carry, number=number, state_ref=state_ref, total=total, source=source):
            row = number % 2
            base = turn * BLOCK
            first_at = list_ref[number, base]
            at, values = [first_at], []
            ones = jnp.ones((16, TILE), jnp.bfloat16)
            for j in range(BLOCK):
                if j:
                    live = base + j < total
                    at.append(jnp.where(live, list_ref[number, base + j], first_at))
                value = jnp.concatenate([tiles_ref[at[j] + 2], ones], axis=0)
                if j:
                    value = value * jnp.where(live, 1.0, 0.0).astype(jnp.bfloat16)
                values.append(value)
            values = jnp.concatenate(values, axis=1)
            keys = jnp.concatenate([tiles_ref[i] for i in at], axis=0)
            chunks = [pl.ds(c * TILE, TILE) for c in range(HEADS)]
            scores = [
                lax.dot_general(
                    keys,
                    source[row * HEADS + h],
                    (((1,), (1,)), ((), ())),
                    preferred_element_type=jnp.float32,
                )
                for h in range(HEADS)
            ]
            probs = []
            for lanes, score in zip(chunks, scores):
                old_max = state_ref[row, pl.ds(MAX_ROW, 1), lanes]
                new_max = jnp.maximum(old_max, jnp.max(score, axis=0, keepdims=True))
                prob = jnp.exp2((score - new_max) * EXP2_SCALE).astype(jnp.bfloat16)
                probs.append((prob, jnp.exp2((old_max - new_max) * EXP2_SCALE)))
                state_ref[row, pl.ds(MAX_ROW, 8), lanes] = jnp.broadcast_to(new_max, (8, TILE))
            for lanes, (prob, fade) in zip(chunks, probs):
                part = lax.dot_general(
                    values, prob, (((1,), (0,)), ((), ())), preferred_element_type=jnp.float32
                )
                state_ref[row, pl.ds(0, MAX_ROW), lanes] = (
                    state_ref[row, pl.ds(0, MAX_ROW), lanes] * fade + part
                )
            return carry

        lax.fori_loop(0, (total + BLOCK - 1) // BLOCK, one_block, 0)


def stage(columns, near, parts, state, numbers, name):
    shape = jax.ShapeDtypeStruct((2, ROWS, WIDE), jnp.float32)
    slots = sum(2 * len(order) for _, order in columns)
    args = [*near, *parts]
    outs = len({number // 2 for number in numbers})
    aliases = {}
    if state is not None:
        aliases = {len(args) + i: i for i in range(outs)}
        args += list(state)
    kernel = lambda *refs: stage_kernel(columns, len(parts), numbers, state is None, *refs)
    return call(
        kernel,
        (shape,) * outs,
        args,
        [smem()] + [vmem()] * (len(args) - 1),
        scratch=(
            pltpu.VMEM((2 * slots, TILE, TILE), jnp.bfloat16),
            pltpu.SMEM((4, slots + BLOCK), jnp.int32),
        ),
        aliases=aliases,
        name=name,
    )


def merge_kernel(own_ref, other_ref, out_ref):
    for t in range(2):
        own_max = own_ref[t, pl.ds(MAX_ROW, 1), :]
        other_max = other_ref[t, pl.ds(MAX_ROW, 1), :]
        row_max = jnp.maximum(own_max, other_max)
        own_weight = jnp.exp2((own_max - row_max) * EXP2_SCALE)
        other_weight = jnp.exp2((other_max - row_max) * EXP2_SCALE)
        total = (
            own_ref[t, pl.ds(SUM_ROW, 1), :] * own_weight
            + other_ref[t, pl.ds(SUM_ROW, 1), :] * other_weight
        )
        own_weight = own_weight / total
        other_weight = other_weight / total
        for h in range(HEADS):
            lanes = slice(h * TILE, (h + 1) * TILE)
            attended = (
                own_ref[t, pl.ds(0, HD), lanes] * own_weight[:, lanes]
                + other_ref[t, pl.ds(0, HD), lanes] * other_weight[:, lanes]
            )
            out_ref[pl.ds(t * TILE, TILE), pl.ds(h * HD, HD)] = attended.T.astype(jnp.bfloat16)


def ring(size, step):
    return [(i, (i + step) % size) for i in range(size)]


def along_y(move):
    pairs = []
    for i in range(8):
        yh, yl, core = move(i // 4, i // 2 % 2, i % 2)
        pairs.append((i, yh % 2 * 4 + yl % 2 * 2 + core % 2))
    return pairs


def next_y(yh, yl, step):
    y = (yh * 2 + yl + step) % 4
    return y // 2, y % 2


Y = ("yh", "yl", "core")
YZ = ("z", "yh", "yl", "core")


def turned(shift):
    turn = along_y(lambda yh, yl, core: (core, yl, yh))
    return [(z * 8 + a, (z + shift) % NZ * 8 + b) for z in range(NZ) for a, b in turn]


def project_kernel(flip, place_ref, near_ref, far_ref, weight_ref, far_weight_ref, out_ref, own_ref, sems):
    width = out_ref.shape[1]
    parts = width // 256
    which = place_ref[1] + flip - 2 * flip * place_ref[1]
    base = pl.multiple_of(place_ref[0] * (2 * width) + which * width, 256)
    copies = [
        pltpu.make_async_copy(
            weight_ref.at[:, pl.ds(base + n * 256, 256)], own_ref.at[n], sems.at[n]
        )
        for n in range(parts)
    ]
    for copy in copies:
        copy.start()
    for n in range(parts):
        at = pl.multiple_of(which * width + n * 256, 256)
        total = jnp.dot(
            far_ref[...], far_weight_ref[:, pl.ds(at, 256)], preferred_element_type=jnp.float32
        )
        copies[n].wait()
        total = total + jnp.dot(near_ref[...], own_ref[n], preferred_element_type=jnp.float32)
        out_ref[:, n * 256 : (n + 1) * 256] = total.astype(out_ref.dtype)


def project(flip, place, near, far, weight, far_weight, dtype, name):
    width = far_weight.shape[1] // 2
    shape = jax.ShapeDtypeStruct((near.shape[0], width), dtype)
    return call(
        lambda *refs: project_kernel(flip, *refs),
        shape,
        (place, near, far, weight, far_weight),
        [smem(), vmem(), vmem(), hbm(), vmem()],
        scratch=(
            pltpu.VMEM((width // 256, weight.shape[0], 256), jnp.bfloat16),
            pltpu.SemaphoreType.DMA((width // 256,)),
        ),
        name=name,
    )


def add_kernel(keep_ref, other_ref, out_ref):
    out_ref[...] = (keep_ref[...] + other_ref[...].astype(jnp.float32)).astype(out_ref.dtype)


def per_device(queries, key_rows, value_rows, tile_mask, out_weight):
    x, z = lax.axis_index("x"), lax.axis_index("z")
    yh, yl, core = lax.axis_index("yh"), lax.axis_index("yl"), lax.axis_index("core")
    turn = along_y(lambda yh, yl, core: (core, yl, yh))
    swap = [(0, 1), (1, 0)]
    together = lax.optimization_barrier

    unit = pack(key_rows, value_rows)
    up, down = ring(NZ, 1), ring(NZ, -1)
    units = {-1: lax.ppermute(unit, YZ, turned(1)), 1: lax.ppermute(unit, YZ, turned(-1))}
    mine = lax.ppermute(bundle(queries, tile_mask, unit), Y, turn)
    half_away = column_half(out_weight, 1 - yl)
    away = along_y(lambda yh, yl, core: (*next_y(yh, yl, 1 - 2 * core), core))
    units[-2] = lax.ppermute(units[-1], "z", up)
    units[2] = lax.ppermute(units[1], "z", down)
    units[-2], units[2], half_away = together((units[-2], units[2], half_away))
    far_weight = lax.ppermute(half_away, Y, away)
    units[-3] = lax.ppermute(units[-2], "z", up)
    units[3] = lax.ppermute(units[2], "z", down)
    units[-3], units[3], mine = together((units[-3], units[3], mine))
    far = [
        lax.ppermute(units[-3][:2], "z", up),
        lax.ppermute(units[3][2:], "z", down),
    ]
    theirs = lax.ppermute(mine, "core", swap)
    *far, theirs = together((*far, theirs))
    place = jnp.pad(jnp.stack([x, z, core]).astype(jnp.int32), (0, 125))[None]
    masks = jnp.concatenate([mine[MASK_AT, :2], theirs[MASK_AT, :2]]).astype(jnp.int32)
    table = jnp.concatenate([masks, place])

    units[0] = mine[UNIT_AT:]
    column = join([units[d] for d in Z_ORDER[:-1]] + far)
    forth, back = ring(NX, 1), ring(NX, -1)
    before = lax.ppermute(column, "x", forth)
    after = lax.ppermute(column, "x", back)
    near = (table, mine, theirs)
    every = (0, 1, 2, 3)
    state = stage(((0, Z_ORDER),), near, [column], None, every, "stage_a")
    before, after, *state = together((before, after, *state))
    half = column.shape[0] // 2
    far_low = lax.ppermute(before[:half], "x", forth)
    far_high = lax.ppermute(after[half:], "x", back)
    keep, send = stage(
        ((-1, Z_ORDER), (1, Z_ORDER)), near, [before, after], state, every, "stage_b"
    )
    far_low, far_high, keep, send = together((far_low, far_high, keep, send))
    last = (((2, Z_ORDER),), near, [far_low, far_high])
    (send,) = stage(*last, (send,), (2, 3), "stage_c")
    received = lax.ppermute(send, "core", swap)
    (keep,) = stage(*last, (keep,), (0, 1), "stage_d")
    keep, received, far_weight = together((keep, received, far_weight))
    shape = jax.ShapeDtypeStruct((2 * TILE, WIDE), jnp.bfloat16)
    attended = call(merge_kernel, shape, (keep, received), [vmem()] * 2, name="merge")

    near_part = lax.ppermute(attended, Y, turn)
    far_part = lax.ppermute(attended, Y, along_y(lambda yh, yl, core: (core, 1 - yl, yh)))
    where = jnp.stack([yl, core]).astype(jnp.int32)
    sides = (where, near_part, far_part, out_weight, far_weight)
    other = project(1, *sides, jnp.bfloat16, "project_send")
    other = lax.ppermute(other, "core", swap)
    own = project(0, *sides, jnp.float32, "project_keep")
    shape = jax.ShapeDtypeStruct(own.shape, jnp.bfloat16)
    return call(add_kernel, shape, (own, other), [vmem()] * 2, name="add")


def solution(mesh):
    fine = Mesh(mesh.devices.reshape(NX, NZ, 2, 2, 2), ("x", "z", "yh", "yl", "core"))
    tok, head = ("x", "z", "yh"), ("yl", "core")
    return jax.shard_map(
        per_device,
        mesh=fine,
        in_specs=(P(tok, head), P(tok, head), P(tok, head), P(tok, None), P(head, None)),
        out_specs=P(tok, head),
        check_vma=False,
    )
```

```python
import math

import jax
import jax.numpy as jnp
from jax import lax
from jax.experimental import pallas as pl
from jax.experimental.pallas import tpu as pltpu
from jax.sharding import Mesh, PartitionSpec as P

HD = 128
TILE = 128
NX, NZ = 4, 8
HEADS = 6
WIDE = HEADS * TILE
SUM_ROW = HD
MAX_ROW = HD + 16
ROWS = HD + 24
NEGATIVE = -1e30
BLOCK = 4
MASK_AT = 2 * HEADS
UNIT_AT = MASK_AT + 1
EXP2_SCALE = math.log2(math.e) / math.sqrt(HD)
Z_ORDER = (0, -1, 1, -2, 2, -3, 3, 4)


def vmem():
    return pl.BlockSpec(memory_space=pltpu.VMEM)


def smem():
    return pl.BlockSpec(memory_space=pltpu.SMEM)


def hbm():
    return pl.BlockSpec(memory_space=pl.ANY)


def call(kernel, out_shape, args, in_specs, scratch=(), aliases=None, name=None, flops=0):
    return pl.pallas_call(
        kernel,
        out_shape=out_shape,
        in_specs=in_specs,
        out_specs=jax.tree.map(lambda s: vmem(), out_shape),
        scratch_shapes=list(scratch),
        input_output_aliases=aliases or {},
        compiler_params=pltpu.CompilerParams(vmem_limit_bytes=24 * 1024 * 1024),
        cost_estimate=pl.CostEstimate(flops=flops, transcendentals=0, bytes_accessed=0),
        name=name,
    )(*args)


def pack_kernel(key_hbm, value_hbm, out_ref, key_ref, value_ref, sems):
    copies = [
        pltpu.make_async_copy(key_hbm, key_ref, sems.at[0]),
        pltpu.make_async_copy(value_hbm, value_ref, sems.at[1]),
    ]
    for copy in copies:
        copy.start()
    for copy in copies:
        copy.wait()
    for t in range(2):
        rows = pl.ds(t * TILE, TILE)
        out_ref[t] = key_ref[rows, :]
        out_ref[2 + t] = value_ref[rows, :].astype(jnp.float32).T.astype(jnp.bfloat16)


def pack(key_rows, value_rows):
    rows = pltpu.VMEM((2 * TILE, HD), jnp.bfloat16)
    return call(
        pack_kernel,
        jax.ShapeDtypeStruct((4, TILE, TILE), jnp.bfloat16),
        (key_rows, value_rows),
        [hbm()] * 2,
        scratch=(rows, rows, pltpu.SemaphoreType.DMA((2,))),
        name="pack",
    )


def bundle_kernel(query_ref, mask_ref, unit_ref, out_ref):
    for t in range(2):
        for h in range(HEADS):
            out_ref[t * HEADS + h] = query_ref[pl.ds(t * TILE, TILE), pl.ds(h * HD, HD)]
    out_ref[MASK_AT] = jnp.zeros((TILE, TILE), jnp.bfloat16)
    out_ref[MASK_AT, 0:2, :] = mask_ref[...].astype(jnp.float32).astype(jnp.bfloat16)
    out_ref[UNIT_AT:] = unit_ref[...]


def bundle(queries, tile_mask, unit):
    shape = jax.ShapeDtypeStruct((UNIT_AT + 4, TILE, TILE), jnp.bfloat16)
    return call(bundle_kernel, shape, (queries, tile_mask, unit), [vmem()] * 3, name="bundle")


def half_kernel(half_ref, source_ref, out_ref, sems):
    rows = out_ref.shape[0] // 8
    start = pl.multiple_of(half_ref[0] * out_ref.shape[1], out_ref.shape[1])
    copies = [
        pltpu.make_async_copy(
            source_ref.at[pl.ds(i * rows, rows), pl.ds(start, out_ref.shape[1])],
            out_ref.at[pl.ds(i * rows, rows), :],
            sems.at[i],
        )
        for i in range(8)
    ]
    for copy in copies:
        copy.start()
    for copy in copies:
        copy.wait()


def column_half(source, number):
    return call(
        half_kernel,
        jax.ShapeDtypeStruct((source.shape[0], source.shape[1] // 2), source.dtype),
        (number.reshape(1).astype(jnp.int32), source),
        [smem(), hbm()],
        scratch=(pltpu.SemaphoreType.DMA((8,)),),
        name="column_half",
    )


def join_kernel(*refs):
    out_ref = refs[-1]
    at = 0
    for ref in refs[:-1]:
        out_ref[pl.ds(at, ref.shape[0])] = ref[...]
        at += ref.shape[0]


def join(parts):
    total = sum(p.shape[0] for p in parts)
    shape = jax.ShapeDtypeStruct((total, *parts[0].shape[1:]), parts[0].dtype)
    return call(join_kernel, shape, parts, [vmem()] * len(parts), name="join")


def stage_kernel(columns, count, numbers, first, table_ref, mine_ref, theirs_ref, *refs):
    parts, refs = refs[:count], refs[count:]
    targets = sorted({number // 2 for number in numbers})
    if not first:
        refs = refs[len(targets) :]
    states, (tiles_ref, list_ref) = refs[: len(targets)], refs[len(targets) :]
    x, z, core = table_ref[4, 0], table_ref[4, 1], table_ref[4, 2]
    at = 0
    for part in parts:
        tiles_ref[pl.ds(at, part.shape[0])] = part[...]
        at += part.shape[0]
    if first:
        for ref in states:
            ref[:, :MAX_ROW, :] = jnp.zeros((2, MAX_ROW, WIDE), jnp.float32)
            ref[:, MAX_ROW:, :] = jnp.full((2, ROWS - MAX_ROW, WIDE), NEGATIVE, jnp.float32)

    counts = [jnp.int32(0)] * 4
    slot = 0
    for dx, order in columns:
        for dz in order:
            block = lax.rem(x + dx + NX, NX) * NZ + lax.rem(z + dz + NZ, NZ)
            for r in range(2):
                tile = (block * 2 + core) * 2 + r
                for number in numbers:
                    list_ref[number, counts[number]] = slot // 2 * 4 + slot % 2
                    counts[number] = counts[number] + table_ref[number, tile]
                slot += 1

    for number in numbers:
        state_ref = states[targets.index(number // 2)]
        total = counts[number]
        source = mine_ref if number < 2 else theirs_ref

        def one_block(turn, carry, number=number, state_ref=state_ref, total=total, source=source):
            row = number % 2
            base = turn * BLOCK
            first_at = list_ref[number, base]
            at, values = [first_at], []
            ones = jnp.ones((16, TILE), jnp.bfloat16)
            for j in range(BLOCK):
                if j:
                    live = base + j < total
                    at.append(jnp.where(live, list_ref[number, base + j], first_at))
                value = jnp.concatenate([tiles_ref[at[j] + 2], ones], axis=0)
                if j:
                    value = value * jnp.where(live, 1.0, 0.0).astype(jnp.bfloat16)
                values.append(value)
            values = jnp.concatenate(values, axis=1)
            keys = jnp.concatenate([tiles_ref[i] for i in at], axis=0)
            chunks = [pl.ds(c * TILE, TILE) for c in range(HEADS)]
            scores = [
                lax.dot_general(
                    keys,
                    source[row * HEADS + h],
                    (((1,), (1,)), ((), ())),
                    preferred_element_type=jnp.float32,
                )
                for h in range(HEADS)
            ]
            probs = []
            for lanes, score in zip(chunks, scores):
                old_max = state_ref[row, pl.ds(MAX_ROW, 1), lanes]
                new_max = jnp.maximum(old_max, jnp.max(score, axis=0, keepdims=True))
                prob = jnp.exp2((score - new_max) * EXP2_SCALE).astype(jnp.bfloat16)
                probs.append((prob, jnp.exp2((old_max - new_max) * EXP2_SCALE)))
                state_ref[row, pl.ds(MAX_ROW, 8), lanes] = jnp.broadcast_to(new_max, (8, TILE))
            for lanes, (prob, fade) in zip(chunks, probs):
                part = lax.dot_general(
                    values, prob, (((1,), (0,)), ((), ())), preferred_element_type=jnp.float32
                )
                state_ref[row, pl.ds(0, MAX_ROW), lanes] = (
                    state_ref[row, pl.ds(0, MAX_ROW), lanes] * fade + part
                )
            return carry

        lax.fori_loop(0, (total + BLOCK - 1) // BLOCK, one_block, 0)


def stage(columns, near, parts, state, numbers, name):
    shape = jax.ShapeDtypeStruct((2, ROWS, WIDE), jnp.float32)
    slots = sum(2 * len(order) for _, order in columns)
    args = [*near, *parts]
    outs = len({number // 2 for number in numbers})
    aliases = {}
    if state is not None:
        aliases = {len(args) + i: i for i in range(outs)}
        args += list(state)
    kernel = lambda *refs: stage_kernel(columns, len(parts), numbers, state is None, *refs)
    return call(
        kernel,
        (shape,) * outs,
        args,
        [smem()] + [vmem()] * (len(args) - 1),
        scratch=(
            pltpu.VMEM((2 * slots, TILE, TILE), jnp.bfloat16),
            pltpu.SMEM((4, slots + BLOCK), jnp.int32),
        ),
        aliases=aliases,
        name=name,
    )


def merge_kernel(own_ref, other_ref, out_ref):
    for t in range(2):
        own_max = own_ref[t, pl.ds(MAX_ROW, 1), :]
        other_max = other_ref[t, pl.ds(MAX_ROW, 1), :]
        row_max = jnp.maximum(own_max, other_max)
        own_weight = jnp.exp2((own_max - row_max) * EXP2_SCALE)
        other_weight = jnp.exp2((other_max - row_max) * EXP2_SCALE)
        total = (
            own_ref[t, pl.ds(SUM_ROW, 1), :] * own_weight
            + other_ref[t, pl.ds(SUM_ROW, 1), :] * other_weight
        )
        own_weight = own_weight / total
        other_weight = other_weight / total
        for h in range(HEADS):
            lanes = slice(h * TILE, (h + 1) * TILE)
            attended = (
                own_ref[t, pl.ds(0, HD), lanes] * own_weight[:, lanes]
                + other_ref[t, pl.ds(0, HD), lanes] * other_weight[:, lanes]
            )
            out_ref[pl.ds(t * TILE, TILE), pl.ds(h * HD, HD)] = attended.T.astype(jnp.bfloat16)


def ring(size, step):
    return [(i, (i + step) % size) for i in range(size)]


def along_y(move):
    pairs = []
    for i in range(8):
        yh, yl, core = move(i // 4, i // 2 % 2, i % 2)
        pairs.append((i, yh % 2 * 4 + yl % 2 * 2 + core % 2))
    return pairs


def next_y(yh, yl, step):
    y = (yh * 2 + yl + step) % 4
    return y // 2, y % 2


Y = ("yh", "yl", "core")
YZ = ("z", "yh", "yl", "core")


def turned(shift):
    turn = along_y(lambda yh, yl, core: (core, yl, yh))
    return [(z * 8 + a, (z + shift) % NZ * 8 + b) for z in range(NZ) for a, b in turn]


def project_kernel(flip, place_ref, near_ref, far_ref, weight_ref, far_weight_ref, out_ref):
    width = out_ref.shape[1]
    which = place_ref[1] + flip - 2 * flip * place_ref[1]
    for n in range(width // 256):
        at = pl.multiple_of(which * width + n * 256, 256)
        far = far_weight_ref[:, pl.ds(at, 256)]
        total = jnp.dot(far_ref[...], far, preferred_element_type=jnp.float32)
        at = pl.multiple_of(place_ref[0] * (2 * width) + which * width + n * 256, 256)
        near = weight_ref[:, pl.ds(at, 256)]
        total = total + jnp.dot(near_ref[...], near, preferred_element_type=jnp.float32)
        out_ref[:, n * 256 : (n + 1) * 256] = total.astype(out_ref.dtype)


def project(flip, place, near, far, weight, far_weight, dtype, name):
    shape = jax.ShapeDtypeStruct((near.shape[0], far_weight.shape[1] // 2), dtype)
    return call(
        lambda *refs: project_kernel(flip, *refs),
        shape,
        (place, near, far, weight, far_weight),
        [smem()] + [vmem()] * 4,
        name=name,
    )


def add_kernel(keep_ref, other_ref, out_ref):
    out_ref[...] = (keep_ref[...] + other_ref[...].astype(jnp.float32)).astype(out_ref.dtype)


def per_device(queries, key_rows, value_rows, tile_mask, out_weight):
    x, z = lax.axis_index("x"), lax.axis_index("z")
    yh, yl, core = lax.axis_index("yh"), lax.axis_index("yl"), lax.axis_index("core")
    turn = along_y(lambda yh, yl, core: (core, yl, yh))
    swap = [(0, 1), (1, 0)]
    together = lax.optimization_barrier

    unit = pack(key_rows, value_rows)
    up, down = ring(NZ, 1), ring(NZ, -1)
    units = {-1: lax.ppermute(unit, YZ, turned(1)), 1: lax.ppermute(unit, YZ, turned(-1))}
    queries, units[-1], units[1] = together((queries, units[-1], units[1]))
    mine = lax.ppermute(bundle(queries, tile_mask, unit), Y, turn)
    half_away = column_half(out_weight, 1 - yl)
    away = along_y(lambda yh, yl, core: (*next_y(yh, yl, 1 - 2 * core), core))
    units[-2] = lax.ppermute(units[-1], "z", up)
    units[2] = lax.ppermute(units[1], "z", down)
    units[-2], units[2], half_away = together((units[-2], units[2], half_away))
    units[-3] = lax.ppermute(units[-2], "z", up)
    units[3] = lax.ppermute(units[2], "z", down)
    units[-3], units[3], mine, half_away = together((units[-3], units[3], mine, half_away))
    far_weight = lax.ppermute(half_away, Y, away)
    far = [
        lax.ppermute(units[-3][:2], "z", up),
        lax.ppermute(units[3][2:], "z", down),
    ]
    theirs = lax.ppermute(mine, "core", swap)
    *far, theirs = together((*far, theirs))
    place = jnp.pad(jnp.stack([x, z, core]).astype(jnp.int32), (0, 125))[None]
    masks = jnp.concatenate([mine[MASK_AT, :2], theirs[MASK_AT, :2]]).astype(jnp.int32)
    table = jnp.concatenate([masks, place])

    units[0] = mine[UNIT_AT:]
    column = join([units[d] for d in Z_ORDER[:-1]] + far)
    forth, back = ring(NX, 1), ring(NX, -1)
    before = lax.ppermute(column, "x", forth)
    after = lax.ppermute(column, "x", back)
    near = (table, mine, theirs)
    every = (0, 1, 2, 3)
    state = stage(((0, Z_ORDER),), near, [column], None, every, "stage_a")
    before, after, *state = together((before, after, *state))
    half = column.shape[0] // 2
    far_low = lax.ppermute(before[:half], "x", forth)
    far_high = lax.ppermute(after[half:], "x", back)
    keep, send = stage(
        ((-1, Z_ORDER), (1, Z_ORDER)), near, [before, after], state, every, "stage_b"
    )
    far_low, far_high, keep, send = together((far_low, far_high, keep, send))
    last = (((2, Z_ORDER),), near, [far_low, far_high])
    (send,) = stage(*last, (send,), (2, 3), "stage_c")
    received = lax.ppermute(send, "core", swap)
    (keep,) = stage(*last, (keep,), (0, 1), "stage_d")
    keep, received, far_weight = together((keep, received, far_weight))
    shape = jax.ShapeDtypeStruct((2 * TILE, WIDE), jnp.bfloat16)
    attended = call(merge_kernel, shape, (keep, received), [vmem()] * 2, name="merge")

    near_part = lax.ppermute(attended, Y, turn)
    far_part = lax.ppermute(attended, Y, along_y(lambda yh, yl, core: (core, 1 - yl, yh)))
    where = jnp.stack([yl, core]).astype(jnp.int32)
    sides = (where, near_part, far_part, out_weight, far_weight)
    other = project(1, *sides, jnp.bfloat16, "project_send")
    other = lax.ppermute(other, "core", swap)
    own = project(0, *sides, jnp.float32, "project_keep")
    shape = jax.ShapeDtypeStruct(own.shape, jnp.bfloat16)
    return call(add_kernel, shape, (own, other), [vmem()] * 2, name="add")


def solution(mesh):
    fine = Mesh(mesh.devices.reshape(NX, NZ, 2, 2, 2), ("x", "z", "yh", "yl", "core"))
    tok, head = ("x", "z", "yh"), ("yl", "core")
    return jax.shard_map(
        per_device,
        mesh=fine,
        in_specs=(P(tok, head), P(tok, head), P(tok, head), P(tok, None), P(head, None)),
        out_specs=P(tok, head),
        check_vma=False,
    )
```

```python
import math

import jax
import jax.numpy as jnp
from jax import lax
from jax.experimental import pallas as pl
from jax.experimental.pallas import tpu as pltpu
from jax.sharding import Mesh, PartitionSpec as P

HD = 128
TILE = 128
NX, NZ = 4, 8
HEADS = 6
WIDE = HEADS * TILE
SUM_ROW = HD
MAX_ROW = HD + 16
ROWS = HD + 24
NEGATIVE = -1e30
MASK_AT = 2 * HEADS
UNIT_AT = MASK_AT + 1
EXP2_SCALE = math.log2(math.e) / math.sqrt(HD)
EARLY = (-1, 1, -2, 2)
LATE = (0, -3, 3, 4)


def vmem():
    return pl.BlockSpec(memory_space=pltpu.VMEM)


def smem():
    return pl.BlockSpec(memory_space=pltpu.SMEM)


def hbm():
    return pl.BlockSpec(memory_space=pl.ANY)


def call(kernel, out_shape, args, in_specs, scratch=(), aliases=None, name=None, flops=0):
    return pl.pallas_call(
        kernel,
        out_shape=out_shape,
        in_specs=in_specs,
        out_specs=jax.tree.map(lambda s: vmem(), out_shape),
        scratch_shapes=list(scratch),
        input_output_aliases=aliases or {},
        compiler_params=pltpu.CompilerParams(vmem_limit_bytes=24 * 1024 * 1024),
        cost_estimate=pl.CostEstimate(flops=flops, transcendentals=0, bytes_accessed=0),
        name=name,
    )(*args)


def pack_kernel(key_hbm, value_hbm, out_ref, key_ref, value_ref, sems):
    copies = [
        pltpu.make_async_copy(key_hbm, key_ref, sems.at[0]),
        pltpu.make_async_copy(value_hbm, value_ref, sems.at[1]),
    ]
    for copy in copies:
        copy.start()
    for copy in copies:
        copy.wait()
    for t in range(2):
        rows = pl.ds(t * TILE, TILE)
        out_ref[t] = key_ref[rows, :]
        out_ref[2 + t] = value_ref[rows, :].astype(jnp.float32).T.astype(jnp.bfloat16)


def pack(key_rows, value_rows):
    rows = pltpu.VMEM((2 * TILE, HD), jnp.bfloat16)
    return call(
        pack_kernel,
        jax.ShapeDtypeStruct((4, TILE, TILE), jnp.bfloat16),
        (key_rows, value_rows),
        [hbm()] * 2,
        scratch=(rows, rows, pltpu.SemaphoreType.DMA((2,))),
        name="pack",
    )


def bundle_kernel(query_ref, mask_ref, unit_ref, out_ref):
    for t in range(2):
        for h in range(HEADS):
            out_ref[t * HEADS + h] = query_ref[pl.ds(t * TILE, TILE), pl.ds(h * HD, HD)]
    out_ref[MASK_AT] = jnp.zeros((TILE, TILE), jnp.bfloat16)
    out_ref[MASK_AT, 0:2, :] = mask_ref[...].astype(jnp.float32).astype(jnp.bfloat16)
    out_ref[UNIT_AT:] = unit_ref[...]


def bundle(queries, tile_mask, unit):
    shape = jax.ShapeDtypeStruct((UNIT_AT + 4, TILE, TILE), jnp.bfloat16)
    return call(bundle_kernel, shape, (queries, tile_mask, unit), [vmem()] * 3, name="bundle")


def half_kernel(half_ref, source_ref, out_ref, sems):
    rows = out_ref.shape[0] // 8
    start = pl.multiple_of(half_ref[0] * out_ref.shape[1], out_ref.shape[1])
    copies = [
        pltpu.make_async_copy(
            source_ref.at[pl.ds(i * rows, rows), pl.ds(start, out_ref.shape[1])],
            out_ref.at[pl.ds(i * rows, rows), :],
            sems.at[i],
        )
        for i in range(8)
    ]
    for copy in copies:
        copy.start()
    for copy in copies:
        copy.wait()


def column_half(source, number):
    return call(
        half_kernel,
        jax.ShapeDtypeStruct((source.shape[0], source.shape[1] // 2), source.dtype),
        (number.reshape(1).astype(jnp.int32), source),
        [smem(), hbm()],
        scratch=(pltpu.SemaphoreType.DMA((8,)),),
        name="column_half",
    )


def join_kernel(*refs):
    out_ref = refs[-1]
    at = 0
    for ref in refs[:-1]:
        out_ref[pl.ds(at, ref.shape[0])] = ref[...]
        at += ref.shape[0]


def join(parts):
    total = sum(p.shape[0] for p in parts)
    shape = jax.ShapeDtypeStruct((total, *parts[0].shape[1:]), parts[0].dtype)
    return call(join_kernel, shape, parts, [vmem()] * len(parts), name="join")


def stage_kernel(columns, count, numbers, first, table_ref, mine_ref, theirs_ref, *refs):
    parts, refs = refs[:count], refs[count:]
    targets = sorted({number // 2 for number in numbers})
    if not first:
        refs = refs[len(targets) :]
    states, (tiles_ref, list_ref) = refs[: len(targets)], refs[len(targets) :]
    x, z, core = table_ref[4, 0], table_ref[4, 1], table_ref[4, 2]
    at = 0
    for part in parts:
        tiles_ref[pl.ds(at, part.shape[0])] = part[...]
        at += part.shape[0]
    if first:
        for ref in states:
            ref[:, :MAX_ROW, :] = jnp.zeros((2, MAX_ROW, WIDE), jnp.float32)
            ref[:, MAX_ROW:, :] = jnp.full((2, ROWS - MAX_ROW, WIDE), NEGATIVE, jnp.float32)

    counts = [jnp.int32(0)] * 4
    slot = 0
    for dx, order in columns:
        for dz in order:
            block = lax.rem(x + dx + NX, NX) * NZ + lax.rem(z + dz + NZ, NZ)
            for r in range(2):
                tile = (block * 2 + core) * 2 + r
                for number in numbers:
                    list_ref[number, counts[number]] = slot // 2 * 4 + slot % 2
                    counts[number] = counts[number] + table_ref[number, tile]
                slot += 1

    for number in numbers:
        list_ref[number, slot] = counts[number]

    def block(target, row, base, size):
        state_ref = states[targets.index(target)]
        source = theirs_ref if target else mine_ref
        number = 2 * target + row
        at = [list_ref[number, base + j] for j in range(size - 1)]
        live = base + size - 1 < list_ref[number, slot]
        at.append(jnp.where(live, list_ref[number, base + size - 1], at[0]))
        ones = jnp.ones((16, TILE), jnp.bfloat16)
        values = [jnp.concatenate([tiles_ref[i + 2], ones], axis=0) for i in at]
        values[-1] = values[-1] * jnp.where(live, 1.0, 0.0).astype(jnp.bfloat16)
        values = jnp.concatenate(values, axis=1)
        keys = jnp.concatenate([tiles_ref[i] for i in at], axis=0)
        chunks = [pl.ds(h * TILE, TILE) for h in range(HEADS)]
        scores = [
            lax.dot_general(
                keys,
                source[row * HEADS + h],
                (((1,), (1,)), ((), ())),
                preferred_element_type=jnp.float32,
            )
            for h in range(HEADS)
        ]
        probs = []
        for lanes, score in zip(chunks, scores):
            old_max = state_ref[row, pl.ds(MAX_ROW, 1), lanes]
            new_max = jnp.maximum(old_max, jnp.max(score, axis=0, keepdims=True))
            prob = jnp.exp2((score - new_max) * EXP2_SCALE).astype(jnp.bfloat16)
            probs.append((prob, jnp.exp2((old_max - new_max) * EXP2_SCALE)))
            state_ref[row, pl.ds(MAX_ROW, 8), lanes] = jnp.broadcast_to(new_max, (8, TILE))
        for lanes, (prob, fade) in zip(chunks, probs):
            part = lax.dot_general(
                values, prob, (((1,), (0,)), ((), ())), preferred_element_type=jnp.float32
            )
            state_ref[row, pl.ds(0, MAX_ROW), lanes] = (
                state_ref[row, pl.ds(0, MAX_ROW), lanes] * fade + part
            )

    def one_query_tile(target, row):
        total = list_ref[2 * target + row, slot]
        blocks = (total + 1) // 4
        rest = total - 4 * blocks

        def full(turn, carry):
            block(target, row, 4 * turn, 4)
            return carry

        lax.fori_loop(0, blocks, full, 0)

        @pl.when(rest > 0)
        def _():
            block(target, row, 4 * blocks, 2)

    for target in targets:
        for row in range(2):
            one_query_tile(target, row)


def stage(columns, near, parts, state, numbers, name):
    shape = jax.ShapeDtypeStruct((2, ROWS, WIDE), jnp.float32)
    slots = sum(2 * len(order) for _, order in columns)
    args = [*near, *parts]
    outs = len({number // 2 for number in numbers})
    aliases = {}
    if state is not None:
        aliases = {len(args) + i: i for i in range(outs)}
        args += list(state)
    kernel = lambda *refs: stage_kernel(columns, len(parts), numbers, state is None, *refs)
    return call(
        kernel,
        (shape,) * outs,
        args,
        [smem()] + [vmem()] * (len(args) - 1),
        scratch=(
            pltpu.VMEM((2 * slots, TILE, TILE), jnp.bfloat16),
            pltpu.SMEM((4, slots + 1), jnp.int32),
        ),
        aliases=aliases,
        name=name,
    )


def merge_kernel(own_ref, other_ref, out_ref):
    for t in range(2):
        own_max = own_ref[t, pl.ds(MAX_ROW, 1), :]
        other_max = other_ref[t, pl.ds(MAX_ROW, 1), :]
        row_max = jnp.maximum(own_max, other_max)
        own_weight = jnp.exp2((own_max - row_max) * EXP2_SCALE)
        other_weight = jnp.exp2((other_max - row_max) * EXP2_SCALE)
        total = (
            own_ref[t, pl.ds(SUM_ROW, 1), :] * own_weight
            + other_ref[t, pl.ds(SUM_ROW, 1), :] * other_weight
        )
        own_weight = own_weight / total
        other_weight = other_weight / total
        for h in range(HEADS):
            lanes = slice(h * TILE, (h + 1) * TILE)
            attended = (
                own_ref[t, pl.ds(0, HD), lanes] * own_weight[:, lanes]
                + other_ref[t, pl.ds(0, HD), lanes] * other_weight[:, lanes]
            )
            out_ref[pl.ds(t * TILE, TILE), pl.ds(h * HD, HD)] = attended.T.astype(jnp.bfloat16)


def ring(size, step):
    return [(i, (i + step) % size) for i in range(size)]


def along_y(move):
    pairs = []
    for i in range(8):
        yh, yl, core = move(i // 4, i // 2 % 2, i % 2)
        pairs.append((i, yh % 2 * 4 + yl % 2 * 2 + core % 2))
    return pairs


def next_y(yh, yl, step):
    y = (yh * 2 + yl + step) % 4
    return y // 2, y % 2


Y = ("yh", "yl", "core")
YZ = ("z", "yh", "yl", "core")


def turned(shift):
    turn = along_y(lambda yh, yl, core: (core, yl, yh))
    return [(z * 8 + a, (z + shift) % NZ * 8 + b) for z in range(NZ) for a, b in turn]


def project_kernel(flip, place_ref, near_ref, far_ref, weight_ref, far_weight_ref, out_ref):
    width = out_ref.shape[1]
    which = place_ref[1] + flip - 2 * flip * place_ref[1]
    for n in range(width // 256):
        at = pl.multiple_of(which * width + n * 256, 256)
        far = far_weight_ref[:, pl.ds(at, 256)]
        total = jnp.dot(far_ref[...], far, preferred_element_type=jnp.float32)
        at = pl.multiple_of(place_ref[0] * (2 * width) + which * width + n * 256, 256)
        near = weight_ref[:, pl.ds(at, 256)]
        total = total + jnp.dot(near_ref[...], near, preferred_element_type=jnp.float32)
        out_ref[:, n * 256 : (n + 1) * 256] = total.astype(out_ref.dtype)


def project(flip, place, near, far, weight, far_weight, dtype, name):
    shape = jax.ShapeDtypeStruct((near.shape[0], far_weight.shape[1] // 2), dtype)
    return call(
        lambda *refs: project_kernel(flip, *refs),
        shape,
        (place, near, far, weight, far_weight),
        [smem()] + [vmem()] * 4,
        name=name,
    )


def add_kernel(keep_ref, other_ref, out_ref):
    out_ref[...] = (keep_ref[...] + other_ref[...].astype(jnp.float32)).astype(out_ref.dtype)


def per_device(queries, key_rows, value_rows, tile_mask, out_weight):
    x, z = lax.axis_index("x"), lax.axis_index("z")
    yh, yl, core = lax.axis_index("yh"), lax.axis_index("yl"), lax.axis_index("core")
    turn = along_y(lambda yh, yl, core: (core, yl, yh))
    swap = [(0, 1), (1, 0)]
    together = lax.optimization_barrier

    unit = pack(key_rows, value_rows)
    up, down = ring(NZ, 1), ring(NZ, -1)
    units = {-1: lax.ppermute(unit, YZ, turned(1)), 1: lax.ppermute(unit, YZ, turned(-1))}
    half_away = column_half(out_weight, 1 - yl)
    units[-1], units[1], unit, half_away = together((units[-1], units[1], unit, half_away))
    mine = lax.ppermute(bundle(queries, tile_mask, unit), Y, turn)
    units[-2] = lax.ppermute(units[-1], "z", up)
    units[2] = lax.ppermute(units[1], "z", down)
    units[-2], units[2] = together((units[-2], units[2]))
    early = join([units[d] for d in EARLY])
    forth, back = ring(NX, 1), ring(NX, -1)
    early_before = lax.ppermute(early, "x", forth)
    early_after = lax.ppermute(early, "x", back)
    units[-3] = lax.ppermute(units[-2], "z", up)
    units[3] = lax.ppermute(units[2], "z", down)
    units[-3], units[3], mine = together((units[-3], units[3], mine))
    far = [
        lax.ppermute(units[-3][:2], "z", up),
        lax.ppermute(units[3][2:], "z", down),
    ]
    theirs = lax.ppermute(mine, "core", swap)
    *far, theirs, early_before, early_after = together((*far, theirs, early_before, early_after))
    late = join([mine[UNIT_AT:], units[-3], units[3], *far])
    late_before = lax.ppermute(late, "x", forth)
    late_after = lax.ppermute(late, "x", back)
    away = along_y(lambda yh, yl, core: (*next_y(yh, yl, 1 - 2 * core), core))
    half_away, theirs = together((half_away, theirs))
    far_weight = lax.ppermute(half_away, Y, away)
    place = jnp.pad(jnp.stack([x, z, core]).astype(jnp.int32), (0, 125))[None]
    masks = jnp.concatenate([mine[MASK_AT, :2], theirs[MASK_AT, :2]]).astype(jnp.int32)
    table = jnp.concatenate([masks, place])

    near = (table, mine, theirs)
    every = (0, 1, 2, 3)
    state = stage(((0, EARLY), (0, LATE)), near, [early, late], None, every, "own_column")
    early_far = lax.ppermute(early_before, "x", forth)
    state = stage(
        ((-1, EARLY), (1, EARLY)), near, [early_before, early_after], state, every, "early"
    )
    late_before, late_after, *state = together((late_before, late_after, *state))
    late_far = lax.ppermute(late_after, "x", back)
    keep, send = stage(
        ((-1, LATE), (1, LATE)), near, [late_before, late_after], state, every, "late"
    )
    early_far, late_far, keep, send = together((early_far, late_far, keep, send))
    last = (((2, EARLY), (2, LATE)), near, [early_far, late_far])
    (send,) = stage(*last, (send,), (2, 3), "last_send")
    received = lax.ppermute(send, "core", swap)
    (keep,) = stage(*last, (keep,), (0, 1), "last_keep")
    keep, received, far_weight = together((keep, received, far_weight))
    shape = jax.ShapeDtypeStruct((2 * TILE, WIDE), jnp.bfloat16)
    attended = call(merge_kernel, shape, (keep, received), [vmem()] * 2, name="merge")

    near_part = lax.ppermute(attended, Y, turn)
    far_part = lax.ppermute(attended, Y, along_y(lambda yh, yl, core: (core, 1 - yl, yh)))
    where = jnp.stack([yl, core]).astype(jnp.int32)
    sides = (where, near_part, far_part, out_weight, far_weight)
    other = project(1, *sides, jnp.bfloat16, "project_send")
    other = lax.ppermute(other, "core", swap)
    own = project(0, *sides, jnp.float32, "project_keep")
    shape = jax.ShapeDtypeStruct(own.shape, jnp.bfloat16)
    return call(add_kernel, shape, (own, other), [vmem()] * 2, name="add")


def solution(mesh):
    fine = Mesh(mesh.devices.reshape(NX, NZ, 2, 2, 2), ("x", "z", "yh", "yl", "core"))
    tok, head = ("x", "z", "yh"), ("yl", "core")
    return jax.shard_map(
        per_device,
        mesh=fine,
        in_specs=(P(tok, head), P(tok, head), P(tok, head), P(tok, None), P(head, None)),
        out_specs=P(tok, head),
        check_vma=False,
    )
```

```python
import math

import jax
import jax.numpy as jnp
from jax import lax
from jax.experimental import pallas as pl
from jax.experimental.pallas import tpu as pltpu
from jax.sharding import Mesh, PartitionSpec as P

HD = 128
TILE = 128
NX, NZ = 4, 8
HEADS = 6
WIDE = HEADS * TILE
SUM_ROW = HD
MAX_ROW = HD + 16
ROWS = HD + 24
NEGATIVE = -1e30
MASK_AT = 2 * HEADS
UNIT_AT = MASK_AT + 1
EXP2_SCALE = math.log2(math.e) / math.sqrt(HD)
EARLY = (-1, 1, -2, 2)
LATE = (0, -3, 3, 4)


def vmem():
    return pl.BlockSpec(memory_space=pltpu.VMEM)


def smem():
    return pl.BlockSpec(memory_space=pltpu.SMEM)


def hbm():
    return pl.BlockSpec(memory_space=pl.ANY)


def in_hbm(x):
    return pltpu.with_memory_space_constraint(x, pltpu.HBM)


def call(kernel, out_shape, args, in_specs, scratch=(), aliases=None, name=None, flops=0):
    return pl.pallas_call(
        kernel,
        out_shape=out_shape,
        in_specs=in_specs,
        out_specs=jax.tree.map(lambda s: vmem(), out_shape),
        scratch_shapes=list(scratch),
        input_output_aliases=aliases or {},
        compiler_params=pltpu.CompilerParams(vmem_limit_bytes=14 * 1024 * 1024),
        cost_estimate=pl.CostEstimate(flops=flops, transcendentals=0, bytes_accessed=0),
        name=name,
    )(*args)


def pack_kernel(key_hbm, value_hbm, out_ref, key_ref, value_ref, sems):
    copies = [
        pltpu.make_async_copy(key_hbm, key_ref, sems.at[0]),
        pltpu.make_async_copy(value_hbm, value_ref, sems.at[1]),
    ]
    for copy in copies:
        copy.start()
    for copy in copies:
        copy.wait()
    for t in range(2):
        rows = pl.ds(t * TILE, TILE)
        out_ref[t] = key_ref[rows, :]
        out_ref[2 + t] = value_ref[rows, :].astype(jnp.float32).T.astype(jnp.bfloat16)


def pack(key_rows, value_rows):
    rows = pltpu.VMEM((2 * TILE, HD), jnp.bfloat16)
    return call(
        pack_kernel,
        jax.ShapeDtypeStruct((4, TILE, TILE), jnp.bfloat16),
        (in_hbm(key_rows), in_hbm(value_rows)),
        [hbm()] * 2,
        scratch=(rows, rows, pltpu.SemaphoreType.DMA((2,))),
        name="pack",
    )


def bundle_kernel(query_ref, mask_ref, unit_ref, out_ref):
    for t in range(2):
        for h in range(HEADS):
            out_ref[t * HEADS + h] = query_ref[pl.ds(t * TILE, TILE), pl.ds(h * HD, HD)]
    out_ref[MASK_AT] = jnp.zeros((TILE, TILE), jnp.bfloat16)
    out_ref[MASK_AT, 0:2, :] = mask_ref[...].astype(jnp.float32).astype(jnp.bfloat16)
    out_ref[UNIT_AT:] = unit_ref[...]


def bundle(queries, tile_mask, unit):
    shape = jax.ShapeDtypeStruct((UNIT_AT + 4, TILE, TILE), jnp.bfloat16)
    return call(bundle_kernel, shape, (queries, tile_mask, unit), [vmem()] * 3, name="bundle")


def half_kernel(half_ref, source_ref, out_ref, sems):
    rows = out_ref.shape[0] // 8
    start = pl.multiple_of(half_ref[0] * out_ref.shape[1], out_ref.shape[1])
    copies = [
        pltpu.make_async_copy(
            source_ref.at[pl.ds(i * rows, rows), pl.ds(start, out_ref.shape[1])],
            out_ref.at[pl.ds(i * rows, rows), :],
            sems.at[i],
        )
        for i in range(8)
    ]
    for copy in copies:
        copy.start()
    for copy in copies:
        copy.wait()


def column_half(source, number):
    return call(
        half_kernel,
        jax.ShapeDtypeStruct((source.shape[0], source.shape[1] // 2), source.dtype),
        (number.reshape(1).astype(jnp.int32), in_hbm(source)),
        [smem(), hbm()],
        scratch=(pltpu.SemaphoreType.DMA((8,)),),
        name="column_half",
    )


def join_kernel(*refs):
    out_ref = refs[-1]
    at = 0
    for ref in refs[:-1]:
        out_ref[pl.ds(at, ref.shape[0])] = ref[...]
        at += ref.shape[0]


def join(parts):
    total = sum(p.shape[0] for p in parts)
    shape = jax.ShapeDtypeStruct((total, *parts[0].shape[1:]), parts[0].dtype)
    return call(join_kernel, shape, parts, [vmem()] * len(parts), name="join")


def stage_kernel(columns, count, numbers, first, table_ref, mine_ref, theirs_ref, *refs):
    parts, refs = refs[:count], refs[count:]
    targets = sorted({number // 2 for number in numbers})
    if not first:
        refs = refs[len(targets) :]
    states, (tiles_ref, list_ref) = refs[: len(targets)], refs[len(targets) :]
    x, z, core = table_ref[4, 0], table_ref[4, 1], table_ref[4, 2]
    at = 0
    for part in parts:
        tiles_ref[pl.ds(at, part.shape[0])] = part[...]
        at += part.shape[0]
    if first:
        for ref in states:
            ref[:, :MAX_ROW, :] = jnp.zeros((2, MAX_ROW, WIDE), jnp.float32)
            ref[:, MAX_ROW:, :] = jnp.full((2, ROWS - MAX_ROW, WIDE), NEGATIVE, jnp.float32)

    counts = [jnp.int32(0)] * 4
    slot = 0
    for dx, order in columns:
        for dz in order:
            block = lax.rem(x + dx + NX, NX) * NZ + lax.rem(z + dz + NZ, NZ)
            for r in range(2):
                tile = (block * 2 + core) * 2 + r
                for number in numbers:
                    list_ref[number, counts[number]] = slot // 2 * 4 + slot % 2
                    counts[number] = counts[number] + table_ref[number, tile]
                slot += 1

    for number in numbers:
        list_ref[number, slot] = counts[number]

    def block(target, row, base, size):
        state_ref = states[targets.index(target)]
        source = theirs_ref if target else mine_ref
        number = 2 * target + row
        at = [list_ref[number, base + j] for j in range(size - 1)]
        live = base + size - 1 < list_ref[number, slot]
        at.append(jnp.where(live, list_ref[number, base + size - 1], at[0]))
        ones = jnp.ones((16, TILE), jnp.bfloat16)
        values = [jnp.concatenate([tiles_ref[i + 2], ones], axis=0) for i in at]
        values[-1] = values[-1] * jnp.where(live, 1.0, 0.0).astype(jnp.bfloat16)
        values = jnp.concatenate(values, axis=1)
        keys = jnp.concatenate([tiles_ref[i] for i in at], axis=0)
        chunks = [pl.ds(h * TILE, TILE) for h in range(HEADS)]
        scores = [
            lax.dot_general(
                keys,
                source[row * HEADS + h],
                (((1,), (1,)), ((), ())),
                preferred_element_type=jnp.float32,
            )
            for h in range(HEADS)
        ]
        probs = []
        for lanes, score in zip(chunks, scores):
            old_max = state_ref[row, pl.ds(MAX_ROW, 1), lanes]
            new_max = jnp.maximum(old_max, jnp.max(score, axis=0, keepdims=True))
            prob = jnp.exp2((score - new_max) * EXP2_SCALE).astype(jnp.bfloat16)
            probs.append((prob, jnp.exp2((old_max - new_max) * EXP2_SCALE)))
            state_ref[row, pl.ds(MAX_ROW, 8), lanes] = jnp.broadcast_to(new_max, (8, TILE))
        for lanes, (prob, fade) in zip(chunks, probs):
            part = lax.dot_general(
                values, prob, (((1,), (0,)), ((), ())), preferred_element_type=jnp.float32
            )
            state_ref[row, pl.ds(0, MAX_ROW), lanes] = (
                state_ref[row, pl.ds(0, MAX_ROW), lanes] * fade + part
            )

    def one_query_tile(target, row):
        total = list_ref[2 * target + row, slot]
        blocks = (total + 1) // 4
        rest = total - 4 * blocks

        def full(turn, carry):
            block(target, row, 4 * turn, 4)
            return carry

        lax.fori_loop(0, blocks, full, 0)

        @pl.when(rest > 0)
        def _():
            block(target, row, 4 * blocks, 2)

    for target in targets:
        for row in range(2):
            one_query_tile(target, row)


def stage(columns, near, parts, state, numbers, name):
    shape = jax.ShapeDtypeStruct((2, ROWS, WIDE), jnp.float32)
    slots = sum(2 * len(order) for _, order in columns)
    args = [*near, *parts]
    outs = len({number // 2 for number in numbers})
    aliases = {}
    if state is not None:
        aliases = {len(args) + i: i for i in range(outs)}
        args += list(state)
    kernel = lambda *refs: stage_kernel(columns, len(parts), numbers, state is None, *refs)
    return call(
        kernel,
        (shape,) * outs,
        args,
        [smem()] + [vmem()] * (len(args) - 1),
        scratch=(
            pltpu.VMEM((2 * slots, TILE, TILE), jnp.bfloat16),
            pltpu.SMEM((4, slots + 1), jnp.int32),
        ),
        aliases=aliases,
        name=name,
    )


def merge_kernel(own_ref, other_ref, out_ref):
    for t in range(2):
        own_max = own_ref[t, pl.ds(MAX_ROW, 1), :]
        other_max = other_ref[t, pl.ds(MAX_ROW, 1), :]
        row_max = jnp.maximum(own_max, other_max)
        own_weight = jnp.exp2((own_max - row_max) * EXP2_SCALE)
        other_weight = jnp.exp2((other_max - row_max) * EXP2_SCALE)
        total = (
            own_ref[t, pl.ds(SUM_ROW, 1), :] * own_weight
            + other_ref[t, pl.ds(SUM_ROW, 1), :] * other_weight
        )
        own_weight = own_weight / total
        other_weight = other_weight / total
        for h in range(HEADS):
            lanes = slice(h * TILE, (h + 1) * TILE)
            attended = (
                own_ref[t, pl.ds(0, HD), lanes] * own_weight[:, lanes]
                + other_ref[t, pl.ds(0, HD), lanes] * other_weight[:, lanes]
            )
            out_ref[pl.ds(t * TILE, TILE), pl.ds(h * HD, HD)] = attended.T.astype(jnp.bfloat16)


def ring(size, step):
    return [(i, (i + step) % size) for i in range(size)]


def along_y(move):
    pairs = []
    for i in range(8):
        yh, yl, core = move(i // 4, i // 2 % 2, i % 2)
        pairs.append((i, yh % 2 * 4 + yl % 2 * 2 + core % 2))
    return pairs


def next_y(yh, yl, step):
    y = (yh * 2 + yl + step) % 4
    return y // 2, y % 2


Y = ("yh", "yl", "core")
YZ = ("z", "yh", "yl", "core")


def turned(shift):
    turn = along_y(lambda yh, yl, core: (core, yl, yh))
    return [(z * 8 + a, (z + shift) % NZ * 8 + b) for z in range(NZ) for a, b in turn]


def project_kernel(flip, place_ref, near_ref, far_ref, weight_ref, far_weight_ref, out_ref):
    width = out_ref.shape[1]
    which = place_ref[1] + flip - 2 * flip * place_ref[1]
    for n in range(width // 256):
        at = pl.multiple_of(which * width + n * 256, 256)
        far = far_weight_ref[:, pl.ds(at, 256)]
        total = jnp.dot(far_ref[...], far, preferred_element_type=jnp.float32)
        at = pl.multiple_of(place_ref[0] * (2 * width) + which * width + n * 256, 256)
        near = weight_ref[:, pl.ds(at, 256)]
        total = total + jnp.dot(near_ref[...], near, preferred_element_type=jnp.float32)
        out_ref[:, n * 256 : (n + 1) * 256] = total.astype(out_ref.dtype)


def project(flip, place, near, far, weight, far_weight, dtype, name):
    shape = jax.ShapeDtypeStruct((near.shape[0], far_weight.shape[1] // 2), dtype)
    return call(
        lambda *refs: project_kernel(flip, *refs),
        shape,
        (place, near, far, weight, far_weight),
        [smem()] + [vmem()] * 4,
        name=name,
    )


def add_kernel(keep_ref, other_ref, out_ref):
    out_ref[...] = (keep_ref[...] + other_ref[...].astype(jnp.float32)).astype(out_ref.dtype)


def per_device(queries, key_rows, value_rows, tile_mask, out_weight):
    x, z = lax.axis_index("x"), lax.axis_index("z")
    yh, yl, core = lax.axis_index("yh"), lax.axis_index("yl"), lax.axis_index("core")
    turn = along_y(lambda yh, yl, core: (core, yl, yh))
    swap = [(0, 1), (1, 0)]
    together = lax.optimization_barrier

    unit = pack(key_rows, value_rows)
    up, down = ring(NZ, 1), ring(NZ, -1)
    units = {-1: lax.ppermute(unit, YZ, turned(1)), 1: lax.ppermute(unit, YZ, turned(-1))}
    half_away = column_half(out_weight, 1 - yl)
    units[-1], units[1], unit, half_away = together((units[-1], units[1], unit, half_away))
    mine = lax.ppermute(bundle(queries, tile_mask, unit), Y, turn)
    units[-2] = lax.ppermute(units[-1], "z", up)
    units[2] = lax.ppermute(units[1], "z", down)
    units[-2], units[2], mine, half_away = together((units[-2], units[2], mine, half_away))
    away = along_y(lambda yh, yl, core: (*next_y(yh, yl, 1 - 2 * core), core))
    far_weight = lax.ppermute(half_away, Y, away)
    early = join([units[d] for d in EARLY])
    forth, back = ring(NX, 1), ring(NX, -1)
    early_before = lax.ppermute(early, "x", forth)
    early_after = lax.ppermute(early, "x", back)
    units[-3] = lax.ppermute(units[-2], "z", up)
    units[3] = lax.ppermute(units[2], "z", down)
    units[4] = lax.ppermute(units[-3], "z", up)
    late = join([mine[UNIT_AT:]] + [units[d] for d in LATE[1:]])
    late, mine, early_before, early_after = together((late, mine, early_before, early_after))
    theirs = lax.ppermute(mine, "core", swap)
    late_before = lax.ppermute(late, "x", forth)
    late_after = lax.ppermute(late, "x", back)
    place = jnp.pad(jnp.stack([x, z, core]).astype(jnp.int32), (0, 125))[None]
    masks = jnp.concatenate([mine[MASK_AT, :2], theirs[MASK_AT, :2]]).astype(jnp.int32)
    table = jnp.concatenate([masks, place])

    near = (table, mine, theirs)
    every = (0, 1, 2, 3)
    state = stage(((0, EARLY), (0, LATE)), near, [early, late], None, every, "own_column")
    early_far = lax.ppermute(early_before, "x", forth)
    state = stage(
        ((-1, EARLY), (1, EARLY)), near, [early_before, early_after], state, every, "early"
    )
    late_before, late_after, *state = together((late_before, late_after, *state))
    half = late.shape[0] // 2
    late_far = [
        lax.ppermute(late_before[:half], "x", forth),
        lax.ppermute(late_after[half:], "x", back),
    ]
    keep, send = stage(
        ((-1, LATE), (1, LATE)), near, [late_before, late_after], state, every, "late"
    )
    early_far, *late_far, keep, send = together((early_far, *late_far, keep, send))
    last = (((2, EARLY), (2, LATE)), near, [early_far, *late_far])
    (send,) = stage(*last, (send,), (2, 3), "last_send")
    received = lax.ppermute(send, "core", swap)
    (keep,) = stage(*last, (keep,), (0, 1), "last_keep")
    keep, received, far_weight = together((keep, received, far_weight))
    shape = jax.ShapeDtypeStruct((2 * TILE, WIDE), jnp.bfloat16)
    attended = call(merge_kernel, shape, (keep, received), [vmem()] * 2, name="merge")

    near_part = lax.ppermute(attended, Y, turn)
    far_part = lax.ppermute(attended, Y, along_y(lambda yh, yl, core: (core, 1 - yl, yh)))
    where = jnp.stack([yl, core]).astype(jnp.int32)
    sides = (where, near_part, far_part, out_weight, far_weight)
    other = project(1, *sides, jnp.bfloat16, "project_send")
    other = lax.ppermute(other, "core", swap)
    own = project(0, *sides, jnp.float32, "project_keep")
    shape = jax.ShapeDtypeStruct(own.shape, jnp.bfloat16)
    return call(add_kernel, shape, (own, other), [vmem()] * 2, name="add")


def solution(mesh):
    fine = Mesh(mesh.devices.reshape(NX, NZ, 2, 2, 2), ("x", "z", "yh", "yl", "core"))
    tok, head = ("x", "z", "yh"), ("yl", "core")
    return jax.shard_map(
        per_device,
        mesh=fine,
        in_specs=(P(tok, head), P(tok, head), P(tok, head), P(tok, None), P(head, None)),
        out_specs=P(tok, head),
        check_vma=False,
    )
```

```python
import math

import jax
import jax.numpy as jnp
from jax import lax
from jax.experimental import pallas as pl
from jax.experimental.pallas import tpu as pltpu
from jax.sharding import Mesh, PartitionSpec as P

HD = 128
TILE = 128
NX, NZ = 4, 8
HEADS = 6
WIDE = HEADS * TILE
SUM_ROW = HD
MAX_ROW = HD + 16
ROWS = HD + 24
NEGATIVE = -1e30
MASK_AT = 2 * HEADS
UNIT_AT = MASK_AT + 1
EXP2_SCALE = math.log2(math.e) / math.sqrt(HD)
EARLY = (-1, 1, -2, 2)
LATE = (0, -3, 3, 4)


def vmem():
    return pl.BlockSpec(memory_space=pltpu.VMEM)


def smem():
    return pl.BlockSpec(memory_space=pltpu.SMEM)


def hbm():
    return pl.BlockSpec(memory_space=pl.ANY)


def in_hbm(x):
    return pltpu.with_memory_space_constraint(x, pltpu.HBM)


def call(kernel, out_shape, args, in_specs, scratch=(), aliases=None, name=None, flops=0):
    return pl.pallas_call(
        kernel,
        out_shape=out_shape,
        in_specs=in_specs,
        out_specs=jax.tree.map(lambda s: vmem(), out_shape),
        scratch_shapes=list(scratch),
        input_output_aliases=aliases or {},
        compiler_params=pltpu.CompilerParams(vmem_limit_bytes=14 * 1024 * 1024),
        cost_estimate=pl.CostEstimate(flops=flops, transcendentals=0, bytes_accessed=0),
        name=name,
    )(*args)


def pack_kernel(key_hbm, value_hbm, query_hbm, mask_hbm, unit_ref, out_ref, *scratch):
    *buffers, sems = scratch
    key_ref, value_ref, query_ref, mask_ref = buffers
    copies = [
        pltpu.make_async_copy(source, target, sems.at[i])
        for i, (source, target) in enumerate(
            zip((key_hbm, value_hbm, query_hbm, mask_hbm), buffers)
        )
    ]
    for copy in copies:
        copy.start()
    for copy in copies:
        copy.wait()
    for t in range(2):
        rows = pl.ds(t * TILE, TILE)
        values = value_ref[rows, :].astype(jnp.float32).T.astype(jnp.bfloat16)
        for ref, at in ((unit_ref, 0), (out_ref, UNIT_AT)):
            ref[at + t] = key_ref[rows, :]
            ref[at + 2 + t] = values
        for h in range(HEADS):
            out_ref[t * HEADS + h] = query_ref[rows, pl.ds(h * HD, HD)]
    out_ref[MASK_AT] = jnp.zeros((TILE, TILE), jnp.bfloat16)
    out_ref[MASK_AT, 0:2, :] = mask_ref[...].astype(jnp.float32).astype(jnp.bfloat16)


def pack(*arrays):
    return call(
        pack_kernel,
        tuple(
            jax.ShapeDtypeStruct((size, TILE, TILE), jnp.bfloat16) for size in (4, UNIT_AT + 4)
        ),
        tuple(in_hbm(a) for a in arrays),
        [hbm()] * 4,
        scratch=[pltpu.VMEM(a.shape, a.dtype) for a in arrays] + [pltpu.SemaphoreType.DMA((4,))],
        name="pack",
    )


def half_kernel(half_ref, source_ref, out_ref, sems):
    rows = out_ref.shape[0] // 8
    start = pl.multiple_of(half_ref[0] * out_ref.shape[1], out_ref.shape[1])
    copies = [
        pltpu.make_async_copy(
            source_ref.at[pl.ds(i * rows, rows), pl.ds(start, out_ref.shape[1])],
            out_ref.at[pl.ds(i * rows, rows), :],
            sems.at[i],
        )
        for i in range(8)
    ]
    for copy in copies:
        copy.start()
    for copy in copies:
        copy.wait()


def column_half(source, number):
    return call(
        half_kernel,
        jax.ShapeDtypeStruct((source.shape[0], source.shape[1] // 2), source.dtype),
        (number.reshape(1).astype(jnp.int32), in_hbm(source)),
        [smem(), hbm()],
        scratch=(pltpu.SemaphoreType.DMA((8,)),),
        name="column_half",
    )


def fetch_kernel(source_ref, out_ref, sems):
    rows = out_ref.shape[0] // 4
    copies = [
        pltpu.make_async_copy(
            source_ref.at[pl.ds(i * rows, rows), :], out_ref.at[pl.ds(i * rows, rows), :], sems.at[i]
        )
        for i in range(4)
    ]
    for copy in copies:
        copy.start()
    for copy in copies:
        copy.wait()


def fetch(source):
    shape = jax.ShapeDtypeStruct(source.shape, source.dtype)
    scratch = (pltpu.SemaphoreType.DMA((4,)),)
    return call(fetch_kernel, shape, (in_hbm(source),), [hbm()], scratch=scratch, name="fetch")


def join_kernel(*refs):
    out_ref = refs[-1]
    at = 0
    for ref in refs[:-1]:
        out_ref[pl.ds(at, ref.shape[0])] = ref[...]
        at += ref.shape[0]


def join(parts):
    total = sum(p.shape[0] for p in parts)
    shape = jax.ShapeDtypeStruct((total, *parts[0].shape[1:]), parts[0].dtype)
    return call(join_kernel, shape, parts, [vmem()] * len(parts), name="join")


def stage_kernel(columns, count, numbers, first, table_ref, mine_ref, theirs_ref, *refs):
    parts, refs = refs[:count], refs[count:]
    targets = sorted({number // 2 for number in numbers})
    if not first:
        refs = refs[len(targets) :]
    states, (tiles_ref, list_ref) = refs[: len(targets)], refs[len(targets) :]
    x, z, core = table_ref[4, 0], table_ref[4, 1], table_ref[4, 2]
    at = 0
    for part in parts:
        tiles_ref[pl.ds(at, part.shape[0])] = part[...]
        at += part.shape[0]
    if first:
        for ref in states:
            ref[:, :MAX_ROW, :] = jnp.zeros((2, MAX_ROW, WIDE), jnp.float32)
            ref[:, MAX_ROW:, :] = jnp.full((2, ROWS - MAX_ROW, WIDE), NEGATIVE, jnp.float32)

    counts = [jnp.int32(0)] * 4
    slot = 0
    for dx, order in columns:
        for dz in order:
            block = lax.rem(x + dx + NX, NX) * NZ + lax.rem(z + dz + NZ, NZ)
            for r in range(2):
                tile = (block * 2 + core) * 2 + r
                for number in numbers:
                    list_ref[number, counts[number]] = slot // 2 * 4 + slot % 2
                    counts[number] = counts[number] + table_ref[number, tile]
                slot += 1

    for number in numbers:
        list_ref[number, slot] = counts[number]

    def block(target, row, base, size):
        state_ref = states[targets.index(target)]
        source = theirs_ref if target else mine_ref
        number = 2 * target + row
        at = [list_ref[number, base + j] for j in range(size - 1)]
        live = base + size - 1 < list_ref[number, slot]
        at.append(jnp.where(live, list_ref[number, base + size - 1], at[0]))
        ones = jnp.ones((16, TILE), jnp.bfloat16)
        values = [jnp.concatenate([tiles_ref[i + 2], ones], axis=0) for i in at]
        values[-1] = values[-1] * jnp.where(live, 1.0, 0.0).astype(jnp.bfloat16)
        values = jnp.concatenate(values, axis=1)
        keys = jnp.concatenate([tiles_ref[i] for i in at], axis=0)
        chunks = [pl.ds(h * TILE, TILE) for h in range(HEADS)]
        scores = [
            lax.dot_general(
                keys,
                source[row * HEADS + h],
                (((1,), (1,)), ((), ())),
                preferred_element_type=jnp.float32,
            )
            for h in range(HEADS)
        ]
        probs = []
        for lanes, score in zip(chunks, scores):
            old_max = state_ref[row, pl.ds(MAX_ROW, 1), lanes]
            new_max = jnp.maximum(old_max, jnp.max(score, axis=0, keepdims=True))
            prob = jnp.exp2((score - new_max) * EXP2_SCALE).astype(jnp.bfloat16)
            probs.append((prob, jnp.exp2((old_max - new_max) * EXP2_SCALE)))
            state_ref[row, pl.ds(MAX_ROW, 8), lanes] = jnp.broadcast_to(new_max, (8, TILE))
        for lanes, (prob, fade) in zip(chunks, probs):
            part = lax.dot_general(
                values, prob, (((1,), (0,)), ((), ())), preferred_element_type=jnp.float32
            )
            state_ref[row, pl.ds(0, MAX_ROW), lanes] = (
                state_ref[row, pl.ds(0, MAX_ROW), lanes] * fade + part
            )

    def one_query_tile(target, row):
        total = list_ref[2 * target + row, slot]
        blocks = (total + 1) // 4
        rest = total - 4 * blocks

        def full(turn, carry):
            block(target, row, 4 * turn, 4)
            return carry

        lax.fori_loop(0, blocks, full, 0)

        @pl.when(rest > 0)
        def _():
            block(target, row, 4 * blocks, 2)

    for target in targets:
        for row in range(2):
            one_query_tile(target, row)


def stage(columns, near, parts, state, numbers, name):
    shape = jax.ShapeDtypeStruct((2, ROWS, WIDE), jnp.float32)
    slots = sum(2 * len(order) for _, order in columns)
    args = [*near, *parts]
    outs = len({number // 2 for number in numbers})
    aliases = {}
    if state is not None:
        aliases = {len(args) + i: i for i in range(outs)}
        args += list(state)
    kernel = lambda *refs: stage_kernel(columns, len(parts), numbers, state is None, *refs)
    return call(
        kernel,
        (shape,) * outs,
        args,
        [smem()] + [vmem()] * (len(args) - 1),
        scratch=(
            pltpu.VMEM((2 * slots, TILE, TILE), jnp.bfloat16),
            pltpu.SMEM((4, slots + 1), jnp.int32),
        ),
        aliases=aliases,
        name=name,
    )


def merge_kernel(own_ref, other_ref, out_ref):
    for t in range(2):
        own_max = own_ref[t, pl.ds(MAX_ROW, 1), :]
        other_max = other_ref[t, pl.ds(MAX_ROW, 1), :]
        row_max = jnp.maximum(own_max, other_max)
        own_weight = jnp.exp2((own_max - row_max) * EXP2_SCALE)
        other_weight = jnp.exp2((other_max - row_max) * EXP2_SCALE)
        total = (
            own_ref[t, pl.ds(SUM_ROW, 1), :] * own_weight
            + other_ref[t, pl.ds(SUM_ROW, 1), :] * other_weight
        )
        own_weight = own_weight / total
        other_weight = other_weight / total
        for h in range(HEADS):
            lanes = slice(h * TILE, (h + 1) * TILE)
            attended = (
                own_ref[t, pl.ds(0, HD), lanes] * own_weight[:, lanes]
                + other_ref[t, pl.ds(0, HD), lanes] * other_weight[:, lanes]
            )
            out_ref[pl.ds(t * TILE, TILE), pl.ds(h * HD, HD)] = attended.T.astype(jnp.bfloat16)


def ring(size, step):
    return [(i, (i + step) % size) for i in range(size)]


def along_y(move):
    pairs = []
    for i in range(8):
        yh, yl, core = move(i // 4, i // 2 % 2, i % 2)
        pairs.append((i, yh % 2 * 4 + yl % 2 * 2 + core % 2))
    return pairs


def next_y(yh, yl, step):
    y = (yh * 2 + yl + step) % 4
    return y // 2, y % 2


Y = ("yh", "yl", "core")
YZ = ("z", "yh", "yl", "core")


def turned(shift):
    turn = along_y(lambda yh, yl, core: (core, yl, yh))
    return [(z * 8 + a, (z + shift) % NZ * 8 + b) for z in range(NZ) for a, b in turn]


def project_kernel(flip, place_ref, near_ref, far_ref, weight_ref, far_weight_ref, out_ref):
    width = out_ref.shape[1]
    which = place_ref[1] + flip - 2 * flip * place_ref[1]
    for n in range(width // 256):
        at = pl.multiple_of(which * width + n * 256, 256)
        far = far_weight_ref[:, pl.ds(at, 256)]
        total = jnp.dot(far_ref[...], far, preferred_element_type=jnp.float32)
        at = pl.multiple_of(place_ref[0] * (2 * width) + which * width + n * 256, 256)
        near = weight_ref[:, pl.ds(at, 256)]
        total = total + jnp.dot(near_ref[...], near, preferred_element_type=jnp.float32)
        out_ref[:, n * 256 : (n + 1) * 256] = total.astype(out_ref.dtype)


def project(flip, place, near, far, weight, far_weight, dtype, name):
    shape = jax.ShapeDtypeStruct((near.shape[0], far_weight.shape[1] // 2), dtype)
    return call(
        lambda *refs: project_kernel(flip, *refs),
        shape,
        (place, near, far, weight, far_weight),
        [smem()] + [vmem()] * 4,
        name=name,
    )


def add_kernel(keep_ref, other_ref, out_ref):
    out_ref[...] = (keep_ref[...] + other_ref[...].astype(jnp.float32)).astype(out_ref.dtype)


def per_device(queries, key_rows, value_rows, tile_mask, out_weight):
    x, z = lax.axis_index("x"), lax.axis_index("z")
    yh, yl, core = lax.axis_index("yh"), lax.axis_index("yl"), lax.axis_index("core")
    turn = along_y(lambda yh, yl, core: (core, yl, yh))
    swap = [(0, 1), (1, 0)]
    together = lax.optimization_barrier

    unit, bundle = pack(key_rows, value_rows, queries, tile_mask)
    up, down = ring(NZ, 1), ring(NZ, -1)
    units = {-1: lax.ppermute(unit, YZ, turned(1)), 1: lax.ppermute(unit, YZ, turned(-1))}
    mine = lax.ppermute(bundle, Y, turn)
    half_away = column_half(out_weight, 1 - yl)
    units[-1], units[1], mine, half_away = together((units[-1], units[1], mine, half_away))
    away = along_y(lambda yh, yl, core: (*next_y(yh, yl, 1 - 2 * core), core))
    far_weight = lax.ppermute(half_away, Y, away)
    units[-2] = lax.ppermute(units[-1], "z", up)
    units[2] = lax.ppermute(units[1], "z", down)
    units[-2], units[2] = together((units[-2], units[2]))
    early = join([units[d] for d in EARLY])
    forth, back = ring(NX, 1), ring(NX, -1)
    early_before = lax.ppermute(early, "x", forth)
    early_after = lax.ppermute(early, "x", back)
    units[-3] = lax.ppermute(units[-2], "z", up)
    units[3] = lax.ppermute(units[2], "z", down)
    units[4] = lax.ppermute(units[-3], "z", up)
    late = join([mine[UNIT_AT:]] + [units[d] for d in LATE[1:]])
    theirs = lax.ppermute(mine, "core", swap)
    late, theirs, early_before, early_after = together((late, theirs, early_before, early_after))
    late_before = lax.ppermute(late, "x", forth)
    late_after = lax.ppermute(late, "x", back)
    place = jnp.pad(jnp.stack([x, z, core]).astype(jnp.int32), (0, 125))[None]
    masks = jnp.concatenate([mine[MASK_AT, :2], theirs[MASK_AT, :2]]).astype(jnp.int32)
    table = jnp.concatenate([masks, place])

    near = (table, mine, theirs)
    every = (0, 1, 2, 3)
    state = stage(((0, EARLY), (0, LATE)), near, [early, late], None, every, "own_column")
    half = early.shape[0] // 2
    early_far = [
        lax.ppermute(early_before[:half], "x", forth),
        lax.ppermute(early_after[half:], "x", back),
    ]
    state = stage(
        ((-1, EARLY), (1, EARLY)), near, [early_before, early_after], state, every, "early"
    )
    late_before, late_after, *state = together((late_before, late_after, *state))
    late_far = [
        lax.ppermute(late_before[:half], "x", forth),
        lax.ppermute(late_after[half:], "x", back),
    ]
    keep, send = stage(
        ((-1, LATE), (1, LATE)), near, [late_before, late_after], state, every, "late"
    )
    *far, keep, send = together((*early_far, *late_far, keep, send))
    last = (((2, EARLY), (2, LATE)), near, far)
    (send,) = stage(*last, (send,), (2, 3), "last_send")
    received = lax.ppermute(send, "core", swap)
    (keep,) = stage(*last, (keep,), (0, 1), "last_keep")
    keep, received, far_weight = together((keep, received, far_weight))
    shape = jax.ShapeDtypeStruct((2 * TILE, WIDE), jnp.bfloat16)
    attended = call(merge_kernel, shape, (keep, received), [vmem()] * 2, name="merge")

    near_part = lax.ppermute(attended, Y, turn)
    far_part = lax.ppermute(attended, Y, along_y(lambda yh, yl, core: (core, 1 - yl, yh)))
    where = jnp.stack([yl, core]).astype(jnp.int32)
    sides = (where, near_part, far_part, out_weight, fetch(far_weight))
    other = project(1, *sides, jnp.bfloat16, "project_send")
    other = lax.ppermute(other, "core", swap)
    own = project(0, *sides, jnp.float32, "project_keep")
    shape = jax.ShapeDtypeStruct(own.shape, jnp.bfloat16)
    return call(add_kernel, shape, (own, other), [vmem()] * 2, name="add")


def solution(mesh):
    fine = Mesh(mesh.devices.reshape(NX, NZ, 2, 2, 2), ("x", "z", "yh", "yl", "core"))
    tok, head = ("x", "z", "yh"), ("yl", "core")
    return jax.shard_map(
        per_device,
        mesh=fine,
        in_specs=(P(tok, head), P(tok, head), P(tok, head), P(tok, None), P(head, None)),
        out_specs=P(tok, head),
        check_vma=False,
    )
```

```python
import math

import jax
import jax.numpy as jnp
from jax import lax
from jax.experimental import pallas as pl
from jax.experimental.pallas import tpu as pltpu
from jax.sharding import Mesh, PartitionSpec as P

HD = 128
TILE = 128
NX, NZ = 4, 8
HEADS = 6
WIDE = HEADS * TILE
SUM_ROW = HD
MAX_ROW = HD + 16
ROWS = HD + 24
NEGATIVE = -1e30
MASK_AT = 2 * HEADS
UNIT_AT = MASK_AT + 1
EXP2_SCALE = math.log2(math.e) / math.sqrt(HD)
EARLY = (-1, 1, 0, 4)
LATE = (-2, 2, -3, 3)


def vmem():
    return pl.BlockSpec(memory_space=pltpu.VMEM)


def smem():
    return pl.BlockSpec(memory_space=pltpu.SMEM)


def hbm():
    return pl.BlockSpec(memory_space=pl.ANY)


def in_hbm(x):
    return pltpu.with_memory_space_constraint(x, pltpu.HBM)


def call(kernel, out_shape, args, in_specs, scratch=(), aliases=None, name=None, flops=0):
    return pl.pallas_call(
        kernel,
        out_shape=out_shape,
        in_specs=in_specs,
        out_specs=jax.tree.map(lambda s: vmem(), out_shape),
        scratch_shapes=list(scratch),
        input_output_aliases=aliases or {},
        compiler_params=pltpu.CompilerParams(vmem_limit_bytes=14 * 1024 * 1024),
        cost_estimate=pl.CostEstimate(flops=flops, transcendentals=0, bytes_accessed=0),
        name=name,
    )(*args)


def pack_kernel(key_hbm, value_hbm, query_hbm, mask_hbm, unit_ref, out_ref, *scratch):
    *buffers, sems = scratch
    key_ref, value_ref, query_ref, mask_ref = buffers
    copies = [
        pltpu.make_async_copy(source, target, sems.at[i])
        for i, (source, target) in enumerate(
            zip((key_hbm, value_hbm, query_hbm, mask_hbm), buffers)
        )
    ]
    for copy in copies:
        copy.start()
    for copy in copies:
        copy.wait()
    for t in range(2):
        rows = pl.ds(t * TILE, TILE)
        values = value_ref[rows, :].astype(jnp.float32).T.astype(jnp.bfloat16)
        for ref, at in ((unit_ref, 0), (out_ref, UNIT_AT)):
            ref[at + t] = key_ref[rows, :]
            ref[at + 2 + t] = values
        for h in range(HEADS):
            out_ref[t * HEADS + h] = query_ref[rows, pl.ds(h * HD, HD)]
    out_ref[MASK_AT] = jnp.zeros((TILE, TILE), jnp.bfloat16)
    out_ref[MASK_AT, 0:2, :] = mask_ref[...].astype(jnp.float32).astype(jnp.bfloat16)


def pack(*arrays):
    return call(
        pack_kernel,
        tuple(
            jax.ShapeDtypeStruct((size, TILE, TILE), jnp.bfloat16) for size in (4, UNIT_AT + 4)
        ),
        tuple(in_hbm(a) for a in arrays),
        [hbm()] * 4,
        scratch=[pltpu.VMEM(a.shape, a.dtype) for a in arrays] + [pltpu.SemaphoreType.DMA((4,))],
        name="pack",
    )


def half_kernel(half_ref, source_ref, out_ref, sems):
    rows = out_ref.shape[0] // 8
    start = pl.multiple_of(half_ref[0] * out_ref.shape[1], out_ref.shape[1])
    copies = [
        pltpu.make_async_copy(
            source_ref.at[pl.ds(i * rows, rows), pl.ds(start, out_ref.shape[1])],
            out_ref.at[pl.ds(i * rows, rows), :],
            sems.at[i],
        )
        for i in range(8)
    ]
    for copy in copies:
        copy.start()
    for copy in copies:
        copy.wait()


def column_half(source, number):
    return call(
        half_kernel,
        jax.ShapeDtypeStruct((source.shape[0], source.shape[1] // 2), source.dtype),
        (number.reshape(1).astype(jnp.int32), in_hbm(source)),
        [smem(), hbm()],
        scratch=(pltpu.SemaphoreType.DMA((8,)),),
        name="column_half",
    )


def fetch_kernel(source_ref, out_ref, sems):
    rows = out_ref.shape[0] // 4
    copies = [
        pltpu.make_async_copy(
            source_ref.at[pl.ds(i * rows, rows), :], out_ref.at[pl.ds(i * rows, rows), :], sems.at[i]
        )
        for i in range(4)
    ]
    for copy in copies:
        copy.start()
    for copy in copies:
        copy.wait()


def fetch(source):
    shape = jax.ShapeDtypeStruct(source.shape, source.dtype)
    scratch = (pltpu.SemaphoreType.DMA((4,)),)
    return call(fetch_kernel, shape, (in_hbm(source),), [hbm()], scratch=scratch, name="fetch")


def join_kernel(starts, *refs):
    out_ref = refs[-1]
    at = 0
    for start, ref in zip(starts, refs[:-1]):
        size = ref.shape[0] - start
        out_ref[pl.ds(at, size)] = ref[pl.ds(start, size)]
        at += size


def join(parts):
    starts = [p[1] if isinstance(p, tuple) else 0 for p in parts]
    parts = [p[0] if isinstance(p, tuple) else p for p in parts]
    total = sum(p.shape[0] - start for p, start in zip(parts, starts))
    shape = jax.ShapeDtypeStruct((total, *parts[0].shape[1:]), parts[0].dtype)
    kernel = lambda *refs: join_kernel(starts, *refs)
    return call(kernel, shape, parts, [vmem()] * len(parts), name="join")


def stage_kernel(columns, count, numbers, first, table_ref, mine_ref, theirs_ref, *refs):
    parts, refs = refs[:count], refs[count:]
    targets = sorted({number // 2 for number in numbers})
    if not first:
        refs = refs[len(targets) :]
    states, (tiles_ref, list_ref) = refs[: len(targets)], refs[len(targets) :]
    x, z, core = table_ref[4, 0], table_ref[4, 1], table_ref[4, 2]
    at = 0
    for part in parts:
        tiles_ref[pl.ds(at, part.shape[0])] = part[...]
        at += part.shape[0]
    if first:
        for ref in states:
            ref[:, :MAX_ROW, :] = jnp.zeros((2, MAX_ROW, WIDE), jnp.float32)
            ref[:, MAX_ROW:, :] = jnp.full((2, ROWS - MAX_ROW, WIDE), NEGATIVE, jnp.float32)

    counts = [jnp.int32(0)] * 4
    slot = 0
    for dx, order in columns:
        for dz in order:
            block = lax.rem(x + dx + NX, NX) * NZ + lax.rem(z + dz + NZ, NZ)
            for r in range(2):
                tile = (block * 2 + core) * 2 + r
                for number in numbers:
                    list_ref[number, counts[number]] = slot // 2 * 4 + slot % 2
                    counts[number] = counts[number] + table_ref[number, tile]
                slot += 1

    for number in numbers:
        list_ref[number, slot] = counts[number]

    def block(target, row, base, size):
        state_ref = states[targets.index(target)]
        source = theirs_ref if target else mine_ref
        number = 2 * target + row
        at = [list_ref[number, base + j] for j in range(size - 1)]
        live = base + size - 1 < list_ref[number, slot]
        at.append(jnp.where(live, list_ref[number, base + size - 1], at[0]))
        ones = jnp.ones((16, TILE), jnp.bfloat16)
        values = [jnp.concatenate([tiles_ref[i + 2], ones], axis=0) for i in at]
        values[-1] = values[-1] * jnp.where(live, 1.0, 0.0).astype(jnp.bfloat16)
        values = jnp.concatenate(values, axis=1)
        keys = jnp.concatenate([tiles_ref[i] for i in at], axis=0)
        chunks = [pl.ds(h * TILE, TILE) for h in range(HEADS)]
        scores = [
            lax.dot_general(
                keys,
                source[row * HEADS + h],
                (((1,), (1,)), ((), ())),
                preferred_element_type=jnp.float32,
            )
            for h in range(HEADS)
        ]
        probs = []
        for lanes, score in zip(chunks, scores):
            old_max = state_ref[row, pl.ds(MAX_ROW, 1), lanes]
            new_max = jnp.maximum(old_max, jnp.max(score, axis=0, keepdims=True))
            prob = jnp.exp2((score - new_max) * EXP2_SCALE).astype(jnp.bfloat16)
            probs.append((prob, jnp.exp2((old_max - new_max) * EXP2_SCALE)))
            state_ref[row, pl.ds(MAX_ROW, 8), lanes] = jnp.broadcast_to(new_max, (8, TILE))
        for lanes, (prob, fade) in zip(chunks, probs):
            part = lax.dot_general(
                values, prob, (((1,), (0,)), ((), ())), preferred_element_type=jnp.float32
            )
            state_ref[row, pl.ds(0, MAX_ROW), lanes] = (
                state_ref[row, pl.ds(0, MAX_ROW), lanes] * fade + part
            )

    def one_query_tile(target, row):
        total = list_ref[2 * target + row, slot]
        blocks = (total + 1) // 4
        rest = total - 4 * blocks

        def full(turn, carry):
            block(target, row, 4 * turn, 4)
            return carry

        lax.fori_loop(0, blocks, full, 0)

        @pl.when(rest > 0)
        def _():
            block(target, row, 4 * blocks, 2)

    for target in targets:
        for row in range(2):
            one_query_tile(target, row)


def stage(columns, near, parts, state, numbers, name):
    shape = jax.ShapeDtypeStruct((2, ROWS, WIDE), jnp.float32)
    slots = sum(2 * len(order) for _, order in columns)
    args = [*near, *parts]
    outs = len({number // 2 for number in numbers})
    aliases = {}
    if state is not None:
        aliases = {len(args) + i: i for i in range(outs)}
        args += list(state)
    kernel = lambda *refs: stage_kernel(columns, len(parts), numbers, state is None, *refs)
    return call(
        kernel,
        (shape,) * outs,
        args,
        [smem()] + [vmem()] * (len(args) - 1),
        scratch=(
            pltpu.VMEM((2 * slots, TILE, TILE), jnp.bfloat16),
            pltpu.SMEM((4, slots + 1), jnp.int32),
        ),
        aliases=aliases,
        name=name,
    )


def merge_kernel(own_ref, other_ref, out_ref):
    for t in range(2):
        own_max = own_ref[t, pl.ds(MAX_ROW, 1), :]
        other_max = other_ref[t, pl.ds(MAX_ROW, 1), :]
        row_max = jnp.maximum(own_max, other_max)
        own_weight = jnp.exp2((own_max - row_max) * EXP2_SCALE)
        other_weight = jnp.exp2((other_max - row_max) * EXP2_SCALE)
        total = (
            own_ref[t, pl.ds(SUM_ROW, 1), :] * own_weight
            + other_ref[t, pl.ds(SUM_ROW, 1), :] * other_weight
        )
        own_weight = own_weight / total
        other_weight = other_weight / total
        for h in range(HEADS):
            lanes = slice(h * TILE, (h + 1) * TILE)
            attended = (
                own_ref[t, pl.ds(0, HD), lanes] * own_weight[:, lanes]
                + other_ref[t, pl.ds(0, HD), lanes] * other_weight[:, lanes]
            )
            out_ref[pl.ds(t * TILE, TILE), pl.ds(h * HD, HD)] = attended.T.astype(jnp.bfloat16)


def ring(size, step):
    return [(i, (i + step) % size) for i in range(size)]


def along_y(move):
    pairs = []
    for i in range(8):
        yh, yl, core = move(i // 4, i // 2 % 2, i % 2)
        pairs.append((i, yh % 2 * 4 + yl % 2 * 2 + core % 2))
    return pairs


def next_y(yh, yl, step):
    y = (yh * 2 + yl + step) % 4
    return y // 2, y % 2


Y = ("yh", "yl", "core")
YZ = ("z", "yh", "yl", "core")


def turned(shift):
    turn = along_y(lambda yh, yl, core: (core, yl, yh))
    return [(z * 8 + a, (z + shift) % NZ * 8 + b) for z in range(NZ) for a, b in turn]


def project_kernel(flip, place_ref, near_ref, far_ref, weight_ref, far_weight_ref, out_ref):
    width = out_ref.shape[1]
    which = place_ref[1] + flip - 2 * flip * place_ref[1]
    for n in range(width // 256):
        at = pl.multiple_of(which * width + n * 256, 256)
        far = far_weight_ref[:, pl.ds(at, 256)]
        total = jnp.dot(far_ref[...], far, preferred_element_type=jnp.float32)
        at = pl.multiple_of(place_ref[0] * (2 * width) + which * width + n * 256, 256)
        near = weight_ref[:, pl.ds(at, 256)]
        total = total + jnp.dot(near_ref[...], near, preferred_element_type=jnp.float32)
        out_ref[:, n * 256 : (n + 1) * 256] = total.astype(out_ref.dtype)


def project(flip, place, near, far, weight, far_weight, dtype, name):
    shape = jax.ShapeDtypeStruct((near.shape[0], far_weight.shape[1] // 2), dtype)
    return call(
        lambda *refs: project_kernel(flip, *refs),
        shape,
        (place, near, far, weight, far_weight),
        [smem()] + [vmem()] * 4,
        name=name,
    )


def add_kernel(keep_ref, other_ref, out_ref):
    out_ref[...] = (keep_ref[...] + other_ref[...].astype(jnp.float32)).astype(out_ref.dtype)


def per_device(queries, key_rows, value_rows, tile_mask, out_weight):
    x, z = lax.axis_index("x"), lax.axis_index("z")
    yh, yl, core = lax.axis_index("yh"), lax.axis_index("yl"), lax.axis_index("core")
    turn = along_y(lambda yh, yl, core: (core, yl, yh))
    swap = [(0, 1), (1, 0)]
    together = lax.optimization_barrier

    unit, bundle = pack(key_rows, value_rows, queries, tile_mask)
    up, down = ring(NZ, 1), ring(NZ, -1)
    units = {-1: lax.ppermute(unit, YZ, turned(1)), 1: lax.ppermute(unit, YZ, turned(-1))}
    mine = lax.ppermute(bundle, Y, turn)
    units[4] = lax.ppermute(unit, YZ, turned(4))
    half_away = column_half(out_weight, 1 - yl)
    units[-1], units[1], units[4], mine, half_away = together(
        (units[-1], units[1], units[4], mine, half_away)
    )
    away = along_y(lambda yh, yl, core: (*next_y(yh, yl, 1 - 2 * core), core))
    far_weight = lax.ppermute(half_away, Y, away)
    early = join([units[-1], units[1], (mine, UNIT_AT), units[4]])
    forth, back = ring(NX, 1), ring(NX, -1)
    early_before = lax.ppermute(early, "x", forth)
    early_after = lax.ppermute(early, "x", back)
    for step in (2, 3):
        units[-step] = lax.ppermute(units[1 - step], "z", up)
        units[step] = lax.ppermute(units[step - 1], "z", down)
    late, mine, early_before, early_after = together(
        (join([units[d] for d in LATE]), mine, early_before, early_after)
    )
    late_before = lax.ppermute(late, "x", forth)
    late_after = lax.ppermute(late, "x", back)
    theirs = lax.ppermute(mine, "core", swap)
    place = jnp.pad(jnp.stack([x, z, core]).astype(jnp.int32), (0, 125))[None]
    masks = jnp.concatenate([mine[MASK_AT, :2], theirs[MASK_AT, :2]]).astype(jnp.int32)
    table = jnp.concatenate([masks, place])

    near = (table, mine, theirs)
    every = (0, 1, 2, 3)
    state = stage(((0, EARLY), (0, LATE)), near, [early, late], None, every, "own_column")
    half = early.shape[0] // 2
    early_far = [
        lax.ppermute(early_before[:half], "x", forth),
        lax.ppermute(early_after[half:], "x", back),
    ]
    state = stage(
        ((-1, EARLY), (1, EARLY)), near, [early_before, early_after], state, every, "early"
    )
    late_before, late_after, *state = together((late_before, late_after, *state))
    late_far = [
        lax.ppermute(late_before[:half], "x", forth),
        lax.ppermute(late_after[half:], "x", back),
    ]
    keep, send = stage(
        ((-1, LATE), (1, LATE)), near, [late_before, late_after], state, every, "late"
    )
    *far, keep, send = together((*early_far, *late_far, keep, send))
    last = (((2, EARLY), (2, LATE)), near, far)
    (send,) = stage(*last, (send,), (2, 3), "last_send")
    received = lax.ppermute(send, "core", swap)
    (keep,) = stage(*last, (keep,), (0, 1), "last_keep")
    shape = jax.ShapeDtypeStruct((2 * TILE, WIDE), jnp.bfloat16)
    attended = call(merge_kernel, shape, (keep, received), [vmem()] * 2, name="merge")

    near_part = lax.ppermute(attended, Y, turn)
    far_part = lax.ppermute(attended, Y, along_y(lambda yh, yl, core: (core, 1 - yl, yh)))
    where = jnp.stack([yl, core]).astype(jnp.int32)
    sides = (where, near_part, far_part, out_weight, fetch(far_weight))
    other = project(1, *sides, jnp.bfloat16, "project_send")
    other = lax.ppermute(other, "core", swap)
    own = project(0, *sides, jnp.float32, "project_keep")
    shape = jax.ShapeDtypeStruct(own.shape, jnp.bfloat16)
    return call(add_kernel, shape, (own, other), [vmem()] * 2, name="add")


def solution(mesh):
    fine = Mesh(mesh.devices.reshape(NX, NZ, 2, 2, 2), ("x", "z", "yh", "yl", "core"))
    tok, head = ("x", "z", "yh"), ("yl", "core")
    return jax.shard_map(
        per_device,
        mesh=fine,
        in_specs=(P(tok, head), P(tok, head), P(tok, head), P(tok, None), P(head, None)),
        out_specs=P(tok, head),
        check_vma=False,
    )
```

```python
import math

import jax
import jax.numpy as jnp
from jax import lax
from jax.experimental import pallas as pl
from jax.experimental.pallas import tpu as pltpu
from jax.sharding import Mesh, PartitionSpec as P

HD = 128
TILE = 128
NX, NZ = 4, 8
HEADS = 6
WIDE = HEADS * TILE
SUM_ROW = HD
MAX_ROW = HD + 16
ROWS = HD + 24
NEGATIVE = -1e30
MASK_AT = 2 * HEADS
UNIT_AT = MASK_AT + 1
EXP2_SCALE = math.log2(math.e) / math.sqrt(HD)
EARLY = (-1, 1, 0, 4)
LATE = (-2, 2, -3, 3)


def vmem():
    return pl.BlockSpec(memory_space=pltpu.VMEM)


def smem():
    return pl.BlockSpec(memory_space=pltpu.SMEM)


def hbm():
    return pl.BlockSpec(memory_space=pl.ANY)


def in_hbm(x):
    return pltpu.with_memory_space_constraint(x, pltpu.HBM)


def call(kernel, out_shape, args, in_specs, scratch=(), aliases=None, name=None, flops=0):
    return pl.pallas_call(
        kernel,
        out_shape=out_shape,
        in_specs=in_specs,
        out_specs=jax.tree.map(lambda s: vmem(), out_shape),
        scratch_shapes=list(scratch),
        input_output_aliases=aliases or {},
        compiler_params=pltpu.CompilerParams(vmem_limit_bytes=14 * 1024 * 1024),
        cost_estimate=pl.CostEstimate(flops=flops, transcendentals=0, bytes_accessed=0),
        name=name,
    )(*args)


def pack_kernel(key_hbm, value_hbm, query_hbm, mask_hbm, unit_ref, out_ref, *scratch):
    *buffers, sems = scratch
    key_ref, value_ref, query_ref, mask_ref = buffers
    copies = [
        pltpu.make_async_copy(source, target, sems.at[i])
        for i, (source, target) in enumerate(
            zip((key_hbm, value_hbm, query_hbm, mask_hbm), buffers)
        )
    ]
    for copy in copies:
        copy.start()
    for copy in copies:
        copy.wait()
    for t in range(2):
        rows = pl.ds(t * TILE, TILE)
        values = value_ref[rows, :].astype(jnp.float32).T.astype(jnp.bfloat16)
        for ref, at in ((unit_ref, 0), (out_ref, UNIT_AT)):
            ref[at + t] = key_ref[rows, :]
            ref[at + 2 + t] = values
        for h in range(HEADS):
            out_ref[t * HEADS + h] = query_ref[rows, pl.ds(h * HD, HD)]
    out_ref[MASK_AT] = jnp.zeros((TILE, TILE), jnp.bfloat16)
    out_ref[MASK_AT, 0:2, :] = mask_ref[...].astype(jnp.float32).astype(jnp.bfloat16)


def pack(*arrays):
    return call(
        pack_kernel,
        tuple(
            jax.ShapeDtypeStruct((size, TILE, TILE), jnp.bfloat16) for size in (4, UNIT_AT + 4)
        ),
        tuple(in_hbm(a) for a in arrays),
        [hbm()] * 4,
        scratch=[pltpu.VMEM(a.shape, a.dtype) for a in arrays] + [pltpu.SemaphoreType.DMA((4,))],
        name="pack",
    )


def half_kernel(half_ref, source_ref, out_ref, sems):
    rows = out_ref.shape[0] // 8
    start = pl.multiple_of(half_ref[0] * out_ref.shape[1], out_ref.shape[1])
    copies = [
        pltpu.make_async_copy(
            source_ref.at[pl.ds(i * rows, rows), pl.ds(start, out_ref.shape[1])],
            out_ref.at[pl.ds(i * rows, rows), :],
            sems.at[i],
        )
        for i in range(8)
    ]
    for copy in copies:
        copy.start()
    for copy in copies:
        copy.wait()


def column_half(source, number):
    return call(
        half_kernel,
        jax.ShapeDtypeStruct((source.shape[0], source.shape[1] // 2), source.dtype),
        (number.reshape(1).astype(jnp.int32), in_hbm(source)),
        [smem(), hbm()],
        scratch=(pltpu.SemaphoreType.DMA((8,)),),
        name="column_half",
    )


def fetch_kernel(source_ref, out_ref, sems):
    rows = out_ref.shape[0] // 4
    copies = [
        pltpu.make_async_copy(
            source_ref.at[pl.ds(i * rows, rows), :], out_ref.at[pl.ds(i * rows, rows), :], sems.at[i]
        )
        for i in range(4)
    ]
    for copy in copies:
        copy.start()
    for copy in copies:
        copy.wait()


def fetch(source):
    shape = jax.ShapeDtypeStruct(source.shape, source.dtype)
    scratch = (pltpu.SemaphoreType.DMA((4,)),)
    return call(fetch_kernel, shape, (in_hbm(source),), [hbm()], scratch=scratch, name="fetch")


def join_kernel(starts, *refs):
    out_ref = refs[-1]
    at = 0
    for start, ref in zip(starts, refs[:-1]):
        size = ref.shape[0] - start
        out_ref[pl.ds(at, size)] = ref[pl.ds(start, size)]
        at += size


def join(parts):
    starts = [p[1] if isinstance(p, tuple) else 0 for p in parts]
    parts = [p[0] if isinstance(p, tuple) else p for p in parts]
    total = sum(p.shape[0] - start for p, start in zip(parts, starts))
    shape = jax.ShapeDtypeStruct((total, *parts[0].shape[1:]), parts[0].dtype)
    kernel = lambda *refs: join_kernel(starts, *refs)
    return call(kernel, shape, parts, [vmem()] * len(parts), name="join")


def stage_kernel(columns, count, numbers, first, table_ref, mine_ref, theirs_ref, *refs):
    parts, refs = refs[:count], refs[count:]
    targets = sorted({number // 2 for number in numbers})
    if not first:
        refs = refs[len(targets) :]
    states, (tiles_ref, list_ref) = refs[: len(targets)], refs[len(targets) :]
    x, z, core = table_ref[4, 0], table_ref[4, 1], table_ref[4, 2]
    at = 0
    for part in parts:
        tiles_ref[pl.ds(at, part.shape[0])] = part[...]
        at += part.shape[0]
    if first:
        for ref in states:
            ref[:, :MAX_ROW, :] = jnp.zeros((2, MAX_ROW, WIDE), jnp.float32)
            ref[:, MAX_ROW:, :] = jnp.full((2, ROWS - MAX_ROW, WIDE), NEGATIVE, jnp.float32)

    counts = [jnp.int32(0)] * 4
    slot = 0
    for dx, order in columns:
        for dz in order:
            block = lax.rem(x + dx + NX, NX) * NZ + lax.rem(z + dz + NZ, NZ)
            for r in range(2):
                tile = (block * 2 + core) * 2 + r
                for number in numbers:
                    list_ref[number, counts[number]] = slot // 2 * 4 + slot % 2
                    counts[number] = counts[number] + table_ref[number, tile]
                slot += 1

    for number in numbers:
        list_ref[number, slot] = counts[number]

    def block(target, row, base, size):
        state_ref = states[targets.index(target)]
        source = theirs_ref if target else mine_ref
        number = 2 * target + row
        at = [list_ref[number, base + j] for j in range(size - 1)]
        live = base + size - 1 < list_ref[number, slot]
        at.append(jnp.where(live, list_ref[number, base + size - 1], at[0]))
        ones = jnp.ones((16, TILE), jnp.bfloat16)
        values = [jnp.concatenate([tiles_ref[i + 2], ones], axis=0) for i in at]
        values[-1] = values[-1] * jnp.where(live, 1.0, 0.0).astype(jnp.bfloat16)
        values = jnp.concatenate(values, axis=1)
        keys = jnp.concatenate([tiles_ref[i] for i in at], axis=0)
        chunks = [pl.ds(h * TILE, TILE) for h in range(HEADS)]
        scores = [
            lax.dot_general(
                keys,
                source[row * HEADS + h],
                (((1,), (1,)), ((), ())),
                preferred_element_type=jnp.float32,
            )
            for h in range(HEADS)
        ]
        probs = []
        for lanes, score in zip(chunks, scores):
            old_max = state_ref[row, pl.ds(MAX_ROW, 1), lanes]
            new_max = jnp.maximum(old_max, jnp.max(score, axis=0, keepdims=True))
            prob = jnp.exp2((score - new_max) * EXP2_SCALE).astype(jnp.bfloat16)
            probs.append((prob, jnp.exp2((old_max - new_max) * EXP2_SCALE)))
            state_ref[row, pl.ds(MAX_ROW, 8), lanes] = jnp.broadcast_to(new_max, (8, TILE))
        for lanes, (prob, fade) in zip(chunks, probs):
            part = lax.dot_general(
                values, prob, (((1,), (0,)), ((), ())), preferred_element_type=jnp.float32
            )
            state_ref[row, pl.ds(0, MAX_ROW), lanes] = (
                state_ref[row, pl.ds(0, MAX_ROW), lanes] * fade + part
            )

    def one_query_tile(target, row):
        total = list_ref[2 * target + row, slot]
        blocks = (total + 1) // 4
        rest = total - 4 * blocks

        def full(turn, carry):
            block(target, row, 4 * turn, 4)
            return carry

        lax.fori_loop(0, blocks, full, 0)

        @pl.when(rest > 0)
        def _():
            block(target, row, 4 * blocks, 2)

    for target in targets:
        for row in range(2):
            one_query_tile(target, row)


def stage(columns, near, parts, state, numbers, name):
    shape = jax.ShapeDtypeStruct((2, ROWS, WIDE), jnp.float32)
    slots = sum(2 * len(order) for _, order in columns)
    args = [*near, *parts]
    outs = len({number // 2 for number in numbers})
    aliases = {}
    if state is not None:
        aliases = {len(args) + i: i for i in range(outs)}
        args += list(state)
    kernel = lambda *refs: stage_kernel(columns, len(parts), numbers, state is None, *refs)
    return call(
        kernel,
        (shape,) * outs,
        args,
        [smem()] + [vmem()] * (len(args) - 1),
        scratch=(
            pltpu.VMEM((2 * slots, TILE, TILE), jnp.bfloat16),
            pltpu.SMEM((4, slots + 1), jnp.int32),
        ),
        aliases=aliases,
        name=name,
    )


def merge_kernel(own_ref, other_ref, out_ref):
    for t in range(2):
        own_max = own_ref[t, pl.ds(MAX_ROW, 1), :]
        other_max = other_ref[t, pl.ds(MAX_ROW, 1), :]
        row_max = jnp.maximum(own_max, other_max)
        own_weight = jnp.exp2((own_max - row_max) * EXP2_SCALE)
        other_weight = jnp.exp2((other_max - row_max) * EXP2_SCALE)
        total = (
            own_ref[t, pl.ds(SUM_ROW, 1), :] * own_weight
            + other_ref[t, pl.ds(SUM_ROW, 1), :] * other_weight
        )
        own_weight = own_weight / total
        other_weight = other_weight / total
        for h in range(HEADS):
            lanes = slice(h * TILE, (h + 1) * TILE)
            attended = (
                own_ref[t, pl.ds(0, HD), lanes] * own_weight[:, lanes]
                + other_ref[t, pl.ds(0, HD), lanes] * other_weight[:, lanes]
            )
            out_ref[pl.ds(t * TILE, TILE), pl.ds(h * HD, HD)] = attended.T.astype(jnp.bfloat16)


def ring(size, step):
    return [(i, (i + step) % size) for i in range(size)]


def along_y(move):
    pairs = []
    for i in range(8):
        yh, yl, core = move(i // 4, i // 2 % 2, i % 2)
        pairs.append((i, yh % 2 * 4 + yl % 2 * 2 + core % 2))
    return pairs


def next_y(yh, yl, step):
    y = (yh * 2 + yl + step) % 4
    return y // 2, y % 2


Y = ("yh", "yl", "core")
YZ = ("z", "yh", "yl", "core")


def turned(shift):
    turn = along_y(lambda yh, yl, core: (core, yl, yh))
    return [(z * 8 + a, (z + shift) % NZ * 8 + b) for z in range(NZ) for a, b in turn]


def project_kernel(flip, place_ref, near_ref, far_ref, weight_ref, far_weight_ref, out_ref):
    width = out_ref.shape[1]
    which = place_ref[1] + flip - 2 * flip * place_ref[1]
    for n in range(width // 256):
        at = pl.multiple_of(which * width + n * 256, 256)
        far = far_weight_ref[:, pl.ds(at, 256)]
        total = jnp.dot(far_ref[...], far, preferred_element_type=jnp.float32)
        at = pl.multiple_of(place_ref[0] * (2 * width) + which * width + n * 256, 256)
        near = weight_ref[:, pl.ds(at, 256)]
        total = total + jnp.dot(near_ref[...], near, preferred_element_type=jnp.float32)
        out_ref[:, n * 256 : (n + 1) * 256] = total.astype(out_ref.dtype)


def project(flip, place, near, far, weight, far_weight, dtype, name):
    shape = jax.ShapeDtypeStruct((near.shape[0], far_weight.shape[1] // 2), dtype)
    return call(
        lambda *refs: project_kernel(flip, *refs),
        shape,
        (place, near, far, weight, far_weight),
        [smem()] + [vmem()] * 4,
        name=name,
    )


def add_kernel(keep_ref, other_ref, out_ref):
    out_ref[...] = (keep_ref[...] + other_ref[...].astype(jnp.float32)).astype(out_ref.dtype)


def per_device(queries, key_rows, value_rows, tile_mask, out_weight):
    x, z = lax.axis_index("x"), lax.axis_index("z")
    yh, yl, core = lax.axis_index("yh"), lax.axis_index("yl"), lax.axis_index("core")
    turn = along_y(lambda yh, yl, core: (core, yl, yh))
    swap = [(0, 1), (1, 0)]
    together = lax.optimization_barrier

    unit, bundle = pack(key_rows, value_rows, queries, tile_mask)
    up, down = ring(NZ, 1), ring(NZ, -1)
    units = {-1: lax.ppermute(unit, YZ, turned(1)), 1: lax.ppermute(unit, YZ, turned(-1))}
    mine = lax.ppermute(bundle, Y, turn)
    units[4] = lax.ppermute(unit, YZ, turned(4))
    half_away = column_half(out_weight, 1 - yl)
    units[-1], units[1], units[4], mine, half_away = together(
        (units[-1], units[1], units[4], mine, half_away)
    )
    away = along_y(lambda yh, yl, core: (*next_y(yh, yl, 1 - 2 * core), core))
    far_weight = lax.ppermute(half_away, Y, away)
    early = join([units[-1], units[1], (mine, UNIT_AT), units[4]])
    forth, back = ring(NX, 1), ring(NX, -1)
    early_before = lax.ppermute(early, "x", forth)
    early_after = lax.ppermute(early, "x", back)
    for step in (2, 3):
        units[-step] = lax.ppermute(units[1 - step], "z", up)
        units[step] = lax.ppermute(units[step - 1], "z", down)
    late, mine, early_before, early_after = together(
        (join([units[d] for d in LATE]), mine, early_before, early_after)
    )
    late_before = lax.ppermute(late, "x", forth)
    late_after = lax.ppermute(late, "x", back)
    theirs = lax.ppermute(mine, "core", swap)
    place = jnp.pad(jnp.stack([x, z, core]).astype(jnp.int32), (0, 125))[None]
    masks = jnp.concatenate([mine[MASK_AT, :2], theirs[MASK_AT, :2]]).astype(jnp.int32)
    table = jnp.concatenate([masks, place])

    near = (table, mine, theirs)
    every = (0, 1, 2, 3)
    half = early.shape[0] // 2
    early_far = [
        lax.ppermute(early_before[:half], "x", forth),
        lax.ppermute(early_after[half:], "x", back),
    ]
    columns = ((0, EARLY), (0, LATE), (-1, EARLY), (1, EARLY))
    parts = [early, late, early_before, early_after]
    state = stage(columns, near, parts, None, every, "first")
    late_before, late_after, *state = together((late_before, late_after, *state))
    late_far = [
        lax.ppermute(late_before[:half], "x", forth),
        lax.ppermute(late_after[half:], "x", back),
    ]
    keep, send = stage(
        ((-1, LATE), (1, LATE)), near, [late_before, late_after], state, every, "late"
    )
    *far, keep, send = together((*early_far, *late_far, keep, send))
    last = (((2, EARLY), (2, LATE)), near, far)
    (send,) = stage(*last, (send,), (2, 3), "last_send")
    received = lax.ppermute(send, "core", swap)
    (keep,) = stage(*last, (keep,), (0, 1), "last_keep")
    shape = jax.ShapeDtypeStruct((2 * TILE, WIDE), jnp.bfloat16)
    attended = call(merge_kernel, shape, (keep, received), [vmem()] * 2, name="merge")

    near_part = lax.ppermute(attended, Y, turn)
    far_part = lax.ppermute(attended, Y, along_y(lambda yh, yl, core: (core, 1 - yl, yh)))
    where = jnp.stack([yl, core]).astype(jnp.int32)
    sides = (where, near_part, far_part, out_weight, fetch(far_weight))
    other = project(1, *sides, jnp.bfloat16, "project_send")
    other = lax.ppermute(other, "core", swap)
    own = project(0, *sides, jnp.float32, "project_keep")
    shape = jax.ShapeDtypeStruct(own.shape, jnp.bfloat16)
    return call(add_kernel, shape, (own, other), [vmem()] * 2, name="add")


def solution(mesh):
    fine = Mesh(mesh.devices.reshape(NX, NZ, 2, 2, 2), ("x", "z", "yh", "yl", "core"))
    tok, head = ("x", "z", "yh"), ("yl", "core")
    return jax.shard_map(
        per_device,
        mesh=fine,
        in_specs=(P(tok, head), P(tok, head), P(tok, head), P(tok, None), P(head, None)),
        out_specs=P(tok, head),
        check_vma=False,
    )
```

```python
import math

import jax
import jax.numpy as jnp
from jax import lax
from jax.experimental import pallas as pl
from jax.experimental.pallas import tpu as pltpu
from jax.sharding import Mesh, PartitionSpec as P

HD = 128
TILE = 128
NX, NZ = 4, 8
HEADS = 6
WIDE = HEADS * TILE
SUM_ROW = HD
MAX_ROW = HD + 16
ROWS = HD + 24
NEGATIVE = -1e30
MASK_AT = 2 * HEADS
UNIT_AT = MASK_AT + 1
EXP2_SCALE = math.log2(math.e) / math.sqrt(HD)
EARLY = (-1, 1, 0, 4)
LATE = (-2, 2, -3, 3)


def vmem():
    return pl.BlockSpec(memory_space=pltpu.VMEM)


def smem():
    return pl.BlockSpec(memory_space=pltpu.SMEM)


def hbm():
    return pl.BlockSpec(memory_space=pl.ANY)


def in_hbm(x):
    return pltpu.with_memory_space_constraint(x, pltpu.HBM)


def call(kernel, out_shape, args, in_specs, scratch=(), aliases=None, name=None, flops=0):
    return pl.pallas_call(
        kernel,
        out_shape=out_shape,
        in_specs=in_specs,
        out_specs=jax.tree.map(lambda s: vmem(), out_shape),
        scratch_shapes=list(scratch),
        input_output_aliases=aliases or {},
        compiler_params=pltpu.CompilerParams(vmem_limit_bytes=14 * 1024 * 1024),
        cost_estimate=pl.CostEstimate(flops=flops, transcendentals=0, bytes_accessed=0),
        name=name,
    )(*args)


def pack_kernel(key_hbm, value_hbm, query_hbm, mask_hbm, unit_ref, out_ref, *scratch):
    *buffers, sems = scratch
    key_ref, value_ref, query_ref, mask_ref = buffers
    copies = [
        pltpu.make_async_copy(source, target, sems.at[i])
        for i, (source, target) in enumerate(
            zip((key_hbm, value_hbm, query_hbm, mask_hbm), buffers)
        )
    ]
    for copy in copies:
        copy.start()
    for copy in copies:
        copy.wait()
    for t in range(2):
        rows = pl.ds(t * TILE, TILE)
        values = value_ref[rows, :].astype(jnp.float32).T.astype(jnp.bfloat16)
        for ref, at in ((unit_ref, 0), (out_ref, UNIT_AT)):
            ref[at + t] = key_ref[rows, :]
            ref[at + 2 + t] = values
        for h in range(HEADS):
            out_ref[t * HEADS + h] = query_ref[rows, pl.ds(h * HD, HD)]
    out_ref[MASK_AT] = jnp.zeros((TILE, TILE), jnp.bfloat16)
    out_ref[MASK_AT, 0:2, :] = mask_ref[...].astype(jnp.float32).astype(jnp.bfloat16)


def pack(*arrays):
    return call(
        pack_kernel,
        tuple(
            jax.ShapeDtypeStruct((size, TILE, TILE), jnp.bfloat16) for size in (4, UNIT_AT + 4)
        ),
        tuple(in_hbm(a) for a in arrays),
        [hbm()] * 4,
        scratch=[pltpu.VMEM(a.shape, a.dtype) for a in arrays] + [pltpu.SemaphoreType.DMA((4,))],
        name="pack",
    )


def half_kernel(half_ref, source_ref, out_ref, sems):
    rows = out_ref.shape[0] // 8
    start = pl.multiple_of(half_ref[0] * out_ref.shape[1], out_ref.shape[1])
    copies = [
        pltpu.make_async_copy(
            source_ref.at[pl.ds(i * rows, rows), pl.ds(start, out_ref.shape[1])],
            out_ref.at[pl.ds(i * rows, rows), :],
            sems.at[i],
        )
        for i in range(8)
    ]
    for copy in copies:
        copy.start()
    for copy in copies:
        copy.wait()


def column_half(source, number):
    return call(
        half_kernel,
        jax.ShapeDtypeStruct((source.shape[0], source.shape[1] // 2), source.dtype),
        (number.reshape(1).astype(jnp.int32), in_hbm(source)),
        [smem(), hbm()],
        scratch=(pltpu.SemaphoreType.DMA((8,)),),
        name="column_half",
    )


def fetch_kernel(source_ref, out_ref, sems):
    rows = out_ref.shape[0] // 4
    copies = [
        pltpu.make_async_copy(
            source_ref.at[pl.ds(i * rows, rows), :], out_ref.at[pl.ds(i * rows, rows), :], sems.at[i]
        )
        for i in range(4)
    ]
    for copy in copies:
        copy.start()
    for copy in copies:
        copy.wait()


def fetch(source):
    shape = jax.ShapeDtypeStruct(source.shape, source.dtype)
    scratch = (pltpu.SemaphoreType.DMA((4,)),)
    return call(fetch_kernel, shape, (in_hbm(source),), [hbm()], scratch=scratch, name="fetch")


def join_kernel(starts, *refs):
    out_ref = refs[-1]
    at = 0
    for start, ref in zip(starts, refs[:-1]):
        size = ref.shape[0] - start
        out_ref[pl.ds(at, size)] = ref[pl.ds(start, size)]
        at += size


def join(parts):
    starts = [p[1] if isinstance(p, tuple) else 0 for p in parts]
    parts = [p[0] if isinstance(p, tuple) else p for p in parts]
    total = sum(p.shape[0] - start for p, start in zip(parts, starts))
    shape = jax.ShapeDtypeStruct((total, *parts[0].shape[1:]), parts[0].dtype)
    kernel = lambda *refs: join_kernel(starts, *refs)
    return call(kernel, shape, parts, [vmem()] * len(parts), name="join")


def stage_kernel(columns, count, numbers, first, table_ref, mine_ref, theirs_ref, *refs):
    parts, refs = refs[:count], refs[count:]
    targets = sorted({number // 2 for number in numbers})
    if not first:
        refs = refs[len(targets) :]
    states, (tiles_ref, list_ref) = refs[: len(targets)], refs[len(targets) :]
    x, z, core = table_ref[4, 0], table_ref[4, 1], table_ref[4, 2]
    at = 0
    for part in parts:
        tiles_ref[pl.ds(at, part.shape[0])] = part[...]
        at += part.shape[0]
    if first:
        for ref in states:
            ref[:, :MAX_ROW, :] = jnp.zeros((2, MAX_ROW, WIDE), jnp.float32)
            ref[:, MAX_ROW:, :] = jnp.full((2, ROWS - MAX_ROW, WIDE), NEGATIVE, jnp.float32)

    counts = [jnp.int32(0)] * 4
    slot = 0
    for dx, order in columns:
        for dz in order:
            block = lax.rem(x + dx + NX, NX) * NZ + lax.rem(z + dz + NZ, NZ)
            for r in range(2):
                tile = (block * 2 + core) * 2 + r
                for number in numbers:
                    list_ref[number, counts[number]] = slot // 2 * 4 + slot % 2
                    counts[number] = counts[number] + table_ref[number, tile]
                slot += 1

    for number in numbers:
        list_ref[number, slot] = counts[number]

    def block(target, row, base, size):
        state_ref = states[targets.index(target)]
        source = theirs_ref if target else mine_ref
        number = 2 * target + row
        at = [list_ref[number, base + j] for j in range(size - 1)]
        live = base + size - 1 < list_ref[number, slot]
        at.append(jnp.where(live, list_ref[number, base + size - 1], at[0]))
        ones = jnp.ones((16, TILE), jnp.bfloat16)
        values = [jnp.concatenate([tiles_ref[i + 2], ones], axis=0) for i in at]
        values[-1] = values[-1] * jnp.where(live, 1.0, 0.0).astype(jnp.bfloat16)
        values = jnp.concatenate(values, axis=1)
        keys = jnp.concatenate([tiles_ref[i] for i in at], axis=0)
        chunks = [pl.ds(h * TILE, TILE) for h in range(HEADS)]
        scores = [
            lax.dot_general(
                keys,
                source[row * HEADS + h],
                (((1,), (1,)), ((), ())),
                preferred_element_type=jnp.float32,
            )
            for h in range(HEADS)
        ]
        probs = []
        for lanes, score in zip(chunks, scores):
            old_max = state_ref[row, pl.ds(MAX_ROW, 1), lanes]
            new_max = jnp.maximum(old_max, jnp.max(score, axis=0, keepdims=True))
            prob = jnp.exp2((score - new_max) * EXP2_SCALE).astype(jnp.bfloat16)
            probs.append((prob, jnp.exp2((old_max - new_max) * EXP2_SCALE)))
            state_ref[row, pl.ds(MAX_ROW, 8), lanes] = jnp.broadcast_to(new_max, (8, TILE))
        for lanes, (prob, fade) in zip(chunks, probs):
            part = lax.dot_general(
                values, prob, (((1,), (0,)), ((), ())), preferred_element_type=jnp.float32
            )
            state_ref[row, pl.ds(0, MAX_ROW), lanes] = (
                state_ref[row, pl.ds(0, MAX_ROW), lanes] * fade + part
            )

    def one_query_tile(target, row):
        total = list_ref[2 * target + row, slot]
        blocks = (total + 1) // 4
        rest = total - 4 * blocks

        def full(turn, carry):
            block(target, row, 4 * turn, 4)
            return carry

        lax.fori_loop(0, blocks, full, 0)

        @pl.when(rest > 0)
        def _():
            block(target, row, 4 * blocks, 2)

    for target in targets:
        for row in range(2):
            one_query_tile(target, row)


def stage(columns, near, parts, state, numbers, name):
    shape = jax.ShapeDtypeStruct((2, ROWS, WIDE), jnp.float32)
    slots = sum(2 * len(order) for _, order in columns)
    args = [*near, *parts]
    outs = len({number // 2 for number in numbers})
    aliases = {}
    if state is not None:
        aliases = {len(args) + i: i for i in range(outs)}
        args += list(state)
    kernel = lambda *refs: stage_kernel(columns, len(parts), numbers, state is None, *refs)
    return call(
        kernel,
        (shape,) * outs,
        args,
        [smem()] + [vmem()] * (len(args) - 1),
        scratch=(
            pltpu.VMEM((2 * slots, TILE, TILE), jnp.bfloat16),
            pltpu.SMEM((4, slots + 1), jnp.int32),
        ),
        aliases=aliases,
        name=name,
    )


def merge_kernel(own_ref, other_ref, out_ref):
    for t in range(2):
        own_max = own_ref[t, pl.ds(MAX_ROW, 1), :]
        other_max = other_ref[t, pl.ds(MAX_ROW, 1), :]
        row_max = jnp.maximum(own_max, other_max)
        own_weight = jnp.exp2((own_max - row_max) * EXP2_SCALE)
        other_weight = jnp.exp2((other_max - row_max) * EXP2_SCALE)
        total = (
            own_ref[t, pl.ds(SUM_ROW, 1), :] * own_weight
            + other_ref[t, pl.ds(SUM_ROW, 1), :] * other_weight
        )
        own_weight = own_weight / total
        other_weight = other_weight / total
        for h in range(HEADS):
            lanes = slice(h * TILE, (h + 1) * TILE)
            attended = (
                own_ref[t, pl.ds(0, HD), lanes] * own_weight[:, lanes]
                + other_ref[t, pl.ds(0, HD), lanes] * other_weight[:, lanes]
            )
            out_ref[pl.ds(t * TILE, TILE), pl.ds(h * HD, HD)] = attended.T.astype(jnp.bfloat16)


def ring(size, step):
    return [(i, (i + step) % size) for i in range(size)]


def along_y(move):
    pairs = []
    for i in range(8):
        yh, yl, core = move(i // 4, i // 2 % 2, i % 2)
        pairs.append((i, yh % 2 * 4 + yl % 2 * 2 + core % 2))
    return pairs


def next_y(yh, yl, step):
    y = (yh * 2 + yl + step) % 4
    return y // 2, y % 2


Y = ("yh", "yl", "core")
YZ = ("z", "yh", "yl", "core")


def turned(shift):
    turn = along_y(lambda yh, yl, core: (core, yl, yh))
    return [(z * 8 + a, (z + shift) % NZ * 8 + b) for z in range(NZ) for a, b in turn]


def project_kernel(flip, place_ref, near_ref, far_ref, weight_ref, far_weight_ref, out_ref):
    width = out_ref.shape[1]
    which = place_ref[1] + flip - 2 * flip * place_ref[1]
    for n in range(width // 256):
        at = pl.multiple_of(which * width + n * 256, 256)
        far = far_weight_ref[:, pl.ds(at, 256)]
        total = jnp.dot(far_ref[...], far, preferred_element_type=jnp.float32)
        at = pl.multiple_of(place_ref[0] * (2 * width) + which * width + n * 256, 256)
        near = weight_ref[:, pl.ds(at, 256)]
        total = total + jnp.dot(near_ref[...], near, preferred_element_type=jnp.float32)
        out_ref[:, n * 256 : (n + 1) * 256] = total.astype(out_ref.dtype)


def project(flip, place, near, far, weight, far_weight, dtype, name):
    shape = jax.ShapeDtypeStruct((near.shape[0], far_weight.shape[1] // 2), dtype)
    return call(
        lambda *refs: project_kernel(flip, *refs),
        shape,
        (place, near, far, weight, far_weight),
        [smem()] + [vmem()] * 4,
        name=name,
    )


def add_kernel(keep_ref, other_ref, out_ref):
    out_ref[...] = (keep_ref[...] + other_ref[...].astype(jnp.float32)).astype(out_ref.dtype)


def per_device(queries, key_rows, value_rows, tile_mask, out_weight):
    x, z = lax.axis_index("x"), lax.axis_index("z")
    yh, yl, core = lax.axis_index("yh"), lax.axis_index("yl"), lax.axis_index("core")
    turn = along_y(lambda yh, yl, core: (core, yl, yh))
    swap = [(0, 1), (1, 0)]
    together = lax.optimization_barrier

    unit, bundle = pack(key_rows, value_rows, queries, tile_mask)
    up, down = ring(NZ, 1), ring(NZ, -1)
    units = {-1: lax.ppermute(unit, YZ, turned(1)), 1: lax.ppermute(unit, YZ, turned(-1))}
    mine = lax.ppermute(bundle, Y, turn)
    units[4] = lax.ppermute(unit, YZ, turned(4))
    half_away = column_half(out_weight, 1 - yl)
    units[-1], units[1], units[4], mine, half_away = together(
        (units[-1], units[1], units[4], mine, half_away)
    )
    away = along_y(lambda yh, yl, core: (*next_y(yh, yl, 1 - 2 * core), core))
    far_weight = lax.ppermute(half_away, Y, away)
    early = join([units[-1], units[1], (mine, UNIT_AT), units[4]])
    forth, back = ring(NX, 1), ring(NX, -1)
    early_before = lax.ppermute(early, "x", forth)
    early_after = lax.ppermute(early, "x", back)
    for step in (2, 3):
        units[-step] = lax.ppermute(units[1 - step], "z", up)
        units[step] = lax.ppermute(units[step - 1], "z", down)
    late, mine, early_before, early_after = together(
        (join([units[d] for d in LATE]), mine, early_before, early_after)
    )
    late_before = lax.ppermute(late, "x", forth)
    late_after = lax.ppermute(late, "x", back)
    theirs = lax.ppermute(mine, "core", swap)
    place = jnp.pad(jnp.stack([x, z, core]).astype(jnp.int32), (0, 125))[None]
    masks = jnp.concatenate([mine[MASK_AT, :2], theirs[MASK_AT, :2]]).astype(jnp.int32)
    table = jnp.concatenate([masks, place])

    near = (table, mine, theirs)
    every = (0, 1, 2, 3)
    half = early.shape[0] // 2
    early_far = [
        lax.ppermute(early_before[:half], "x", forth),
        lax.ppermute(early_after[half:], "x", back),
    ]
    columns = ((0, EARLY), (0, LATE), (-1, EARLY), (1, EARLY))
    parts = [early, late, early_before, early_after]
    state = stage(columns, near, parts, None, every, "first")
    late_before, late_after, *state = together((late_before, late_after, *state))
    late_far = [
        lax.ppermute(late_before[:half], "x", forth),
        lax.ppermute(late_after[half:], "x", back),
    ]
    columns = ((-1, LATE), (1, LATE), (2, EARLY))
    parts = [late_before, late_after, *early_far]
    keep, send = stage(columns, near, parts, state, every, "late")
    *late_far, keep, send = together((*late_far, keep, send))
    last = (((2, LATE),), near, late_far)
    (send,) = stage(*last, (send,), (2, 3), "last_send")
    received = lax.ppermute(send, "core", swap)
    (keep,) = stage(*last, (keep,), (0, 1), "last_keep")
    shape = jax.ShapeDtypeStruct((2 * TILE, WIDE), jnp.bfloat16)
    attended = call(merge_kernel, shape, (keep, received), [vmem()] * 2, name="merge")

    near_part = lax.ppermute(attended, Y, turn)
    far_part = lax.ppermute(attended, Y, along_y(lambda yh, yl, core: (core, 1 - yl, yh)))
    where = jnp.stack([yl, core]).astype(jnp.int32)
    sides = (where, near_part, far_part, out_weight, fetch(far_weight))
    other = project(1, *sides, jnp.bfloat16, "project_send")
    other = lax.ppermute(other, "core", swap)
    own = project(0, *sides, jnp.float32, "project_keep")
    shape = jax.ShapeDtypeStruct(own.shape, jnp.bfloat16)
    return call(add_kernel, shape, (own, other), [vmem()] * 2, name="add")


def solution(mesh):
    fine = Mesh(mesh.devices.reshape(NX, NZ, 2, 2, 2), ("x", "z", "yh", "yl", "core"))
    tok, head = ("x", "z", "yh"), ("yl", "core")
    return jax.shard_map(
        per_device,
        mesh=fine,
        in_specs=(P(tok, head), P(tok, head), P(tok, head), P(tok, None), P(head, None)),
        out_specs=P(tok, head),
        check_vma=False,
    )
```

```python
import math

import jax
import jax.numpy as jnp
from jax import lax
from jax.experimental import pallas as pl
from jax.experimental.pallas import tpu as pltpu
from jax.sharding import Mesh, PartitionSpec as P

HD = 128
TILE = 128
NX, NZ = 4, 8
HEADS = 6
WIDE = HEADS * TILE
SUM_ROW = HD
MAX_ROW = HD + 16
ROWS = HD + 24
NEGATIVE = -1e30
MASK_AT = 2 * HEADS
UNIT_AT = MASK_AT + 1
EXP2_SCALE = math.log2(math.e) / math.sqrt(HD)
EARLY = (-1, 1, 0, 4)
LATE = (-2, 2, -3, 3)


def vmem():
    return pl.BlockSpec(memory_space=pltpu.VMEM)


def smem():
    return pl.BlockSpec(memory_space=pltpu.SMEM)


def hbm():
    return pl.BlockSpec(memory_space=pl.ANY)


def in_hbm(x):
    return pltpu.with_memory_space_constraint(x, pltpu.HBM)


def call(kernel, out_shape, args, in_specs, scratch=(), aliases=None, name=None, flops=0):
    return pl.pallas_call(
        kernel,
        out_shape=out_shape,
        in_specs=in_specs,
        out_specs=jax.tree.map(lambda s: vmem(), out_shape),
        scratch_shapes=list(scratch),
        input_output_aliases=aliases or {},
        compiler_params=pltpu.CompilerParams(vmem_limit_bytes=14 * 1024 * 1024),
        cost_estimate=pl.CostEstimate(flops=flops, transcendentals=0, bytes_accessed=0),
        name=name,
    )(*args)


def pack_kernel(key_hbm, value_hbm, query_hbm, mask_hbm, unit_ref, out_ref, *scratch):
    *buffers, sems = scratch
    key_ref, value_ref, query_ref, mask_ref = buffers
    copies = [
        pltpu.make_async_copy(source, target, sems.at[i])
        for i, (source, target) in enumerate(
            zip((key_hbm, value_hbm, query_hbm, mask_hbm), buffers)
        )
    ]
    for copy in copies:
        copy.start()
    for copy in copies:
        copy.wait()
    for t in range(2):
        rows = pl.ds(t * TILE, TILE)
        values = value_ref[rows, :].astype(jnp.float32).T.astype(jnp.bfloat16)
        for ref, at in ((unit_ref, 0), (out_ref, UNIT_AT)):
            ref[at + t] = key_ref[rows, :]
            ref[at + 2 + t] = values
        for h in range(HEADS):
            out_ref[t * HEADS + h] = query_ref[rows, pl.ds(h * HD, HD)]
    out_ref[MASK_AT] = jnp.zeros((TILE, TILE), jnp.bfloat16)
    out_ref[MASK_AT, 0:2, :] = mask_ref[...].astype(jnp.float32).astype(jnp.bfloat16)


def pack(*arrays):
    return call(
        pack_kernel,
        tuple(
            jax.ShapeDtypeStruct((size, TILE, TILE), jnp.bfloat16) for size in (4, UNIT_AT + 4)
        ),
        tuple(in_hbm(a) for a in arrays),
        [hbm()] * 4,
        scratch=[pltpu.VMEM(a.shape, a.dtype) for a in arrays] + [pltpu.SemaphoreType.DMA((4,))],
        name="pack",
    )


def half_kernel(half_ref, source_ref, out_ref, sems):
    rows = out_ref.shape[0] // 8
    start = pl.multiple_of(half_ref[0] * out_ref.shape[1], out_ref.shape[1])
    copies = [
        pltpu.make_async_copy(
            source_ref.at[pl.ds(i * rows, rows), pl.ds(start, out_ref.shape[1])],
            out_ref.at[pl.ds(i * rows, rows), :],
            sems.at[i],
        )
        for i in range(8)
    ]
    for copy in copies:
        copy.start()
    for copy in copies:
        copy.wait()


def column_half(source, number):
    return call(
        half_kernel,
        jax.ShapeDtypeStruct((source.shape[0], source.shape[1] // 2), source.dtype),
        (number.reshape(1).astype(jnp.int32), in_hbm(source)),
        [smem(), hbm()],
        scratch=(pltpu.SemaphoreType.DMA((8,)),),
        name="column_half",
    )


def fetch_kernel(source_ref, out_ref, sems):
    rows = out_ref.shape[0] // 4
    copies = [
        pltpu.make_async_copy(
            source_ref.at[pl.ds(i * rows, rows), :], out_ref.at[pl.ds(i * rows, rows), :], sems.at[i]
        )
        for i in range(4)
    ]
    for copy in copies:
        copy.start()
    for copy in copies:
        copy.wait()


def fetch(source):
    shape = jax.ShapeDtypeStruct(source.shape, source.dtype)
    scratch = (pltpu.SemaphoreType.DMA((4,)),)
    return call(fetch_kernel, shape, (in_hbm(source),), [hbm()], scratch=scratch, name="fetch")


def join_kernel(starts, *refs):
    out_ref = refs[-1]
    at = 0
    for start, ref in zip(starts, refs[:-1]):
        size = ref.shape[0] - start
        out_ref[pl.ds(at, size)] = ref[pl.ds(start, size)]
        at += size


def join(parts):
    starts = [p[1] if isinstance(p, tuple) else 0 for p in parts]
    parts = [p[0] if isinstance(p, tuple) else p for p in parts]
    total = sum(p.shape[0] - start for p, start in zip(parts, starts))
    shape = jax.ShapeDtypeStruct((total, *parts[0].shape[1:]), parts[0].dtype)
    kernel = lambda *refs: join_kernel(starts, *refs)
    return call(kernel, shape, parts, [vmem()] * len(parts), name="join")


def stage_kernel(columns, count, numbers, first, table_ref, mine_ref, theirs_ref, *refs):
    parts, refs = refs[:count], refs[count:]
    targets = sorted({number // 2 for number in numbers})
    if not first:
        refs = refs[len(targets) :]
    states, (tiles_ref, list_ref) = refs[: len(targets)], refs[len(targets) :]
    x, z, core = table_ref[4, 0], table_ref[4, 1], table_ref[4, 2]
    at = 0
    for part in parts:
        tiles_ref[pl.ds(at, part.shape[0])] = part[...]
        at += part.shape[0]
    if first:
        for ref in states:
            ref[:, :MAX_ROW, :] = jnp.zeros((2, MAX_ROW, WIDE), jnp.float32)
            ref[:, MAX_ROW:, :] = jnp.full((2, ROWS - MAX_ROW, WIDE), NEGATIVE, jnp.float32)

    counts = [jnp.int32(0)] * 4
    slot = 0
    for dx, order in columns:
        for dz in order:
            block = lax.rem(x + dx + NX, NX) * NZ + lax.rem(z + dz + NZ, NZ)
            for r in range(2):
                tile = (block * 2 + core) * 2 + r
                for number in numbers:
                    list_ref[number, counts[number]] = slot // 2 * 4 + slot % 2
                    counts[number] = counts[number] + table_ref[number, tile]
                slot += 1

    for number in numbers:
        list_ref[number, slot] = counts[number]

    def block(target, row, base, size):
        state_ref = states[targets.index(target)]
        source = theirs_ref if target else mine_ref
        number = 2 * target + row
        at = [list_ref[number, base + j] for j in range(size - 1)]
        live = base + size - 1 < list_ref[number, slot]
        at.append(jnp.where(live, list_ref[number, base + size - 1], at[0]))
        ones = jnp.ones((16, TILE), jnp.bfloat16)
        values = [jnp.concatenate([tiles_ref[i + 2], ones], axis=0) for i in at]
        values[-1] = values[-1] * jnp.where(live, 1.0, 0.0).astype(jnp.bfloat16)
        values = jnp.concatenate(values, axis=1)
        keys = jnp.concatenate([tiles_ref[i] for i in at], axis=0)
        chunks = [pl.ds(h * TILE, TILE) for h in range(HEADS)]
        scores = [
            lax.dot_general(
                keys,
                source[row * HEADS + h],
                (((1,), (1,)), ((), ())),
                preferred_element_type=jnp.float32,
            )
            for h in range(HEADS)
        ]
        probs = []
        for lanes, score in zip(chunks, scores):
            old_max = state_ref[row, pl.ds(MAX_ROW, 1), lanes]
            new_max = jnp.maximum(old_max, jnp.max(score, axis=0, keepdims=True))
            prob = jnp.exp2((score - new_max) * EXP2_SCALE).astype(jnp.bfloat16)
            probs.append((prob, jnp.exp2((old_max - new_max) * EXP2_SCALE)))
            state_ref[row, pl.ds(MAX_ROW, 8), lanes] = jnp.broadcast_to(new_max, (8, TILE))
        for lanes, (prob, fade) in zip(chunks, probs):
            part = lax.dot_general(
                values, prob, (((1,), (0,)), ((), ())), preferred_element_type=jnp.float32
            )
            state_ref[row, pl.ds(0, MAX_ROW), lanes] = (
                state_ref[row, pl.ds(0, MAX_ROW), lanes] * fade + part
            )

    def one_query_tile(target, row):
        total = list_ref[2 * target + row, slot]
        blocks = (total + 1) // 4
        rest = total - 4 * blocks

        def full(turn, carry):
            block(target, row, 4 * turn, 4)
            return carry

        lax.fori_loop(0, blocks, full, 0)

        @pl.when(rest > 0)
        def _():
            block(target, row, 4 * blocks, 2)

    for target in targets:
        for row in range(2):
            one_query_tile(target, row)


def stage(columns, near, parts, state, numbers, name):
    shape = jax.ShapeDtypeStruct((2, ROWS, WIDE), jnp.float32)
    slots = sum(2 * len(order) for _, order in columns)
    args = [*near, *parts]
    outs = len({number // 2 for number in numbers})
    aliases = {}
    if state is not None:
        aliases = {len(args) + i: i for i in range(outs)}
        args += list(state)
    kernel = lambda *refs: stage_kernel(columns, len(parts), numbers, state is None, *refs)
    return call(
        kernel,
        (shape,) * outs,
        args,
        [smem()] + [vmem()] * (len(args) - 1),
        scratch=(
            pltpu.VMEM((2 * slots, TILE, TILE), jnp.bfloat16),
            pltpu.SMEM((4, slots + 1), jnp.int32),
        ),
        aliases=aliases,
        name=name,
    )


def merge_kernel(own_ref, other_ref, out_ref):
    for t in range(2):
        own_max = own_ref[t, pl.ds(MAX_ROW, 1), :]
        other_max = other_ref[t, pl.ds(MAX_ROW, 1), :]
        row_max = jnp.maximum(own_max, other_max)
        own_weight = jnp.exp2((own_max - row_max) * EXP2_SCALE)
        other_weight = jnp.exp2((other_max - row_max) * EXP2_SCALE)
        total = (
            own_ref[t, pl.ds(SUM_ROW, 1), :] * own_weight
            + other_ref[t, pl.ds(SUM_ROW, 1), :] * other_weight
        )
        own_weight = own_weight / total
        other_weight = other_weight / total
        for h in range(HEADS):
            lanes = slice(h * TILE, (h + 1) * TILE)
            attended = (
                own_ref[t, pl.ds(0, HD), lanes] * own_weight[:, lanes]
                + other_ref[t, pl.ds(0, HD), lanes] * other_weight[:, lanes]
            )
            out_ref[pl.ds(t * TILE, TILE), pl.ds(h * HD, HD)] = attended.T.astype(jnp.bfloat16)


def ring(size, step):
    return [(i, (i + step) % size) for i in range(size)]


def along_y(move):
    pairs = []
    for i in range(8):
        yh, yl, core = move(i // 4, i // 2 % 2, i % 2)
        pairs.append((i, yh % 2 * 4 + yl % 2 * 2 + core % 2))
    return pairs


def next_y(yh, yl, step):
    y = (yh * 2 + yl + step) % 4
    return y // 2, y % 2


Y = ("yh", "yl", "core")
YZ = ("z", "yh", "yl", "core")


def turned(shift):
    turn = along_y(lambda yh, yl, core: (core, yl, yh))
    return [(z * 8 + a, (z + shift) % NZ * 8 + b) for z in range(NZ) for a, b in turn]


def near_kernel(place_ref, near_ref, weight_ref, out_ref):
    for n in range(out_ref.shape[1] // 256):
        at = pl.multiple_of(place_ref[0] * out_ref.shape[1] + n * 256, 256)
        out_ref[:, n * 256 : (n + 1) * 256] = jnp.dot(
            near_ref[...], weight_ref[:, pl.ds(at, 256)], preferred_element_type=jnp.float32
        )


def project_near(place, near, weight):
    shape = jax.ShapeDtypeStruct((near.shape[0], weight.shape[1] // 2), jnp.float32)
    return call(
        near_kernel, shape, (place, near, weight), [smem()] + [vmem()] * 2, name="project_near"
    )


def project_kernel(flip, place_ref, far_ref, far_weight_ref, before_ref, out_ref):
    width = out_ref.shape[1]
    which = place_ref[1] + flip - 2 * flip * place_ref[1]
    for n in range(width // 256):
        lanes = pl.ds(pl.multiple_of(which * width + n * 256, 256), 256)
        total = before_ref[:, lanes] + jnp.dot(
            far_ref[...], far_weight_ref[:, lanes], preferred_element_type=jnp.float32
        )
        out_ref[:, n * 256 : (n + 1) * 256] = total.astype(out_ref.dtype)


def project(flip, place, far, far_weight, before, dtype, name):
    shape = jax.ShapeDtypeStruct((far.shape[0], far_weight.shape[1] // 2), dtype)
    return call(
        lambda *refs: project_kernel(flip, *refs),
        shape,
        (place, far, far_weight, before),
        [smem()] + [vmem()] * 3,
        name=name,
    )


def add_kernel(keep_ref, other_ref, out_ref):
    out_ref[...] = (keep_ref[...] + other_ref[...].astype(jnp.float32)).astype(out_ref.dtype)


def per_device(queries, key_rows, value_rows, tile_mask, out_weight):
    x, z = lax.axis_index("x"), lax.axis_index("z")
    yh, yl, core = lax.axis_index("yh"), lax.axis_index("yl"), lax.axis_index("core")
    turn = along_y(lambda yh, yl, core: (core, yl, yh))
    swap = [(0, 1), (1, 0)]
    together = lax.optimization_barrier

    unit, bundle = pack(key_rows, value_rows, queries, tile_mask)
    up, down = ring(NZ, 1), ring(NZ, -1)
    units = {-1: lax.ppermute(unit, YZ, turned(1)), 1: lax.ppermute(unit, YZ, turned(-1))}
    mine = lax.ppermute(bundle, Y, turn)
    units[4] = lax.ppermute(unit, YZ, turned(4))
    half_away = column_half(out_weight, 1 - yl)
    units[-1], units[1], units[4], mine, half_away = together(
        (units[-1], units[1], units[4], mine, half_away)
    )
    away = along_y(lambda yh, yl, core: (*next_y(yh, yl, 1 - 2 * core), core))
    far_weight = lax.ppermute(half_away, Y, away)
    early = join([units[-1], units[1], (mine, UNIT_AT), units[4]])
    forth, back = ring(NX, 1), ring(NX, -1)
    early_before = lax.ppermute(early, "x", forth)
    early_after = lax.ppermute(early, "x", back)
    for step in (2, 3):
        units[-step] = lax.ppermute(units[1 - step], "z", up)
        units[step] = lax.ppermute(units[step - 1], "z", down)
    late, mine, early_before, early_after = together(
        (join([units[d] for d in LATE]), mine, early_before, early_after)
    )
    late_before = lax.ppermute(late, "x", forth)
    late_after = lax.ppermute(late, "x", back)
    theirs = lax.ppermute(mine, "core", swap)
    place = jnp.pad(jnp.stack([x, z, core]).astype(jnp.int32), (0, 125))[None]
    masks = jnp.concatenate([mine[MASK_AT, :2], theirs[MASK_AT, :2]]).astype(jnp.int32)
    table = jnp.concatenate([masks, place])

    near = (table, mine, theirs)
    every = (0, 1, 2, 3)
    half = early.shape[0] // 2
    early_far = [
        lax.ppermute(early_before[:half], "x", forth),
        lax.ppermute(early_after[half:], "x", back),
    ]
    columns = ((0, EARLY), (0, LATE), (-1, EARLY), (1, EARLY))
    parts = [early, late, early_before, early_after]
    state = stage(columns, near, parts, None, every, "first")
    late_before, late_after, *state = together((late_before, late_after, *state))
    late_far = [
        lax.ppermute(late_before[:half], "x", forth),
        lax.ppermute(late_after[half:], "x", back),
    ]
    columns = ((-1, LATE), (1, LATE), (2, EARLY))
    parts = [late_before, late_after, *early_far]
    keep, send = stage(columns, near, parts, state, every, "late")
    *late_far, keep, send = together((*late_far, keep, send))
    last = (((2, LATE),), near, late_far)
    (send,) = stage(*last, (send,), (2, 3), "last_send")
    received = lax.ppermute(send, "core", swap)
    (keep,) = stage(*last, (keep,), (0, 1), "last_keep")
    shape = jax.ShapeDtypeStruct((2 * TILE, WIDE), jnp.bfloat16)
    attended = call(merge_kernel, shape, (keep, received), [vmem()] * 2, name="merge")

    near_part = lax.ppermute(attended, Y, turn)
    far_part = lax.ppermute(attended, Y, along_y(lambda yh, yl, core: (core, 1 - yl, yh)))
    where = jnp.stack([yl, core]).astype(jnp.int32)
    near_part, far_weight = together((near_part, fetch(far_weight)))
    sides = (where, far_part, far_weight, project_near(where, near_part, out_weight))
    other = project(1, *sides, jnp.bfloat16, "project_send")
    other = lax.ppermute(other, "core", swap)
    own = project(0, *sides, jnp.float32, "project_keep")
    shape = jax.ShapeDtypeStruct(own.shape, jnp.bfloat16)
    return call(add_kernel, shape, (own, other), [vmem()] * 2, name="add")


def solution(mesh):
    fine = Mesh(mesh.devices.reshape(NX, NZ, 2, 2, 2), ("x", "z", "yh", "yl", "core"))
    tok, head = ("x", "z", "yh"), ("yl", "core")
    return jax.shard_map(
        per_device,
        mesh=fine,
        in_specs=(P(tok, head), P(tok, head), P(tok, head), P(tok, None), P(head, None)),
        out_specs=P(tok, head),
        check_vma=False,
    )
```

```python
import math

import jax
import jax.numpy as jnp
from jax import lax
from jax.experimental import pallas as pl
from jax.experimental.pallas import tpu as pltpu
from jax.sharding import Mesh, PartitionSpec as P

HD = 128
TILE = 128
NX, NZ = 4, 8
HEADS = 6
WIDE = HEADS * TILE
SUM_ROW = HD
MAX_ROW = HD + 16
ROWS = HD + 24
NEGATIVE = -1e30
MASK_AT = 2 * HEADS
UNIT_AT = MASK_AT + 1
EXP2_SCALE = math.log2(math.e) / math.sqrt(HD)
EARLY = (-1, 1, 0, 4)
LATE = (-2, 2, -3, 3)


def vmem():
    return pl.BlockSpec(memory_space=pltpu.VMEM)


def smem():
    return pl.BlockSpec(memory_space=pltpu.SMEM)


def hbm():
    return pl.BlockSpec(memory_space=pl.ANY)


def in_hbm(x):
    return pltpu.with_memory_space_constraint(x, pltpu.HBM)


def call(kernel, out_shape, args, in_specs, scratch=(), aliases=None, name=None, flops=0):
    return pl.pallas_call(
        kernel,
        out_shape=out_shape,
        in_specs=in_specs,
        out_specs=jax.tree.map(lambda s: vmem(), out_shape),
        scratch_shapes=list(scratch),
        input_output_aliases=aliases or {},
        compiler_params=pltpu.CompilerParams(vmem_limit_bytes=14 * 1024 * 1024),
        cost_estimate=pl.CostEstimate(flops=flops, transcendentals=0, bytes_accessed=0),
        name=name,
    )(*args)


def pack_kernel(key_hbm, value_hbm, query_hbm, mask_hbm, unit_ref, out_ref, *scratch):
    *buffers, sems = scratch
    key_ref, value_ref, query_ref, mask_ref = buffers
    copies = [
        pltpu.make_async_copy(source, target, sems.at[i])
        for i, (source, target) in enumerate(
            zip((key_hbm, value_hbm, query_hbm, mask_hbm), buffers)
        )
    ]
    for copy in copies:
        copy.start()
    for copy in copies:
        copy.wait()
    for t in range(2):
        rows = pl.ds(t * TILE, TILE)
        values = value_ref[rows, :].astype(jnp.float32).T.astype(jnp.bfloat16)
        for ref, at in ((unit_ref, 0), (out_ref, UNIT_AT)):
            ref[at + t] = key_ref[rows, :]
            ref[at + 2 + t] = values
        for h in range(HEADS):
            out_ref[t * HEADS + h] = query_ref[rows, pl.ds(h * HD, HD)]
    out_ref[MASK_AT] = jnp.zeros((TILE, TILE), jnp.bfloat16)
    out_ref[MASK_AT, 0:2, :] = mask_ref[...].astype(jnp.float32).astype(jnp.bfloat16)


def pack(*arrays):
    return call(
        pack_kernel,
        tuple(
            jax.ShapeDtypeStruct((size, TILE, TILE), jnp.bfloat16) for size in (4, UNIT_AT + 4)
        ),
        tuple(in_hbm(a) for a in arrays),
        [hbm()] * 4,
        scratch=[pltpu.VMEM(a.shape, a.dtype) for a in arrays] + [pltpu.SemaphoreType.DMA((4,))],
        name="pack",
    )


def half_kernel(half_ref, source_ref, out_ref, sems):
    rows = out_ref.shape[0] // 8
    start = pl.multiple_of(half_ref[0] * out_ref.shape[1], out_ref.shape[1])
    copies = [
        pltpu.make_async_copy(
            source_ref.at[pl.ds(i * rows, rows), pl.ds(start, out_ref.shape[1])],
            out_ref.at[pl.ds(i * rows, rows), :],
            sems.at[i],
        )
        for i in range(8)
    ]
    for copy in copies:
        copy.start()
    for copy in copies:
        copy.wait()


def column_half(source, number):
    return call(
        half_kernel,
        jax.ShapeDtypeStruct((source.shape[0], source.shape[1] // 2), source.dtype),
        (number.reshape(1).astype(jnp.int32), in_hbm(source)),
        [smem(), hbm()],
        scratch=(pltpu.SemaphoreType.DMA((8,)),),
        name="column_half",
    )


def fetch_kernel(source_ref, out_ref, sems):
    rows = out_ref.shape[0] // 4
    copies = [
        pltpu.make_async_copy(
            source_ref.at[pl.ds(i * rows, rows), :], out_ref.at[pl.ds(i * rows, rows), :], sems.at[i]
        )
        for i in range(4)
    ]
    for copy in copies:
        copy.start()
    for copy in copies:
        copy.wait()


def fetch(source):
    shape = jax.ShapeDtypeStruct(source.shape, source.dtype)
    scratch = (pltpu.SemaphoreType.DMA((4,)),)
    return call(fetch_kernel, shape, (in_hbm(source),), [hbm()], scratch=scratch, name="fetch")


def join_kernel(starts, *refs):
    out_ref = refs[-1]
    at = 0
    for start, ref in zip(starts, refs[:-1]):
        size = ref.shape[0] - start
        out_ref[pl.ds(at, size)] = ref[pl.ds(start, size)]
        at += size


def join(parts):
    starts = [p[1] if isinstance(p, tuple) else 0 for p in parts]
    parts = [p[0] if isinstance(p, tuple) else p for p in parts]
    total = sum(p.shape[0] - start for p, start in zip(parts, starts))
    shape = jax.ShapeDtypeStruct((total, *parts[0].shape[1:]), parts[0].dtype)
    kernel = lambda *refs: join_kernel(starts, *refs)
    return call(kernel, shape, parts, [vmem()] * len(parts), name="join")


def stage_kernel(columns, count, numbers, first, table_ref, mine_ref, theirs_ref, *refs):
    parts, refs = refs[:count], refs[count:]
    targets = sorted({number // 2 for number in numbers})
    if not first:
        refs = refs[len(targets) :]
    states, (tiles_ref, list_ref) = refs[: len(targets)], refs[len(targets) :]
    x, z, core = table_ref[4, 0], table_ref[4, 1], table_ref[4, 2]
    at = 0
    for part in parts:
        tiles_ref[pl.ds(at, part.shape[0])] = part[...]
        at += part.shape[0]
    if first:
        for ref in states:
            ref[:, :MAX_ROW, :] = jnp.zeros((2, MAX_ROW, WIDE), jnp.float32)
            ref[:, MAX_ROW:, :] = jnp.full((2, ROWS - MAX_ROW, WIDE), NEGATIVE, jnp.float32)

    counts = [jnp.int32(0)] * 4
    slot = 0
    for dx, order in columns:
        for dz in order:
            block = lax.rem(x + dx + NX, NX) * NZ + lax.rem(z + dz + NZ, NZ)
            for r in range(2):
                tile = (block * 2 + core) * 2 + r
                for number in numbers:
                    list_ref[number, counts[number]] = slot // 2 * 4 + slot % 2
                    counts[number] = counts[number] + table_ref[number, tile]
                slot += 1

    for number in numbers:
        list_ref[number, slot] = counts[number]

    def block(target, row, base, size):
        state_ref = states[targets.index(target)]
        source = theirs_ref if target else mine_ref
        number = 2 * target + row
        at = [list_ref[number, base + j] for j in range(max(size - 1, 1))]
        ones = jnp.ones((16, TILE), jnp.bfloat16)
        if size > 1:
            live = base + size - 1 < list_ref[number, slot]
            at.append(jnp.where(live, list_ref[number, base + size - 1], at[0]))
        values = [jnp.concatenate([tiles_ref[i + 2], ones], axis=0) for i in at]
        if size > 1:
            values[-1] = values[-1] * jnp.where(live, 1.0, 0.0).astype(jnp.bfloat16)
        values = jnp.concatenate(values, axis=1)
        keys = jnp.concatenate([tiles_ref[i] for i in at], axis=0)
        chunks = [pl.ds(h * TILE, TILE) for h in range(HEADS)]
        scores = [
            lax.dot_general(
                keys,
                source[row * HEADS + h],
                (((1,), (1,)), ((), ())),
                preferred_element_type=jnp.float32,
            )
            for h in range(HEADS)
        ]
        probs = []
        for lanes, score in zip(chunks, scores):
            old_max = state_ref[row, pl.ds(MAX_ROW, 1), lanes]
            new_max = jnp.maximum(old_max, jnp.max(score, axis=0, keepdims=True))
            prob = jnp.exp2((score - new_max) * EXP2_SCALE).astype(jnp.bfloat16)
            probs.append((prob, jnp.exp2((old_max - new_max) * EXP2_SCALE)))
            state_ref[row, pl.ds(MAX_ROW, 8), lanes] = jnp.broadcast_to(new_max, (8, TILE))
        for lanes, (prob, fade) in zip(chunks, probs):
            part = lax.dot_general(
                values, prob, (((1,), (0,)), ((), ())), preferred_element_type=jnp.float32
            )
            state_ref[row, pl.ds(0, MAX_ROW), lanes] = (
                state_ref[row, pl.ds(0, MAX_ROW), lanes] * fade + part
            )

    def one_query_tile(target, row):
        total = list_ref[2 * target + row, slot]
        blocks = (total + 1) // 4
        rest = total - 4 * blocks

        def full(turn, carry):
            block(target, row, 4 * turn, 4)
            return carry

        lax.fori_loop(0, blocks, full, 0)

        @pl.when(rest == 1)
        def _():
            block(target, row, 4 * blocks, 1)

        @pl.when(rest == 2)
        def _():
            block(target, row, 4 * blocks, 2)

    for target in targets:
        for row in range(2):
            one_query_tile(target, row)


def stage(columns, near, parts, state, numbers, name):
    shape = jax.ShapeDtypeStruct((2, ROWS, WIDE), jnp.float32)
    slots = sum(2 * len(order) for _, order in columns)
    args = [*near, *parts]
    outs = len({number // 2 for number in numbers})
    aliases = {}
    if state is not None:
        aliases = {len(args) + i: i for i in range(outs)}
        args += list(state)
    kernel = lambda *refs: stage_kernel(columns, len(parts), numbers, state is None, *refs)
    return call(
        kernel,
        (shape,) * outs,
        args,
        [smem()] + [vmem()] * (len(args) - 1),
        scratch=(
            pltpu.VMEM((2 * slots, TILE, TILE), jnp.bfloat16),
            pltpu.SMEM((4, slots + 1), jnp.int32),
        ),
        aliases=aliases,
        name=name,
    )


def merge_kernel(own_ref, other_ref, out_ref):
    for t in range(2):
        own_max = own_ref[t, pl.ds(MAX_ROW, 1), :]
        other_max = other_ref[t, pl.ds(MAX_ROW, 1), :]
        row_max = jnp.maximum(own_max, other_max)
        own_weight = jnp.exp2((own_max - row_max) * EXP2_SCALE)
        other_weight = jnp.exp2((other_max - row_max) * EXP2_SCALE)
        total = (
            own_ref[t, pl.ds(SUM_ROW, 1), :] * own_weight
            + other_ref[t, pl.ds(SUM_ROW, 1), :] * other_weight
        )
        own_weight = own_weight / total
        other_weight = other_weight / total
        for h in range(HEADS):
            lanes = slice(h * TILE, (h + 1) * TILE)
            attended = (
                own_ref[t, pl.ds(0, HD), lanes] * own_weight[:, lanes]
                + other_ref[t, pl.ds(0, HD), lanes] * other_weight[:, lanes]
            )
            out_ref[pl.ds(t * TILE, TILE), pl.ds(h * HD, HD)] = attended.T.astype(jnp.bfloat16)


def ring(size, step):
    return [(i, (i + step) % size) for i in range(size)]


def along_y(move):
    pairs = []
    for i in range(8):
        yh, yl, core = move(i // 4, i // 2 % 2, i % 2)
        pairs.append((i, yh % 2 * 4 + yl % 2 * 2 + core % 2))
    return pairs


def next_y(yh, yl, step):
    y = (yh * 2 + yl + step) % 4
    return y // 2, y % 2


Y = ("yh", "yl", "core")
YZ = ("z", "yh", "yl", "core")


def turned(shift):
    turn = along_y(lambda yh, yl, core: (core, yl, yh))
    return [(z * 8 + a, (z + shift) % NZ * 8 + b) for z in range(NZ) for a, b in turn]


def project_kernel(flip, place_ref, near_ref, far_ref, weight_ref, far_weight_ref, out_ref):
    width = out_ref.shape[1]
    which = place_ref[1] + flip - 2 * flip * place_ref[1]
    for n in range(width // 256):
        at = pl.multiple_of(which * width + n * 256, 256)
        far = far_weight_ref[:, pl.ds(at, 256)]
        total = jnp.dot(far_ref[...], far, preferred_element_type=jnp.float32)
        at = pl.multiple_of(place_ref[0] * (2 * width) + which * width + n * 256, 256)
        near = weight_ref[:, pl.ds(at, 256)]
        total = total + jnp.dot(near_ref[...], near, preferred_element_type=jnp.float32)
        out_ref[:, n * 256 : (n + 1) * 256] = total.astype(out_ref.dtype)


def project(flip, place, near, far, weight, far_weight, dtype, name):
    shape = jax.ShapeDtypeStruct((near.shape[0], far_weight.shape[1] // 2), dtype)
    return call(
        lambda *refs: project_kernel(flip, *refs),
        shape,
        (place, near, far, weight, far_weight),
        [smem()] + [vmem()] * 4,
        name=name,
    )


def per_device(queries, key_rows, value_rows, tile_mask, out_weight):
    x, z = lax.axis_index("x"), lax.axis_index("z")
    yh, yl, core = lax.axis_index("yh"), lax.axis_index("yl"), lax.axis_index("core")
    turn = along_y(lambda yh, yl, core: (core, yl, yh))
    swap = [(0, 1), (1, 0)]
    together = lax.optimization_barrier

    unit, bundle = pack(key_rows, value_rows, queries, tile_mask)
    up, down = ring(NZ, 1), ring(NZ, -1)
    units = {-1: lax.ppermute(unit, YZ, turned(1)), 1: lax.ppermute(unit, YZ, turned(-1))}
    mine = lax.ppermute(bundle, Y, turn)
    units[4] = lax.ppermute(unit, YZ, turned(4))
    half_away = column_half(out_weight, 1 - yl)
    units[-1], units[1], units[4], mine, half_away = together(
        (units[-1], units[1], units[4], mine, half_away)
    )
    away = along_y(lambda yh, yl, core: (*next_y(yh, yl, 1 - 2 * core), core))
    far_weight = lax.ppermute(half_away, Y, away)
    early = join([units[-1], units[1], (mine, UNIT_AT), units[4]])
    forth, back = ring(NX, 1), ring(NX, -1)
    early_before = lax.ppermute(early, "x", forth)
    early_after = lax.ppermute(early, "x", back)
    for step in (2, 3):
        units[-step] = lax.ppermute(units[1 - step], "z", up)
        units[step] = lax.ppermute(units[step - 1], "z", down)
    late, mine, early_before, early_after = together(
        (join([units[d] for d in LATE]), mine, early_before, early_after)
    )
    late_before = lax.ppermute(late, "x", forth)
    late_after = lax.ppermute(late, "x", back)
    theirs = lax.ppermute(mine, "core", swap)
    place = jnp.pad(jnp.stack([x, z, core]).astype(jnp.int32), (0, 125))[None]
    masks = jnp.concatenate([mine[MASK_AT, :2], theirs[MASK_AT, :2]]).astype(jnp.int32)
    table = jnp.concatenate([masks, place])

    near = (table, mine, theirs)
    every = (0, 1, 2, 3)
    half = early.shape[0] // 2
    early_far = [
        lax.ppermute(early_before[:half], "x", forth),
        lax.ppermute(early_after[half:], "x", back),
    ]
    columns = ((0, EARLY), (0, LATE), (-1, EARLY), (1, EARLY))
    parts = [early, late, early_before, early_after]
    state = stage(columns, near, parts, None, every, "first")
    late_before, late_after, *state = together((late_before, late_after, *state))
    late_far = [
        lax.ppermute(late_before[:half], "x", forth),
        lax.ppermute(late_after[half:], "x", back),
    ]
    keep, send = stage(
        ((-1, LATE), (1, LATE)), near, [late_before, late_after], state, every, "late"
    )
    *far, keep, send = together((*early_far, *late_far, keep, send))
    last = (((2, EARLY), (2, LATE)), near, far)
    (send,) = stage(*last, (send,), (2, 3), "last_send")
    received = lax.ppermute(send, "core", swap)
    (keep,) = stage(*last, (keep,), (0, 1), "last_keep")
    shape = jax.ShapeDtypeStruct((2 * TILE, WIDE), jnp.bfloat16)
    attended = call(merge_kernel, shape, (keep, received), [vmem()] * 2, name="merge")

    near_part = lax.ppermute(attended, Y, turn)
    far_part = lax.ppermute(attended, Y, along_y(lambda yh, yl, core: (core, 1 - yl, yh)))
    where = jnp.stack([yl, core]).astype(jnp.int32)
    sides = (where, near_part, far_part, out_weight, fetch(far_weight))
    other = project(1, *sides, jnp.bfloat16, "project_send")
    other = lax.ppermute(other, "core", swap)
    own = project(0, *sides, jnp.float32, "project_keep")
    return (own + other.astype(jnp.float32)).astype(jnp.bfloat16)


def solution(mesh):
    fine = Mesh(mesh.devices.reshape(NX, NZ, 2, 2, 2), ("x", "z", "yh", "yl", "core"))
    tok, head = ("x", "z", "yh"), ("yl", "core")
    return jax.shard_map(
        per_device,
        mesh=fine,
        in_specs=(P(tok, head), P(tok, head), P(tok, head), P(tok, None), P(head, None)),
        out_specs=P(tok, head),
        check_vma=False,
    )
```

```python
import math

import jax
import jax.numpy as jnp
from jax import lax
from jax.experimental import pallas as pl
from jax.experimental.pallas import tpu as pltpu
from jax.sharding import Mesh, PartitionSpec as P

HD = 128
TILE = 128
NX, NZ = 4, 8
HEADS = 6
WIDE = HEADS * TILE
SUM_ROW = HD
MAX_ROW = HD + 16
ROWS = HD + 24
NEGATIVE = -1e30
MASK_AT = 2 * HEADS
UNIT_AT = MASK_AT + 1
EXP2_SCALE = math.log2(math.e) / math.sqrt(HD)
EARLY = (-1, 1, 0, 4)
LATE = (-2, 2, -3, 3)


def vmem():
    return pl.BlockSpec(memory_space=pltpu.VMEM)


def smem():
    return pl.BlockSpec(memory_space=pltpu.SMEM)


def hbm():
    return pl.BlockSpec(memory_space=pl.ANY)


def in_hbm(x):
    return pltpu.with_memory_space_constraint(x, pltpu.HBM)


def call(kernel, out_shape, args, in_specs, scratch=(), aliases=None, name=None, flops=0):
    return pl.pallas_call(
        kernel,
        out_shape=out_shape,
        in_specs=in_specs,
        out_specs=jax.tree.map(lambda s: vmem(), out_shape),
        scratch_shapes=list(scratch),
        input_output_aliases=aliases or {},
        compiler_params=pltpu.CompilerParams(vmem_limit_bytes=14 * 1024 * 1024),
        cost_estimate=pl.CostEstimate(flops=flops, transcendentals=0, bytes_accessed=0),
        name=name,
    )(*args)


def pack_kernel(key_hbm, value_hbm, query_hbm, mask_hbm, unit_ref, out_ref, *scratch):
    *buffers, sems = scratch
    key_ref, value_ref, query_ref, mask_ref = buffers
    copies = [
        pltpu.make_async_copy(source, target, sems.at[i])
        for i, (source, target) in enumerate(
            zip((key_hbm, value_hbm, query_hbm, mask_hbm), buffers)
        )
    ]
    for copy in copies:
        copy.start()
    for copy in copies:
        copy.wait()
    for t in range(2):
        rows = pl.ds(t * TILE, TILE)
        values = value_ref[rows, :].astype(jnp.float32).T.astype(jnp.bfloat16)
        for ref, at in ((unit_ref, 0), (out_ref, UNIT_AT)):
            ref[at + t] = key_ref[rows, :]
            ref[at + 2 + t] = values
        for h in range(HEADS):
            out_ref[t * HEADS + h] = query_ref[rows, pl.ds(h * HD, HD)]
    out_ref[MASK_AT] = jnp.zeros((TILE, TILE), jnp.bfloat16)
    out_ref[MASK_AT, 0:2, :] = mask_ref[...].astype(jnp.float32).astype(jnp.bfloat16)


def pack(*arrays):
    return call(
        pack_kernel,
        tuple(
            jax.ShapeDtypeStruct((size, TILE, TILE), jnp.bfloat16) for size in (4, UNIT_AT + 4)
        ),
        tuple(in_hbm(a) for a in arrays),
        [hbm()] * 4,
        scratch=[pltpu.VMEM(a.shape, a.dtype) for a in arrays] + [pltpu.SemaphoreType.DMA((4,))],
        name="pack",
    )


def half_kernel(half_ref, source_ref, out_ref, sems):
    rows = out_ref.shape[0] // 8
    start = pl.multiple_of(half_ref[0] * out_ref.shape[1], out_ref.shape[1])
    copies = [
        pltpu.make_async_copy(
            source_ref.at[pl.ds(i * rows, rows), pl.ds(start, out_ref.shape[1])],
            out_ref.at[pl.ds(i * rows, rows), :],
            sems.at[i],
        )
        for i in range(8)
    ]
    for copy in copies:
        copy.start()
    for copy in copies:
        copy.wait()


def column_half(source, number):
    return call(
        half_kernel,
        jax.ShapeDtypeStruct((source.shape[0], source.shape[1] // 2), source.dtype),
        (number.reshape(1).astype(jnp.int32), in_hbm(source)),
        [smem(), hbm()],
        scratch=(pltpu.SemaphoreType.DMA((8,)),),
        name="column_half",
    )


def fetch_kernel(source_ref, out_ref, sems):
    rows = out_ref.shape[0] // 4
    copies = [
        pltpu.make_async_copy(
            source_ref.at[pl.ds(i * rows, rows), :], out_ref.at[pl.ds(i * rows, rows), :], sems.at[i]
        )
        for i in range(4)
    ]
    for copy in copies:
        copy.start()
    for copy in copies:
        copy.wait()


def fetch(source):
    shape = jax.ShapeDtypeStruct(source.shape, source.dtype)
    scratch = (pltpu.SemaphoreType.DMA((4,)),)
    return call(fetch_kernel, shape, (in_hbm(source),), [hbm()], scratch=scratch, name="fetch")


def join_kernel(starts, *refs):
    out_ref = refs[-1]
    at = 0
    for start, ref in zip(starts, refs[:-1]):
        size = ref.shape[0] - start
        out_ref[pl.ds(at, size)] = ref[pl.ds(start, size)]
        at += size


def join(parts):
    starts = [p[1] if isinstance(p, tuple) else 0 for p in parts]
    parts = [p[0] if isinstance(p, tuple) else p for p in parts]
    total = sum(p.shape[0] - start for p, start in zip(parts, starts))
    shape = jax.ShapeDtypeStruct((total, *parts[0].shape[1:]), parts[0].dtype)
    kernel = lambda *refs: join_kernel(starts, *refs)
    return call(kernel, shape, parts, [vmem()] * len(parts), name="join")


def stage_kernel(columns, count, numbers, first, table_ref, mine_ref, theirs_ref, *refs):
    parts, refs = refs[:count], refs[count:]
    targets = sorted({number // 2 for number in numbers})
    if not first:
        refs = refs[len(targets) :]
    states, (tiles_ref, list_ref) = refs[: len(targets)], refs[len(targets) :]
    x, z, core = table_ref[4, 0], table_ref[4, 1], table_ref[4, 2]
    at = 0
    for part in parts:
        tiles_ref[pl.ds(at, part.shape[0])] = part[...]
        at += part.shape[0]
    if first:
        for ref in states:
            ref[:, :MAX_ROW, :] = jnp.zeros((2, MAX_ROW, WIDE), jnp.float32)
            ref[:, MAX_ROW:, :] = jnp.full((2, ROWS - MAX_ROW, WIDE), NEGATIVE, jnp.float32)

    counts = [jnp.int32(0)] * 4
    slot = 0
    for dx, order in columns:
        for dz in order:
            block = lax.rem(x + dx + NX, NX) * NZ + lax.rem(z + dz + NZ, NZ)
            for r in range(2):
                tile = (block * 2 + core) * 2 + r
                for number in numbers:
                    list_ref[number, counts[number]] = slot // 2 * 4 + slot % 2
                    counts[number] = counts[number] + table_ref[number, tile]
                slot += 1

    for number in numbers:
        list_ref[number, slot] = counts[number]

    def block(target, row, base, size):
        state_ref = states[targets.index(target)]
        source = theirs_ref if target else mine_ref
        number = 2 * target + row
        at = [list_ref[number, base + j] for j in range(max(size - 1, 1))]
        ones = jnp.ones((16, TILE), jnp.bfloat16)
        if size > 1:
            live = base + size - 1 < list_ref[number, slot]
            at.append(jnp.where(live, list_ref[number, base + size - 1], at[0]))
        values = [jnp.concatenate([tiles_ref[i + 2], ones], axis=0) for i in at]
        if size > 1:
            values[-1] = values[-1] * jnp.where(live, 1.0, 0.0).astype(jnp.bfloat16)
        values = jnp.concatenate(values, axis=1)
        keys = jnp.concatenate([tiles_ref[i] for i in at], axis=0)
        chunks = [pl.ds(h * TILE, TILE) for h in range(HEADS)]
        scores = [
            lax.dot_general(
                keys,
                source[row * HEADS + h],
                (((1,), (1,)), ((), ())),
                preferred_element_type=jnp.float32,
            )
            for h in range(HEADS)
        ]
        probs = []
        for lanes, score in zip(chunks, scores):
            old_max = state_ref[row, pl.ds(MAX_ROW, 1), lanes]
            new_max = jnp.maximum(old_max, jnp.max(score, axis=0, keepdims=True))
            prob = jnp.exp2((score - new_max) * EXP2_SCALE).astype(jnp.bfloat16)
            probs.append((prob, jnp.exp2((old_max - new_max) * EXP2_SCALE)))
            state_ref[row, pl.ds(MAX_ROW, 8), lanes] = jnp.broadcast_to(new_max, (8, TILE))
        for lanes, (prob, fade) in zip(chunks, probs):
            part = lax.dot_general(
                values, prob, (((1,), (0,)), ((), ())), preferred_element_type=jnp.float32
            )
            state_ref[row, pl.ds(0, MAX_ROW), lanes] = (
                state_ref[row, pl.ds(0, MAX_ROW), lanes] * fade + part
            )

    def one_query_tile(target, row):
        total = list_ref[2 * target + row, slot]
        blocks = (total + 1) // 4
        rest = total - 4 * blocks

        def full(turn, carry):
            block(target, row, 4 * turn, 4)
            return carry

        lax.fori_loop(0, blocks, full, 0)

        @pl.when(rest > 0)
        def _():
            block(target, row, 4 * blocks, 2)

    for target in targets:
        for row in range(2):
            one_query_tile(target, row)


def stage(columns, near, parts, state, numbers, name):
    shape = jax.ShapeDtypeStruct((2, ROWS, WIDE), jnp.float32)
    slots = sum(2 * len(order) for _, order in columns)
    args = [*near, *parts]
    outs = len({number // 2 for number in numbers})
    aliases = {}
    if state is not None:
        aliases = {len(args) + i: i for i in range(outs)}
        args += list(state)
    kernel = lambda *refs: stage_kernel(columns, len(parts), numbers, state is None, *refs)
    return call(
        kernel,
        (shape,) * outs,
        args,
        [smem()] + [vmem()] * (len(args) - 1),
        scratch=(
            pltpu.VMEM((2 * slots, TILE, TILE), jnp.bfloat16),
            pltpu.SMEM((4, slots + 1), jnp.int32),
        ),
        aliases=aliases,
        name=name,
    )


def merge_kernel(own_ref, other_ref, out_ref):
    for t in range(2):
        own_max = own_ref[t, pl.ds(MAX_ROW, 1), :]
        other_max = other_ref[t, pl.ds(MAX_ROW, 1), :]
        row_max = jnp.maximum(own_max, other_max)
        own_weight = jnp.exp2((own_max - row_max) * EXP2_SCALE)
        other_weight = jnp.exp2((other_max - row_max) * EXP2_SCALE)
        total = (
            own_ref[t, pl.ds(SUM_ROW, 1), :] * own_weight
            + other_ref[t, pl.ds(SUM_ROW, 1), :] * other_weight
        )
        own_weight = own_weight / total
        other_weight = other_weight / total
        for h in range(HEADS):
            lanes = slice(h * TILE, (h + 1) * TILE)
            attended = (
                own_ref[t, pl.ds(0, HD), lanes] * own_weight[:, lanes]
                + other_ref[t, pl.ds(0, HD), lanes] * other_weight[:, lanes]
            )
            out_ref[pl.ds(t * TILE, TILE), pl.ds(h * HD, HD)] = attended.T.astype(jnp.bfloat16)


def ring(size, step):
    return [(i, (i + step) % size) for i in range(size)]


def along_y(move):
    pairs = []
    for i in range(8):
        yh, yl, core = move(i // 4, i // 2 % 2, i % 2)
        pairs.append((i, yh % 2 * 4 + yl % 2 * 2 + core % 2))
    return pairs


def next_y(yh, yl, step):
    y = (yh * 2 + yl + step) % 4
    return y // 2, y % 2


Y = ("yh", "yl", "core")
YZ = ("z", "yh", "yl", "core")


def turned(shift):
    turn = along_y(lambda yh, yl, core: (core, yl, yh))
    return [(z * 8 + a, (z + shift) % NZ * 8 + b) for z in range(NZ) for a, b in turn]


def project_kernel(flip, place_ref, near_ref, far_ref, weight_ref, far_weight_ref, out_ref):
    width = out_ref.shape[1]
    which = place_ref[1] + flip - 2 * flip * place_ref[1]
    for n in range(width // 256):
        at = pl.multiple_of(which * width + n * 256, 256)
        far = far_weight_ref[:, pl.ds(at, 256)]
        total = jnp.dot(far_ref[...], far, preferred_element_type=jnp.float32)
        at = pl.multiple_of(place_ref[0] * (2 * width) + which * width + n * 256, 256)
        near = weight_ref[:, pl.ds(at, 256)]
        total = total + jnp.dot(near_ref[...], near, preferred_element_type=jnp.float32)
        out_ref[:, n * 256 : (n + 1) * 256] = total.astype(out_ref.dtype)


def project(flip, place, near, far, weight, far_weight, dtype, name):
    shape = jax.ShapeDtypeStruct((near.shape[0], far_weight.shape[1] // 2), dtype)
    return call(
        lambda *refs: project_kernel(flip, *refs),
        shape,
        (place, near, far, weight, far_weight),
        [smem()] + [vmem()] * 4,
        name=name,
    )


def per_device(queries, key_rows, value_rows, tile_mask, out_weight):
    x, z = lax.axis_index("x"), lax.axis_index("z")
    yh, yl, core = lax.axis_index("yh"), lax.axis_index("yl"), lax.axis_index("core")
    turn = along_y(lambda yh, yl, core: (core, yl, yh))
    swap = [(0, 1), (1, 0)]
    together = lax.optimization_barrier

    unit, bundle = pack(key_rows, value_rows, queries, tile_mask)
    up, down = ring(NZ, 1), ring(NZ, -1)
    units = {-1: lax.ppermute(unit, YZ, turned(1)), 1: lax.ppermute(unit, YZ, turned(-1))}
    mine = lax.ppermute(bundle, Y, turn)
    units[4] = lax.ppermute(unit, YZ, turned(4))
    half_away = column_half(out_weight, 1 - yl)
    units[-1], units[1], units[4], mine, half_away = together(
        (units[-1], units[1], units[4], mine, half_away)
    )
    away = along_y(lambda yh, yl, core: (*next_y(yh, yl, 1 - 2 * core), core))
    far_weight = lax.ppermute(half_away, Y, away)
    early = join([units[-1], units[1], (mine, UNIT_AT), units[4]])
    forth, back = ring(NX, 1), ring(NX, -1)
    early_before = lax.ppermute(early, "x", forth)
    early_after = lax.ppermute(early, "x", back)
    for step in (2, 3):
        units[-step] = lax.ppermute(units[1 - step], "z", up)
        units[step] = lax.ppermute(units[step - 1], "z", down)
    late, mine, early_before, early_after = together(
        (join([units[d] for d in LATE]), mine, early_before, early_after)
    )
    late_before = lax.ppermute(late, "x", forth)
    late_after = lax.ppermute(late, "x", back)
    theirs = lax.ppermute(mine, "core", swap)
    place = jnp.pad(jnp.stack([x, z, core]).astype(jnp.int32), (0, 125))[None]
    masks = jnp.concatenate([mine[MASK_AT, :2], theirs[MASK_AT, :2]]).astype(jnp.int32)
    table = jnp.concatenate([masks, place])

    near = (table, mine, theirs)
    every = (0, 1, 2, 3)
    half = early.shape[0] // 2
    early_far = [
        lax.ppermute(early_before[:half], "x", forth),
        lax.ppermute(early_after[half:], "x", back),
    ]
    columns = ((0, EARLY), (0, LATE), (-1, EARLY), (1, EARLY))
    parts = [early, late, early_before, early_after]
    state = stage(columns, near, parts, None, every, "first")
    late_before, late_after, *state = together((late_before, late_after, *state))
    late_far = [
        lax.ppermute(late_before[:half], "x", forth),
        lax.ppermute(late_after[half:], "x", back),
    ]
    state = stage(
        ((-1, LATE), (1, LATE)), near, [late_before, late_after], state, every, "late"
    )
    keep, send = stage(((2, EARLY),), near, early_far, state, every, "opposite")
    *late_far, keep, send = together((*late_far, keep, send))
    last = (((2, LATE),), near, late_far)
    (send,) = stage(*last, (send,), (2, 3), "last_send")
    received = lax.ppermute(send, "core", swap)
    (keep,) = stage(*last, (keep,), (0, 1), "last_keep")
    shape = jax.ShapeDtypeStruct((2 * TILE, WIDE), jnp.bfloat16)
    attended = call(merge_kernel, shape, (keep, received), [vmem()] * 2, name="merge")

    near_part = lax.ppermute(attended, Y, turn)
    far_part = lax.ppermute(attended, Y, along_y(lambda yh, yl, core: (core, 1 - yl, yh)))
    where = jnp.stack([yl, core]).astype(jnp.int32)
    sides = (where, near_part, far_part, out_weight, fetch(far_weight))
    other = project(1, *sides, jnp.bfloat16, "project_send")
    other = lax.ppermute(other, "core", swap)
    own = project(0, *sides, jnp.float32, "project_keep")
    return (own + other.astype(jnp.float32)).astype(jnp.bfloat16)


def solution(mesh):
    fine = Mesh(mesh.devices.reshape(NX, NZ, 2, 2, 2), ("x", "z", "yh", "yl", "core"))
    tok, head = ("x", "z", "yh"), ("yl", "core")
    return jax.shard_map(
        per_device,
        mesh=fine,
        in_specs=(P(tok, head), P(tok, head), P(tok, head), P(tok, None), P(head, None)),
        out_specs=P(tok, head),
        check_vma=False,
    )
```
